32 devices in a mesh: dp: 8 (over y, x, core), fsdp: 4 (over z).
Axes of the slice: x: 2, y: 2, z: 4, core: 2. Of those that a mesh axis runs over, the one named last changes fastest.
Arguments:
- unit_states: bfloat16 [32, 768, 1024], P(('dp', 'fsdp')), may hold values from -6 to 6
- encoder_states: bfloat16 [32, 256, 1024], P(('dp', 'fsdp')), may hold values from -6 to 6
- cotangent: float32 [32, 768, 1024], P(('dp', 'fsdp')), may hold values from -6 to 6
- unit_lengths: int32 [32], P(('dp', 'fsdp')), may hold values from 384 to 768, as said below
- text_lengths: int32 [32], P(('dp', 'fsdp')), may hold values from 64 to 256, as said below
- self_project: float32 [1024, 3072], P(('dp', 'fsdp')), may hold values from -0.1875 to 0.1875
- self_output: float32 [1024, 1024], P(('dp', 'fsdp')), may hold values from -1.5 to 1.5
- cross_project: float32 [1024, 3072], P(('dp', 'fsdp')), may hold values from -0.1875 to 0.1875
- cross_output: float32 [1024, 1024], P(('dp', 'fsdp')), may hold values from -1.5 to 1.5
- feed_input: float32 [1024, 4096], P(('dp', 'fsdp')), may hold values from -0.375 to 0.375
- feed_output: float32 [4096, 1024], P(('dp', 'fsdp')), may hold values from -0.375 to 0.375
- norm_gains: bfloat16 [4, 1024], P(None, ('dp', 'fsdp')), may hold values from 0.5 to 1.5
- norm_biases: bfloat16 [4, 1024], P(None, ('dp', 'fsdp')), may hold values from -0.59765625 to 0.59765625
Outputs:
- block_output: bfloat16 [32, 768, 1024], P(('dp', 'fsdp'))
- grad_states: float32 [32, 768, 1024], P(('dp', 'fsdp'))
- grad_encoder: float32 [32, 256, 1024], P(('dp', 'fsdp'))
- grad_self_project: float32 [1024, 3072], P(('dp', 'fsdp'))
- grad_self_output: float32 [1024, 1024], P(('dp', 'fsdp'))
- grad_cross_project: float32 [1024, 3072], P(('dp', 'fsdp'))
- grad_cross_output: float32 [1024, 1024], P(('dp', 'fsdp'))
- grad_feed_input: float32 [1024, 4096], P(('dp', 'fsdp'))
- grad_feed_output: float32 [4096, 1024], P(('dp', 'fsdp'))
- grad_gains: float32 [4, 1024], P(None, ('dp', 'fsdp'))
- grad_biases: float32 [4, 1024], P(None, ('dp', 'fsdp'))
The draws below stay inside these ranges and needn't reach their ends.
Inputs may be any that keep to these rules, and one draw needn't show every extreme that they name: `unit_lengths`: units of each sequence; slots at and past it are padding. Some sequence has exactly 768. `text_lengths`: encoder states that count for each sequence; some sequence has exactly 256.
All inputs are finite; a program needn't handle non-finite values.
Results may differ from the reference program's by a relative error of at most 0.02.
Values may be sent and summed in bfloat16 or wider, within the bound.
No kernel may reach another device: no remote copies, remote signals or barrier semaphores. Data moves between devices by JAX's collectives and lax.ppermute only.
A program may use at most 256 MiB of HBM per device.

```python
import jax
import jax.numpy as jnp
from jax import lax

D = 1024
HEADS = 16
HEAD = 64
FF = 4096
UNITS = 768
TEXT = 256
SEQS = 32


def draw_unit_lengths(key, part):
    first_key, second_key = jax.random.split(jax.random.fold_in(key, 11))
    base = jax.random.randint(first_key, (SEQS,), UNITS // 2, UNITS + 1)
    chosen = jax.random.randint(second_key, (), 0, SEQS)
    return jnp.where(jnp.arange(SEQS) == chosen, UNITS, base).astype(jnp.int32)


def draw_text_lengths(key, part):
    first_key, second_key = jax.random.split(jax.random.fold_in(key, 23))
    base = jax.random.randint(first_key, (SEQS,), TEXT // 4, TEXT + 1)
    chosen = jax.random.randint(second_key, (), 0, SEQS)
    return jnp.where(jnp.arange(SEQS) == chosen, TEXT, base).astype(jnp.int32)


def spiked(entries, stream_key, source, target, shards_of, factor):
    owner, partner = [(jnp.arange(entries.shape[dim]) // (entries.shape[dim] // shards_of)).reshape([-1 if axis == dim else 1 for axis in range(entries.ndim)]) for dim in (source, target)]
    chosen = jax.random.permutation(stream_key, shards_of)[partner]
    strong = (owner == chosen) | (owner == (partner + shards_of // 2) % shards_of)
    return jnp.where(strong, factor * entries, entries)


def shard_levels(stream_key, dims, pieces, low, top_value):
    level = 1.0
    for axis_at, shards_of in pieces:
        heights = jax.random.uniform(jax.random.fold_in(jax.random.fold_in(stream_key, 6), axis_at), (shards_of,), jnp.float32, low / len(pieces), top_value / len(pieces))
        level = level * jnp.repeat(jnp.exp(heights), dims[axis_at] // shards_of).reshape((-1,) + (1,) * (len(dims) - 1 - axis_at))
    return level


def centred(rng, extent, width, most, cuts=(), kind=jnp.bfloat16):
    gain = shard_levels(rng, extent, cuts, -0.22, 0.18) if cuts else 1.0
    values = jax.random.normal(rng, extent, jnp.float32) * width * gain
    return jnp.minimum(jnp.maximum(values, -most), most).astype(kind)


def bell_draw_with(rng, extent, width, limit, shards, heavy, kind=jnp.bfloat16):
    values = width * jax.random.normal(rng, extent, jnp.float32)
    if shards:
        values = values * shard_levels(rng, extent, shards, -0.22, 0.18)
    return jnp.clip(spiked(values, jax.random.fold_in(rng, 3), *heavy), -limit, limit).astype(kind)


def setup_inputs(seed: int = 0) -> dict:
    arg_keys = jax.random.split(jax.random.key(seed), 14)
    return {
        "unit_states": bell_draw_with(arg_keys[0], (SEQS, UNITS, D), 1.0, 6.0, ((0, 32),), (0, 2, 32, 2.75)),
        "encoder_states": bell_draw_with(arg_keys[1], (SEQS, TEXT, D), 1.0, 6.0, ((0, 32),), (0, 2, 32, 2.75)),
        "cotangent": bell_draw_with(arg_keys[2], (SEQS, UNITS, D), 1.0, 6.0, ((0, 32),), (0, 2, 32, 2.75), jnp.float32),
        "unit_lengths": draw_unit_lengths(jax.random.fold_in(arg_keys[13], 71), 0),
        "text_lengths": draw_text_lengths(jax.random.fold_in(arg_keys[13], 71), 0),
        "self_project": centred(arg_keys[5], (D, 3 * D), D ** -0.5, 0.1875, ((0, 32),), jnp.float32),
        "self_output": centred(arg_keys[6], (D, D), (D // 64) ** -0.5, 1.5, ((0, 32),), jnp.float32),
        "cross_project": centred(arg_keys[7], (D, 3 * D), D ** -0.5, 0.1875, ((0, 32),), jnp.float32),
        "cross_output": centred(arg_keys[8], (D, D), (D // 64) ** -0.5, 1.5, ((0, 32),), jnp.float32),
        "feed_input": bell_draw_with(arg_keys[9], (D, FF), D ** -0.5, 0.375, ((0, 32),), (0, 1, 32, 2.75), jnp.float32),
        "feed_output": bell_draw_with(arg_keys[10], (FF, D), (FF // 4) ** -0.5, 0.375, ((0, 32),), (0, 1, 32, 2.75), jnp.float32),
        "norm_gains": jnp.clip(1.0 + 0.1 * jax.random.normal(arg_keys[11], (4, D), jnp.float32), 0.5, 1.5).astype(jnp.bfloat16),
        "norm_biases": centred(arg_keys[12], (4, D), 0.1, 0.59765625, ((1, 32),)),
    }


@jax.custom_vjp
def low(v):
    return lax.optimization_barrier(v.astype(jnp.bfloat16)).astype(jnp.float32)

@jax.custom_vjp
def low_back(v):
    return v

def low_keep(v):
    return (low(v), None)

def low_pass(kept, grad):
    return (grad,)

def back_keep(v):
    return (v, None)

def back_low(kept, grad):
    return (low(grad),)
low.defvjp(low_keep, low_pass)
low_back.defvjp(back_keep, back_low)

def matmul_high(left, right):
    return jnp.dot(left, right, precision=lax.Precision.HIGHEST)

def layer_norm(values, gain_row, bias_row):
    centre = values - lax.optimization_barrier(jnp.mean(values, axis=-1, keepdims=True))
    spread = lax.optimization_barrier(jnp.mean(centre * centre, axis=-1, keepdims=True))
    return centre * lax.rsqrt(spread + 1e-05) * gain_row + bias_row

def attention(queries, key_rows, value_rows, visible):
    row_count = queries.shape[0]
    key_count = key_rows.shape[0]
    query_heads = queries.reshape(row_count, HEADS, HEAD)
    key_heads = key_rows.reshape(key_count, HEADS, HEAD)
    value_heads = value_rows.reshape(key_count, HEADS, HEAD)
    scores = jnp.einsum('qhd,khd->hqk', query_heads, key_heads, precision=lax.Precision.HIGHEST)
    scores = low_back(scores) * HEAD ** (-0.5)
    scores = jnp.where(visible[None], scores, -1e+30)
    weights = jax.nn.softmax(scores, axis=-1)
    mixed_heads = jnp.einsum('hqk,khd->qhd', low(weights), value_heads, precision=lax.Precision.HIGHEST)
    return low(low_back(mixed_heads.reshape(row_count, HEADS * HEAD)))

def layer(params, layer_input, encoded, unit_length, text_length):
    self_project, self_output, cross_project, cross_output, feed_input, feed_output, gain_table, bias_table = params
    self_project = low(self_project)
    self_output = low(self_output)
    cross_project = low(cross_project)
    cross_output = low(cross_output)
    feed_input = low(feed_input)
    feed_output = low(feed_output)
    model_width = layer_input.shape[1]
    position = jnp.arange(UNITS, dtype=jnp.int32)
    causal = (position[None, :] <= position[:, None]) & (position[None, :] < unit_length)
    text_visible = jnp.broadcast_to(jnp.arange(TEXT, dtype=jnp.int32)[None, :] < text_length, (UNITS, TEXT))
    normed = low(layer_norm(layer_input, gain_table[0], bias_table[0]))
    projected = low(low_back(matmul_high(normed, self_project)))
    self_mixed = attention(projected[:, :model_width], projected[:, model_width:2 * model_width], projected[:, 2 * model_width:], causal)
    after_self = layer_input + low_back(matmul_high(self_mixed, self_output))
    normed_cross = low(layer_norm(after_self, gain_table[1], bias_table[1]))
    cross_queries = low(low_back(matmul_high(normed_cross, cross_project[:, :model_width])))
    cross_kv = low(low_back(matmul_high(encoded, cross_project[:, model_width:])))
    cross_mixed = attention(cross_queries, cross_kv[:, :model_width], cross_kv[:, model_width:], text_visible)
    after_cross = after_self + low_back(matmul_high(cross_mixed, cross_output))
    normed_feed = low(layer_norm(after_cross, gain_table[2], bias_table[2]))
    hidden_pre = low_back(matmul_high(normed_feed, feed_input))
    hidden = low(jax.nn.gelu(hidden_pre, approximate=False))
    after_feed = after_cross + low_back(matmul_high(hidden, feed_output))
    return layer_norm(after_feed, gain_table[3], bias_table[3])

def reference(unit_states, encoder_states, cotangent, unit_lengths, text_lengths, self_project, self_output, cross_project, cross_output, feed_input, feed_output, norm_gains, norm_biases):
    params = (self_project, self_output, cross_project, cross_output, feed_input, feed_output, norm_gains.astype(jnp.float32), norm_biases.astype(jnp.float32))

    def one_sequence(running, sequence):
        states, encoded, grad_out, unit_length, text_length = sequence

        def apply(weights_all, states_float, encoded_float):
            return layer(weights_all, states_float, encoded_float, unit_length, text_length)
        output, pullback = jax.vjp(apply, params, states.astype(jnp.float32), encoded.astype(jnp.float32))
        row_live = (jnp.arange(UNITS, dtype=jnp.int32) < unit_length).astype(jnp.float32)
        grad_params, grad_input, grad_encoded = pullback(grad_out.astype(jnp.float32) * row_live[:, None])
        running = jax.tree.map(lambda total_sum, addend: total_sum + addend, running, grad_params)
        return (running, (output.astype(jnp.bfloat16), grad_input, grad_encoded))
    zeros = jax.tree.map(jnp.zeros_like, params)
    grads, outputs = lax.scan(one_sequence, zeros, (unit_states, encoder_states, cotangent, unit_lengths, text_lengths))
    block_output, grad_states, grad_encoder = outputs
    return (block_output, grad_states, grad_encoder, grads[0], grads[1], grads[2], grads[3], grads[4], grads[5], grads[6], grads[7])
```

```python
import functools

import jax
import jax.numpy as jnp
from jax import lax
from jax.experimental import pallas as pl
from jax.experimental.pallas import tpu as pltpu
from jax.sharding import PartitionSpec as P

HEAD = 64
LANES = 128
BOTH = ("dp", "fsdp")
VMEM_BYTES = 60 * 1024 * 1024
TAIL_RATE = 0.2316419
TAIL_POLY = (
    0.09252224973357535,
    0.09042007971374488,
    0.10265042640370807,
    0.013551821473999732,
    0.2252533241128307,
    -0.2016603378863937,
    0.24768663093443657,
    -0.07042413008644138,
)


def product(left, right):
    return jnp.dot(left, right, preferred_element_type=jnp.float32)


def contract_rows(left, right):
    return lax.dot_general(
        left, right, (((0,), (0,)), ((), ())), preferred_element_type=jnp.float32
    )


def times_transposed(left, right):
    return lax.dot_general(
        left, right, (((1,), (1,)), ((), ())), preferred_element_type=jnp.float32
    )


def layer_norm(values, gain_row, bias_row):
    centre = values - jnp.mean(values, axis=-1, keepdims=True)
    spread = jnp.mean(centre * centre, axis=-1, keepdims=True)
    return centre * lax.rsqrt(spread + 1e-05) * gain_row + bias_row


def norm_backward(values, gain_row, grad):
    centre = values - jnp.mean(values, axis=-1, keepdims=True)
    rate = lax.rsqrt(jnp.mean(centre * centre, axis=-1, keepdims=True) + 1e-05)
    normed = centre * rate
    scaled = grad * gain_row
    grad_input = rate * (
        scaled
        - jnp.mean(scaled, axis=-1, keepdims=True)
        - normed * jnp.mean(scaled * normed, axis=-1, keepdims=True)
    )
    return grad_input, jnp.sum(grad * normed, axis=0), jnp.sum(grad, axis=0)


def masked_scores(keys, queries, key_limit, causal, query_start):
    scores = times_transposed(keys, queries)
    key_count, query_count = scores.shape
    if not causal:
        row = lax.broadcasted_iota(jnp.int32, scores.shape, 0)
        return jnp.where(row < key_limit, scores, -1e30)
    row = query_start + lax.broadcasted_iota(jnp.int32, (query_count, query_count), 0)
    column = query_start + lax.broadcasted_iota(jnp.int32, (query_count, query_count), 1)
    diagonal = jnp.where(
        (row <= column) & (row < key_limit), scores[query_start:, :], -1e30
    )
    if query_start == 0:
        return diagonal
    below_row = lax.broadcasted_iota(jnp.int32, (query_start, query_count), 0)
    below = jnp.where(below_row < key_limit, scores[:query_start, :], -1e30)
    return jnp.concatenate([below, diagonal], axis=0)


def query_blocks(row_count, key_count, causal):
    width = 256 if row_count % 256 == 0 else row_count
    return [
        (start, width, start + width if causal else key_count)
        for start in range(0, row_count, width)
    ]


def head_lanes(head, shape):
    lane = lax.broadcasted_iota(jnp.int32, shape, 1)
    return (lane >= head * HEAD) & (lane < (head + 1) * HEAD)


def attention_forward_kernel(causal, limit_ref, q_ref, k_ref, v_ref, mixed_ref, total_ref, mixed_turned):
    key_limit = limit_ref[0]
    row_count, key_count = q_ref.shape[0], k_ref.shape[0]
    values_turned = v_ref[...].T
    scaled = q_ref[...] * jnp.bfloat16(HEAD**-0.5)
    for head in range(2):
        own = jnp.where(head_lanes(head, scaled.shape), scaled, jnp.zeros_like(scaled))
        lanes = slice(head * HEAD, (head + 1) * HEAD)
        for start, width, stop in query_blocks(row_count, key_count, causal):
            scores = masked_scores(
                k_ref[:stop, :], own[start : start + width, :], key_limit, causal, start
            )
            highest = jnp.max(scores, axis=0, keepdims=True)
            expanded = jnp.exp(scores - highest)
            total = jnp.sum(expanded, axis=0, keepdims=True)
            mixed = product(values_turned[lanes, :stop], expanded.astype(jnp.bfloat16))
            mixed_turned[lanes, start : start + width] = mixed / total
            total_ref[0, head : head + 1, start : start + width] = highest + jnp.log(total)
    mixed_ref[...] = mixed_turned[...].T.astype(jnp.bfloat16)


def attention_forward(limit, queries, q_at, keys, k_at, values, v_at, causal):
    row_count, key_count = queries.shape[0], keys.shape[0]
    width = 1024
    pairs = width // LANES
    cost = pl.CostEstimate(
        flops=4 * row_count * key_count * width,
        transcendentals=row_count * key_count * pairs * 2,
        bytes_accessed=4 * row_count * width + 4 * key_count * width,
    )
    return pl.pallas_call(
        functools.partial(attention_forward_kernel, causal),
        grid_spec=pltpu.PrefetchScalarGridSpec(
            num_scalar_prefetch=1,
            grid=(pairs,),
            in_specs=[
                pl.BlockSpec((row_count, LANES), lambda p, s: (0, q_at + p)),
                pl.BlockSpec((key_count, LANES), lambda p, s: (0, k_at + p)),
                pl.BlockSpec((key_count, LANES), lambda p, s: (0, v_at + p)),
            ],
            out_specs=[
                pl.BlockSpec((row_count, LANES), lambda p, s: (0, p)),
                pl.BlockSpec((1, 2, row_count), lambda p, s: (p, 0, 0)),
            ],
            scratch_shapes=[pltpu.VMEM((LANES, row_count), jnp.float32)],
        ),
        out_shape=[
            jax.ShapeDtypeStruct((row_count, width), jnp.bfloat16),
            jax.ShapeDtypeStruct((pairs, 2, row_count), jnp.float32),
        ],
        compiler_params=pltpu.CompilerParams(vmem_limit_bytes=VMEM_BYTES),
        cost_estimate=cost,
        name="attention_forward",
    )(limit, queries, keys, values)


def attention_backward_kernel(
    causal,
    limit_ref,
    q_ref,
    k_ref,
    v_ref,
    mixed_ref,
    grad_ref,
    total_ref,
    grad_q_ref,
    grad_k_ref,
    grad_v_ref,
    grad_q_turned,
    grad_k_sum,
    grad_v_sum,
):
    key_limit = limit_ref[0]
    row_count, key_count = q_ref.shape[0], k_ref.shape[0]
    keys_turned = k_ref[...].T
    scaled = q_ref[...] * jnp.bfloat16(HEAD**-0.5)
    grad = grad_ref[...]
    inner_turned = (grad.astype(jnp.float32) * mixed_ref[...].astype(jnp.float32)).T
    grad_k_sum[...] = jnp.zeros_like(grad_k_sum)
    grad_v_sum[...] = jnp.zeros_like(grad_v_sum)
    for head in range(2):
        mask = head_lanes(head, scaled.shape)
        own = jnp.where(mask, scaled, jnp.zeros_like(scaled))
        own_grad = jnp.where(mask, grad, jnp.zeros_like(grad))
        lanes = slice(head * HEAD, (head + 1) * HEAD)
        inner = jnp.sum(inner_turned[lanes, :], axis=0, keepdims=True)
        for start, width, stop in query_blocks(row_count, key_count, causal):
            columns = slice(start, start + width)
            queries, grads = own[columns, :], own_grad[columns, :]
            scores = masked_scores(k_ref[:stop, :], queries, key_limit, causal, start)
            probs = jnp.exp(scores - total_ref[0, head : head + 1, columns])
            grad_v_sum[:stop, :] += product(probs.astype(jnp.bfloat16), grads)
            grad_probs = times_transposed(v_ref[:stop, :], grads)
            grad_scores = (probs * (grad_probs - inner[:, columns])).astype(jnp.bfloat16)
            grad_k_sum[:stop, :] += product(grad_scores, queries)
            grad_q_turned[lanes, columns] = product(keys_turned[lanes, :stop], grad_scores)
    grad_q_ref[...] = (grad_q_turned[...].T * HEAD**-0.5).astype(jnp.bfloat16)
    grad_k_ref[...] = grad_k_sum[...].astype(jnp.bfloat16)
    grad_v_ref[...] = grad_v_sum[...].astype(jnp.bfloat16)


def attention_backward(limit, queries, q_at, keys, k_at, values, v_at, mixed, grad_mixed, totals, causal):
    row_count, key_count = queries.shape[0], keys.shape[0]
    width = 1024
    pairs = width // LANES
    cost = pl.CostEstimate(
        flops=10 * row_count * key_count * width,
        transcendentals=row_count * key_count * pairs * 2,
        bytes_accessed=8 * row_count * width + 8 * key_count * width,
    )
    row_block = pl.BlockSpec((row_count, LANES), lambda p, s: (0, p))
    key_block = pl.BlockSpec((key_count, LANES), lambda p, s: (0, p))
    return pl.pallas_call(
        functools.partial(attention_backward_kernel, causal),
        grid_spec=pltpu.PrefetchScalarGridSpec(
            num_scalar_prefetch=1,
            grid=(pairs,),
            in_specs=[
                pl.BlockSpec((row_count, LANES), lambda p, s: (0, q_at + p)),
                pl.BlockSpec((key_count, LANES), lambda p, s: (0, k_at + p)),
                pl.BlockSpec((key_count, LANES), lambda p, s: (0, v_at + p)),
                row_block,
                row_block,
                pl.BlockSpec((1, 2, row_count), lambda p, s: (p, 0, 0)),
            ],
            out_specs=[row_block, key_block, key_block],
            scratch_shapes=[
                pltpu.VMEM((LANES, row_count), jnp.float32),
                pltpu.VMEM((key_count, LANES), jnp.float32),
                pltpu.VMEM((key_count, LANES), jnp.float32),
            ],
        ),
        out_shape=[
            jax.ShapeDtypeStruct((row_count, width), jnp.bfloat16),
            jax.ShapeDtypeStruct((key_count, width), jnp.bfloat16),
            jax.ShapeDtypeStruct((key_count, width), jnp.bfloat16),
        ],
        compiler_params=pltpu.CompilerParams(vmem_limit_bytes=VMEM_BYTES),
        cost_estimate=cost,
        name="attention_backward",
    )(limit, queries, keys, values, mixed, grad_mixed, totals)


def gelu_and_slope(values):
    size = jnp.abs(values)
    bell = jnp.exp(-0.5 * values * values)
    t = 1.0 / (1.0 + TAIL_RATE * size)
    poly = TAIL_POLY[-1] * t + TAIL_POLY[-2]
    for coefficient in TAIL_POLY[-3::-1]:
        poly = poly * t + coefficient
    tail = poly * t * bell
    normal_cdf = jnp.where(values >= 0, 1.0 - tail, tail)
    return values * normal_cdf, normal_cdf + values * (bell * (2.0 * jnp.pi) ** (-0.5))


def feed_forward_kernel(normed_ref, input_ref, output_ref, base_ref, hidden_ref, slope_ref, after_ref):
    @pl.when(pl.program_id(0) == 0)
    def _():
        after_ref[...] = base_ref[...]

    row_count = normed_ref.shape[0]
    step = 256 if row_count % 256 == 0 else row_count
    for start in range(0, row_count, step):
        rows = slice(start, start + step)
        hidden, slope = gelu_and_slope(product(normed_ref[rows, :], input_ref[...]))
        hidden = hidden.astype(jnp.bfloat16)
        hidden_ref[rows, :] = hidden
        slope_ref[rows, :] = slope.astype(jnp.bfloat16)
        after_ref[rows, :] += product(hidden, output_ref[...])


def feed_forward(normed, input_low, output_low, after_cross):
    row_count, width = normed.shape
    hidden_width = input_low.shape[1]
    tile = 512
    whole = pl.BlockSpec((row_count, width), lambda j: (0, 0))
    tall = pl.BlockSpec((row_count, tile), lambda j: (0, j))
    return pl.pallas_call(
        feed_forward_kernel,
        grid=(hidden_width // tile,),
        in_specs=[
            whole,
            pl.BlockSpec((width, tile), lambda j: (0, j)),
            pl.BlockSpec((tile, width), lambda j: (j, 0)),
            whole,
        ],
        out_specs=[tall, tall, whole],
        out_shape=[
            jax.ShapeDtypeStruct((row_count, hidden_width), jnp.bfloat16),
            jax.ShapeDtypeStruct((row_count, hidden_width), jnp.bfloat16),
            jax.ShapeDtypeStruct((row_count, width), jnp.float32),
        ],
        compiler_params=pltpu.CompilerParams(vmem_limit_bytes=VMEM_BYTES),
        cost_estimate=pl.CostEstimate(
            flops=4 * row_count * width * hidden_width,
            transcendentals=2 * row_count * hidden_width,
            bytes_accessed=4 * width * hidden_width + 4 * row_count * hidden_width,
        ),
        name="feed_forward",
    )(normed, input_low, output_low, after_cross)


def feed_backward_kernel(
    grad_ref,
    turned_ref,
    hidden_ref,
    slope_ref,
    input_ref,
    output_ref,
    grad_in_ref,
    grad_out_ref,
    grad_normed_ref,
):
    @pl.when(pl.program_id(0) == 0)
    def _():
        grad_normed_ref[...] = jnp.zeros_like(grad_normed_ref)

    grad_hidden = times_transposed(grad_ref[...], output_ref[...])
    grad_pre = (grad_hidden * slope_ref[...].astype(jnp.float32)).astype(jnp.bfloat16)
    grad_out_ref[...] = contract_rows(hidden_ref[...], grad_ref[...]).astype(jnp.bfloat16)
    grad_in_ref[...] = product(turned_ref[...], grad_pre).astype(jnp.bfloat16)
    grad_normed_ref[...] += times_transposed(grad_pre, input_ref[...])


def feed_backward(table, grad_branch, normed_turned, hidden, slope, input_low, output_low):
    row_count, width = grad_branch.shape
    hidden_width = hidden.shape[1]
    tile = hidden_width // table.shape[0]
    whole = pl.BlockSpec((row_count, width), lambda j, t: (0, 0))
    tall = pl.BlockSpec((row_count, tile), lambda j, t: (0, t[j]))
    return pl.pallas_call(
        lambda table_ref, *refs: feed_backward_kernel(*refs),
        grid_spec=pltpu.PrefetchScalarGridSpec(
            num_scalar_prefetch=1,
            grid=(hidden_width // tile,),
            in_specs=[
                whole,
                pl.BlockSpec((width, row_count), lambda j, t: (0, 0)),
                tall,
                tall,
                pl.BlockSpec((width, tile), lambda j, t: (0, t[j])),
                pl.BlockSpec((tile, width), lambda j, t: (t[j], 0)),
            ],
            out_specs=[
                pl.BlockSpec((width, tile), lambda j, t: (0, t[j])),
                pl.BlockSpec((tile, width), lambda j, t: (j, 0)),
                whole,
            ],
        ),
        out_shape=[
            jax.ShapeDtypeStruct((width, hidden_width), jnp.bfloat16),
            jax.ShapeDtypeStruct((hidden_width, width), jnp.bfloat16),
            jax.ShapeDtypeStruct((row_count, width), jnp.float32),
        ],
        compiler_params=pltpu.CompilerParams(vmem_limit_bytes=VMEM_BYTES),
        cost_estimate=pl.CostEstimate(
            flops=8 * row_count * width * hidden_width,
            transcendentals=0,
            bytes_accessed=8 * width * hidden_width + 4 * row_count * hidden_width,
        ),
        name="feed_backward",
    )(table, grad_branch, normed_turned, hidden, slope, input_low, output_low)


def place_rows_kernel(starts, table_ref, *refs):
    out_ref = refs[-1]
    step = pl.program_id(0)
    for index, ref in enumerate(refs[:-1]):

        @pl.when((step >= starts[index]) & (step < starts[index + 1]))
        def _(ref=ref):
            out_ref[...] = ref[...]


def place_rows(table, pieces, rows):
    starts = [0]
    for piece in pieces:
        starts.append(starts[-1] + piece.shape[0] // rows)
    columns = pieces[0].shape[1]

    def piece_spec(first, last):
        return pl.BlockSpec((rows, columns), lambda j, t: (jnp.clip(j - first, 0, last - first - 1), 0))

    return pl.pallas_call(
        functools.partial(place_rows_kernel, starts),
        grid_spec=pltpu.PrefetchScalarGridSpec(
            num_scalar_prefetch=1,
            grid=(starts[-1],),
            in_specs=[piece_spec(starts[i], starts[i + 1]) for i in range(len(pieces))],
            out_specs=pl.BlockSpec((rows, columns), lambda j, t: (t[j], 0)),
        ),
        out_shape=jax.ShapeDtypeStruct((starts[-1] * rows, columns), pieces[0].dtype),
        compiler_params=pltpu.CompilerParams(vmem_limit_bytes=VMEM_BYTES),
        cost_estimate=pl.CostEstimate(
            flops=0, transcendentals=0, bytes_accessed=4 * starts[-1] * rows * columns
        ),
        name="place_rows",
    )(table, *pieces)


def turn_blocks_kernel(table_ref, in_ref, out_ref):
    out_ref[...] = in_ref[...].T


def turn_blocks(table, matrix, block):
    row_count = matrix.shape[0]
    count = matrix.shape[1] // block
    return pl.pallas_call(
        turn_blocks_kernel,
        grid_spec=pltpu.PrefetchScalarGridSpec(
            num_scalar_prefetch=1,
            grid=(count,),
            in_specs=[pl.BlockSpec((row_count, block), lambda j, t: (0, t[j]))],
            out_specs=pl.BlockSpec((block, row_count), lambda j, t: (j, 0)),
        ),
        out_shape=jax.ShapeDtypeStruct((matrix.shape[1], row_count), matrix.dtype),
        compiler_params=pltpu.CompilerParams(vmem_limit_bytes=VMEM_BYTES),
        cost_estimate=pl.CostEstimate(flops=0, transcendentals=0, bytes_accessed=4 * matrix.size),
        name="turn_blocks",
    )(table, matrix)


class Links:
    def __init__(self, dp_count, fsdp_count, width):
        self.dp_count, self.fsdp_count = dp_count, fsdp_count
        power = (dp_count & (dp_count - 1)) == 0 and (fsdp_count & (fsdp_count - 1)) == 0
        self.pairwise = power and dp_count > 1 and (width // dp_count) % LANES == 0 and width // dp_count >= 16 * fsdp_count
        self.dp_index = lax.axis_index("dp")
        self.fsdp_index = lax.axis_index("fsdp")
        self.blocks = dp_count if self.pairwise else width // LANES
        self.high_bits = [1 << b for b in range(1, dp_count.bit_length() - 1)]
        if self.pairwise:
            self.fsdp_table = (self.fsdp_index ^ jnp.arange(fsdp_count, dtype=jnp.int32)).astype(jnp.int32)

    def order(self, flip):
        return self.high_bits[::-1] if flip else self.high_bits

    def table(self, masks):
        return (self.dp_index ^ jnp.asarray(masks, dtype=jnp.int32)).astype(jnp.int32)

    def swap(self, array, bit):
        return lax.ppermute(array, "dp", [(i, i ^ bit) for i in range(self.dp_count)])

    def swap_fsdp(self, array, bit):
        return lax.ppermute(array, "fsdp", [(i, i ^ bit) for i in range(self.fsdp_count)])

    def gather(self, shard, flip):
        if not self.pairwise:
            return lax.all_gather(shard, BOTH, axis=0, tiled=True)
        return self.spread(self.gather_fsdp(shard), flip)

    def gather_fsdp(self, shard):
        parts = [shard] + [self.swap_fsdp(shard, k) for k in range(1, self.fsdp_count)]
        return place_rows(self.fsdp_table, parts, shard.shape[0])

    def spread(self, block, flip):
        pieces, masks = [block], [0]
        for bit in self.order(flip) + [1]:
            pieces = pieces + [self.swap(piece, bit) for piece in pieces]
            masks = masks + [mask ^ bit for mask in masks]
        return place_rows(self.table(masks), pieces, block.shape[0])

    def row_masks(self, flip):
        if not self.pairwise:
            return None
        masks = [0]
        for bit in self.order(flip) + [1]:
            masks = [mask ^ bit for mask in masks] + masks
        return masks

    def row_table(self, flip):
        if not self.pairwise:
            return jnp.arange(self.blocks, dtype=jnp.int32)
        return self.table(self.row_masks(flip))

    def scatter(self, grad, flip):
        if not self.pairwise:
            part = lax.psum_scatter(grad.astype(jnp.float32), "dp", scatter_dimension=0, tiled=True)
            return lax.psum_scatter(part, "fsdp", scatter_dimension=0, tiled=True)
        for bit in [1] + self.order(flip)[::-1]:
            half = grad.shape[0] // 2
            other = self.swap(grad[:half], bit)
            grad = (grad[half:].astype(jnp.float32) + other.astype(jnp.float32)).astype(jnp.bfloat16)
        rows = grad.shape[0] // self.fsdp_count

        def block(index):
            return lax.dynamic_slice_in_dim(grad, index * rows, rows, 0)

        total = block(self.fsdp_index).astype(jnp.float32)
        for k in range(1, self.fsdp_count):
            total = total + self.swap_fsdp(block(self.fsdp_index ^ k), k).astype(jnp.float32)
        return total


def body(
    unit_states,
    encoder_states,
    cotangent,
    unit_lengths,
    text_lengths,
    self_project,
    self_output,
    cross_project,
    cross_output,
    feed_input,
    feed_output,
    norm_gains,
    norm_biases,
):
    low = jnp.bfloat16
    layer_input = unit_states[0].astype(jnp.float32)
    encoded = encoder_states[0]
    row_count, width = layer_input.shape
    links = Links(lax.axis_size("dp"), lax.axis_size("fsdp"), width)
    shard_rows = self_project.shape[0]

    tables = jnp.concatenate([norm_gains, norm_biases], axis=0).T
    tables = jnp.pad(tables, ((0, 0), (0, LANES - tables.shape[1])))
    self_shard = jnp.concatenate([self_project.astype(low), self_output.astype(low), tables], axis=1)
    cross_shard = jnp.concatenate([cross_project.astype(low), cross_output.astype(low)], axis=1)
    if links.pairwise:
        self_part = links.gather_fsdp(self_shard)
        cross_part = links.gather_fsdp(cross_shard)
        self_first = links.spread(self_part[:, : 2 * width], False)
        self_second = links.spread(self_part[:, 2 * width :], True)
        cross_first = links.spread(cross_part[:, width : 3 * width], False)
        cross_second = links.spread(
            jnp.concatenate([cross_part[:, :width], cross_part[:, 3 * width :]], axis=1), True
        )
    else:
        self_whole = links.gather(self_shard, False)
        cross_whole = links.gather(cross_shard, False)
        self_first, self_second = self_whole[:, : 2 * width], self_whole[:, 2 * width :]
        cross_first = cross_whole[:, width : 3 * width]
        cross_second = jnp.concatenate([cross_whole[:, :width], cross_whole[:, 3 * width :]], axis=1)
    feed_input_low = links.gather(feed_input.astype(low), False)
    feed_output_low = links.gather(feed_output.astype(low), True)

    self_value, self_output_low = self_second[:, :width], self_second[:, width : 2 * width]
    norm_rows = self_second[:, 2 * width : 2 * width + 8].astype(jnp.float32).T
    gain_table, bias_table = norm_rows[:4], norm_rows[4:]
    cross_query, cross_output_low = cross_second[:, :width], cross_second[:, width:]

    normed_self = layer_norm(layer_input, gain_table[0], bias_table[0]).astype(low)
    query_key = product(normed_self, self_first).astype(low)
    self_values = product(normed_self, self_value).astype(low)
    self_mixed, self_totals = attention_forward(
        unit_lengths, query_key, 0, query_key, width // LANES, self_values, 0, True
    )
    after_self = layer_input + product(self_mixed, self_output_low)
    normed_cross = layer_norm(after_self, gain_table[1], bias_table[1]).astype(low)
    cross_queries = product(normed_cross, cross_query).astype(low)
    cross_kv = product(encoded, cross_first).astype(low)
    cross_mixed, cross_totals = attention_forward(
        text_lengths, cross_queries, 0, cross_kv, 0, cross_kv, width // LANES, False
    )
    after_cross = after_self + product(cross_mixed, cross_output_low)
    normed_feed = layer_norm(after_cross, gain_table[2], bias_table[2]).astype(low)
    hidden, slope, after_feed = feed_forward(normed_feed, feed_input_low, feed_output_low, after_cross)
    block_output = layer_norm(after_feed, gain_table[3], bias_table[3]).astype(low)

    row_live = (jnp.arange(row_count, dtype=jnp.int32) < unit_lengths[0]).astype(jnp.float32)
    grad_y = cotangent[0] * row_live[:, None]
    grad_after_feed, grad_gain_3, grad_bias_3 = norm_backward(after_feed, gain_table[3], grad_y)
    first_rows, second_rows = links.row_table(False), links.row_table(True)
    lane_block = width // links.blocks
    grad_feed_in, grad_feed_out, grad_normed = feed_backward(
        first_rows,
        grad_after_feed.astype(low),
        turn_blocks(second_rows, normed_feed, lane_block),
        hidden,
        slope,
        feed_input_low,
        feed_output_low,
    )
    feed_out_part = links.scatter(grad_feed_out, False)
    feed_in_part = links.scatter(grad_feed_in, True)
    grad_input, grad_gain_2, grad_bias_2 = norm_backward(after_cross, gain_table[2], grad_normed)
    grad_after_cross = grad_after_feed + grad_input

    cross_branch = grad_after_cross.astype(low)
    grad_cross_mixed = times_transposed(cross_branch, cross_output_low).astype(low)
    grad_cross_out = product(turn_blocks(first_rows, cross_mixed, lane_block), cross_branch).astype(low)
    cross_out_part = links.scatter(grad_cross_out, False)
    grad_q, grad_k, grad_v = attention_backward(
        text_lengths,
        cross_queries,
        0,
        cross_kv,
        0,
        cross_kv,
        width // LANES,
        cross_mixed,
        grad_cross_mixed,
        cross_totals,
        False,
    )
    grad_kv = jnp.concatenate([grad_k, grad_v], axis=1)
    grad_cross_query = product(turn_blocks(first_rows, normed_cross, lane_block), grad_q).astype(low)
    grad_cross_kv = product(turn_blocks(second_rows, encoded, lane_block), grad_kv).astype(low)
    cross_query_part = links.scatter(grad_cross_query, False)
    cross_kv_part = links.scatter(grad_cross_kv, True)
    grad_normed = times_transposed(grad_q, cross_query)
    grad_encoded = times_transposed(grad_kv, cross_first)
    grad_input, grad_gain_1, grad_bias_1 = norm_backward(after_self, gain_table[1], grad_normed)
    grad_after_self = grad_after_cross + grad_input

    self_branch = grad_after_self.astype(low)
    grad_self_mixed = times_transposed(self_branch, self_output_low).astype(low)
    grad_self_out = product(turn_blocks(first_rows, self_mixed, lane_block), self_branch).astype(low)
    self_out_part = links.scatter(grad_self_out, False)
    grad_q, grad_k, grad_v = attention_backward(
        unit_lengths,
        query_key,
        0,
        query_key,
        width // LANES,
        self_values,
        0,
        self_mixed,
        grad_self_mixed,
        self_totals,
        True,
    )
    grad_qk = jnp.concatenate([grad_q, grad_k], axis=1)
    grad_normed = times_transposed(grad_qk, self_first) + times_transposed(grad_v, self_value)
    grad_input, grad_gain_0, grad_bias_0 = norm_backward(layer_input, gain_table[0], grad_normed)
    grad_states = grad_after_self + grad_input
    grad_tables = jnp.stack(
        [grad_gain_0, grad_gain_1, grad_gain_2, grad_gain_3, grad_bias_0, grad_bias_1, grad_bias_2, grad_bias_3]
    )
    grad_tables = jnp.pad(grad_tables.T, ((0, 0), (0, LANES - 8))).astype(low)
    self_turned = turn_blocks(first_rows, normed_self, lane_block)
    if links.pairwise:
        grad_tables = place_rows(jnp.arange(links.blocks, dtype=jnp.int32), [
            lax.dynamic_slice_in_dim(grad_tables, first_rows[j] * lane_block, lane_block, 0)
            for j in range(links.blocks)
        ], lane_block)
    grad_self_qk = product(self_turned, grad_qk).astype(low)
    grad_self_v = product(turn_blocks(second_rows, normed_self, lane_block), grad_v).astype(low)
    self_qk_part = links.scatter(grad_self_qk, False)
    self_v_part = links.scatter(grad_self_v, True)
    table_part = links.scatter(grad_tables, False)

    return (
        block_output[None],
        grad_states[None],
        grad_encoded[None],
        jnp.concatenate([self_qk_part, self_v_part], axis=1),
        self_out_part,
        jnp.concatenate([cross_query_part, cross_kv_part], axis=1),
        cross_out_part,
        feed_in_part,
        feed_out_part,
        table_part[:, :4].T,
        table_part[:, 4:8].T,
    )


def solution(mesh):
    return jax.shard_map(
        body,
        mesh=mesh,
        in_specs=(
            P(BOTH, None, None),
            P(BOTH, None, None),
            P(BOTH, None, None),
            P(BOTH),
            P(BOTH),
            P(BOTH, None),
            P(BOTH, None),
            P(BOTH, None),
            P(BOTH, None),
            P(BOTH, None),
            P(BOTH, None),
            P(None, BOTH),
            P(None, BOTH),
        ),
        out_specs=(
            P(BOTH, None, None),
            P(BOTH, None, None),
            P(BOTH, None, None),
            P(BOTH, None),
            P(BOTH, None),
            P(BOTH, None),
            P(BOTH, None),
            P(BOTH, None),
            P(BOTH, None),
            P(None, BOTH),
            P(None, BOTH),
        ),
        check_vma=False,
    )
```

```python
import functools

import jax
import jax.numpy as jnp
from jax import lax
from jax.experimental import pallas as pl
from jax.experimental.pallas import tpu as pltpu
from jax.sharding import Mesh
from jax.sharding import PartitionSpec as P

HEAD = 64
LANES = 128
BOTH = ("h", "c", "fsdp")
VMEM_BYTES = 60 * 1024 * 1024
SHORT = pl.CostEstimate(flops=1024, transcendentals=0, bytes_accessed=1024)
TAIL_RATE = 0.2316419
TAIL_POLY = (
    0.09252224973357535,
    0.09042007971374488,
    0.10265042640370807,
    0.013551821473999732,
    0.2252533241128307,
    -0.2016603378863937,
    0.24768663093443657,
    -0.07042413008644138,
)


def product(left, right):
    return jnp.dot(left, right, preferred_element_type=jnp.float32)


def contract_rows(left, right):
    return lax.dot_general(
        left, right, (((0,), (0,)), ((), ())), preferred_element_type=jnp.float32
    )


def times_transposed(left, right):
    return lax.dot_general(
        left, right, (((1,), (1,)), ((), ())), preferred_element_type=jnp.float32
    )


def layer_norm(values, gain_row, bias_row):
    centre = values - jnp.mean(values, axis=-1, keepdims=True)
    spread = jnp.mean(centre * centre, axis=-1, keepdims=True)
    return centre * lax.rsqrt(spread + 1e-05) * gain_row + bias_row


def norm_backward(values, gain_row, grad):
    centre = values - jnp.mean(values, axis=-1, keepdims=True)
    rate = lax.rsqrt(jnp.mean(centre * centre, axis=-1, keepdims=True) + 1e-05)
    normed = centre * rate
    scaled = grad * gain_row
    grad_input = rate * (
        scaled
        - jnp.mean(scaled, axis=-1, keepdims=True)
        - normed * jnp.mean(scaled * normed, axis=-1, keepdims=True)
    )
    return grad_input, jnp.sum(grad * normed, axis=0), jnp.sum(grad, axis=0)


def masked_scores(keys, queries, key_limit, causal, query_start):
    scores = times_transposed(keys, queries)
    key_count, query_count = scores.shape
    if not causal:
        row = lax.broadcasted_iota(jnp.int32, scores.shape, 0)
        return jnp.where(row < key_limit, scores, -1e30)
    row = query_start + lax.broadcasted_iota(jnp.int32, (query_count, query_count), 0)
    column = query_start + lax.broadcasted_iota(jnp.int32, (query_count, query_count), 1)
    diagonal = jnp.where(
        (row <= column) & (row < key_limit), scores[query_start:, :], -1e30
    )
    if query_start == 0:
        return diagonal
    below_row = lax.broadcasted_iota(jnp.int32, (query_start, query_count), 0)
    below = jnp.where(below_row < key_limit, scores[:query_start, :], -1e30)
    return jnp.concatenate([below, diagonal], axis=0)


def query_blocks(row_count, key_count, causal):
    width = 256 if row_count % 256 == 0 else row_count
    return [
        (start, width, start + width if causal else key_count)
        for start in range(0, row_count, width)
    ]


def head_lanes(head, shape):
    lane = lax.broadcasted_iota(jnp.int32, shape, 1)
    return (lane >= head * HEAD) & (lane < (head + 1) * HEAD)


def attention_forward_kernel(causal, limit_ref, q_ref, k_ref, v_ref, mixed_ref, total_ref, mixed_turned):
    key_limit = limit_ref[0]
    row_count, key_count = q_ref.shape[0], k_ref.shape[0]
    values_turned = v_ref[...].T
    scaled = q_ref[...] * jnp.bfloat16(HEAD**-0.5)
    for head in range(2):
        own = jnp.where(head_lanes(head, scaled.shape), scaled, jnp.zeros_like(scaled))
        lanes = slice(head * HEAD, (head + 1) * HEAD)
        for start, width, stop in query_blocks(row_count, key_count, causal):
            scores = masked_scores(
                k_ref[:stop, :], own[start : start + width, :], key_limit, causal, start
            )
            highest = jnp.max(scores, axis=0, keepdims=True)
            expanded = jnp.exp(scores - highest)
            total = jnp.sum(expanded, axis=0, keepdims=True)
            mixed = product(values_turned[lanes, :stop], expanded.astype(jnp.bfloat16))
            mixed_turned[lanes, start : start + width] = mixed / total
            total_ref[0, head : head + 1, start : start + width] = highest + jnp.log(total)
    mixed_ref[...] = mixed_turned[...].T.astype(jnp.bfloat16)


def attention_forward(limit, queries, q_at, keys, k_at, values, v_at, causal):
    row_count, key_count = queries.shape[0], keys.shape[0]
    width = 1024
    pairs = width // LANES
    return pl.pallas_call(
        functools.partial(attention_forward_kernel, causal),
        grid_spec=pltpu.PrefetchScalarGridSpec(
            num_scalar_prefetch=1,
            grid=(pairs,),
            in_specs=[
                pl.BlockSpec((row_count, LANES), lambda p, s: (0, q_at + p)),
                pl.BlockSpec((key_count, LANES), lambda p, s: (0, k_at + p)),
                pl.BlockSpec((key_count, LANES), lambda p, s: (0, v_at + p)),
            ],
            out_specs=[
                pl.BlockSpec((row_count, LANES), lambda p, s: (0, p)),
                pl.BlockSpec((1, 2, row_count), lambda p, s: (p, 0, 0)),
            ],
            scratch_shapes=[pltpu.VMEM((LANES, row_count), jnp.float32)],
        ),
        out_shape=[
            jax.ShapeDtypeStruct((row_count, width), jnp.bfloat16),
            jax.ShapeDtypeStruct((pairs, 2, row_count), jnp.float32),
        ],
        compiler_params=pltpu.CompilerParams(vmem_limit_bytes=VMEM_BYTES),
        cost_estimate=SHORT,
        name="attention_forward",
    )(limit, queries, keys, values)


def attention_backward_kernel(
    causal,
    limit_ref,
    q_ref,
    k_ref,
    v_ref,
    mixed_ref,
    grad_ref,
    total_ref,
    grad_q_ref,
    grad_k_ref,
    grad_v_ref,
    grad_q_turned,
    grad_k_sum,
    grad_v_sum,
):
    key_limit = limit_ref[0]
    row_count, key_count = q_ref.shape[0], k_ref.shape[0]
    keys_turned = k_ref[...].T
    scaled = q_ref[...] * jnp.bfloat16(HEAD**-0.5)
    grad = grad_ref[...]
    inner_turned = (grad.astype(jnp.float32) * mixed_ref[...].astype(jnp.float32)).T
    grad_k_sum[...] = jnp.zeros_like(grad_k_sum)
    grad_v_sum[...] = jnp.zeros_like(grad_v_sum)
    for head in range(2):
        mask = head_lanes(head, scaled.shape)
        own = jnp.where(mask, scaled, jnp.zeros_like(scaled))
        own_grad = jnp.where(mask, grad, jnp.zeros_like(grad))
        lanes = slice(head * HEAD, (head + 1) * HEAD)
        inner = jnp.sum(inner_turned[lanes, :], axis=0, keepdims=True)
        for start, width, stop in query_blocks(row_count, key_count, causal):
            columns = slice(start, start + width)
            queries, grads = own[columns, :], own_grad[columns, :]
            scores = masked_scores(k_ref[:stop, :], queries, key_limit, causal, start)
            probs = jnp.exp(scores - total_ref[0, head : head + 1, columns])
            grad_v_sum[:stop, :] += product(probs.astype(jnp.bfloat16), grads)
            grad_probs = times_transposed(v_ref[:stop, :], grads)
            grad_scores = (probs * (grad_probs - inner[:, columns])).astype(jnp.bfloat16)
            grad_k_sum[:stop, :] += product(grad_scores, queries)
            grad_q_turned[lanes, columns] = product(keys_turned[lanes, :stop], grad_scores)
    grad_q_ref[...] = (grad_q_turned[...].T * HEAD**-0.5).astype(jnp.bfloat16)
    grad_k_ref[...] = grad_k_sum[...].astype(jnp.bfloat16)
    grad_v_ref[...] = grad_v_sum[...].astype(jnp.bfloat16)


def attention_backward(limit, queries, q_at, keys, k_at, values, v_at, mixed, grad_mixed, totals, causal):
    row_count, key_count = queries.shape[0], keys.shape[0]
    width = 1024
    pairs = width // LANES
    row_block = pl.BlockSpec((row_count, LANES), lambda p, s: (0, p))
    key_block = pl.BlockSpec((key_count, LANES), lambda p, s: (0, p))
    return pl.pallas_call(
        functools.partial(attention_backward_kernel, causal),
        grid_spec=pltpu.PrefetchScalarGridSpec(
            num_scalar_prefetch=1,
            grid=(pairs,),
            in_specs=[
                pl.BlockSpec((row_count, LANES), lambda p, s: (0, q_at + p)),
                pl.BlockSpec((key_count, LANES), lambda p, s: (0, k_at + p)),
                pl.BlockSpec((key_count, LANES), lambda p, s: (0, v_at + p)),
                row_block,
                row_block,
                pl.BlockSpec((1, 2, row_count), lambda p, s: (p, 0, 0)),
            ],
            out_specs=[row_block, key_block, key_block],
            scratch_shapes=[
                pltpu.VMEM((LANES, row_count), jnp.float32),
                pltpu.VMEM((key_count, LANES), jnp.float32),
                pltpu.VMEM((key_count, LANES), jnp.float32),
            ],
        ),
        out_shape=[
            jax.ShapeDtypeStruct((row_count, width), jnp.bfloat16),
            jax.ShapeDtypeStruct((key_count, width), jnp.bfloat16),
            jax.ShapeDtypeStruct((key_count, width), jnp.bfloat16),
        ],
        compiler_params=pltpu.CompilerParams(vmem_limit_bytes=VMEM_BYTES),
        cost_estimate=SHORT,
        name="attention_backward",
    )(limit, queries, keys, values, mixed, grad_mixed, totals)


def gelu_and_slope(values):
    size = jnp.abs(values)
    bell = jnp.exp(-0.5 * values * values)
    t = 1.0 / (1.0 + TAIL_RATE * size)
    poly = TAIL_POLY[-1] * t + TAIL_POLY[-2]
    for coefficient in TAIL_POLY[-3::-1]:
        poly = poly * t + coefficient
    tail = poly * t * bell
    normal_cdf = jnp.where(values >= 0, 1.0 - tail, tail)
    return values * normal_cdf, normal_cdf + values * (bell * (2.0 * jnp.pi) ** (-0.5))


def unfold_rows(folded_ref, unfolded, rows):
    width = unfolded.shape[1]
    folds = folded_ref.shape[1] // width
    for shard in range(folded_ref.shape[0] // rows):
        for fold in range(folds):
            start = (shard * folds + fold) * rows
            unfolded[start : start + rows, :] = folded_ref[
                shard * rows : (shard + 1) * rows, fold * width : (fold + 1) * width
            ]


def fold_rows(unfolded, folded_ref, rows):
    width = unfolded.shape[1]
    folds = folded_ref.shape[1] // width
    for shard in range(folded_ref.shape[0] // rows):
        for fold in range(folds):
            start = (shard * folds + fold) * rows
            folded_ref[shard * rows : (shard + 1) * rows, fold * width : (fold + 1) * width] = unfolded[
                start : start + rows, :
            ]


def feed_forward_kernel(
    rows, normed_ref, input_ref, output_ref, base_ref, hidden_ref, slope_ref, after_ref, unfolded
):
    if rows:
        unfold_rows(output_ref, unfolded, rows)
        output_ref = unfolded

    @pl.when(pl.program_id(0) == 0)
    def _():
        after_ref[...] = base_ref[...]

    row_count = normed_ref.shape[0]
    step = 256 if row_count % 256 == 0 else row_count
    for start in range(0, row_count, step):
        rows = slice(start, start + step)
        hidden, slope = gelu_and_slope(product(normed_ref[rows, :], input_ref[...]))
        hidden = hidden.astype(jnp.bfloat16)
        hidden_ref[rows, :] = hidden
        slope_ref[rows, :] = slope.astype(jnp.bfloat16)
        after_ref[rows, :] += product(hidden, output_ref[...])


FEED_TILE = 512


def feed_weight_specs(folds, width, tile, index):
    first = pl.BlockSpec((width, tile), lambda *at: (0, index(*at)))
    if folds:
        return first, pl.BlockSpec((tile // folds, folds * width), lambda *at: (index(*at), 1))
    return first, pl.BlockSpec((tile, width), lambda *at: (index(*at), 0))


def feed_forward(rows, normed, input_low, output_low, after_cross):
    row_count, width = normed.shape
    hidden_width = 4 * width
    tile = FEED_TILE
    whole = pl.BlockSpec((row_count, width), lambda j: (0, 0))
    tall = pl.BlockSpec((row_count, tile), lambda j: (0, j))
    weight_specs = feed_weight_specs(hidden_width // width if rows else 0, width, tile, lambda j: j)
    return pl.pallas_call(
        functools.partial(feed_forward_kernel, rows),
        grid=(hidden_width // tile,),
        in_specs=[whole, *weight_specs, whole],
        out_specs=[tall, tall, whole],
        out_shape=[
            jax.ShapeDtypeStruct((row_count, hidden_width), jnp.bfloat16),
            jax.ShapeDtypeStruct((row_count, hidden_width), jnp.bfloat16),
            jax.ShapeDtypeStruct((row_count, width), jnp.float32),
        ],
        scratch_shapes=[pltpu.VMEM((tile, width), jnp.bfloat16)],
        compiler_params=pltpu.CompilerParams(vmem_limit_bytes=VMEM_BYTES),
        cost_estimate=SHORT,
        name="feed_forward",
    )(normed, input_low, output_low, after_cross)


def turn_rows(x_ref, turned, positions_ref):
    for j in range(x_ref.shape[1] // LANES):
        start = pl.multiple_of(positions_ref[j] * LANES, LANES)
        turned[pl.ds(start, LANES), :] = x_ref[:, j * LANES : (j + 1) * LANES].T


def feed_backward_kernel(
    rows,
    half_blocks,
    positions_ref,
    grad_ref,
    normed_ref,
    hidden_ref,
    slope_ref,
    input_ref,
    output_ref,
    in_send_ref,
    in_keep_ref,
    out_ref,
    grad_normed_ref,
    turned,
    unfolded,
):
    step = pl.program_id(0)
    if rows:
        unfold_rows(output_ref, unfolded, rows)
        output_ref = unfolded

    @pl.when(step == 0)
    def _():
        grad_normed_ref[...] = jnp.zeros_like(grad_normed_ref)
        turn_rows(normed_ref, turned, positions_ref)

    grad_hidden = times_transposed(grad_ref[...], output_ref[...])
    grad_pre = (grad_hidden * slope_ref[...].astype(jnp.float32)).astype(jnp.bfloat16)
    grad_out = contract_rows(hidden_ref[...], grad_ref[...]).astype(jnp.bfloat16)
    if rows:
        fold_rows(grad_out, out_ref, rows)
    else:
        out_ref[...] = grad_out
    half = turned.shape[0] // 2
    in_send_ref[...] = product(turned[:half, :], grad_pre).astype(jnp.bfloat16)
    in_keep_ref[...] = product(turned[half:, :], grad_pre).astype(jnp.bfloat16)
    grad_normed_ref[...] += times_transposed(grad_pre, input_ref[...])


def feed_backward(rows, positions, grad_branch, normed, hidden, slope, input_low, output_low):
    row_count, width = grad_branch.shape
    hidden_width = hidden.shape[1]
    count = positions.shape[0]
    tile = hidden_width // count
    whole = pl.BlockSpec((row_count, width), lambda j, p: (0, 0))
    tall = pl.BlockSpec((row_count, tile), lambda j, p: (0, j))
    in_half = pl.BlockSpec((width // 2, tile), lambda j, p: (0, j))
    folds = hidden_width // width if rows else 1
    weight_specs = feed_weight_specs(folds if rows else 0, width, tile, lambda j, p: j)
    return pl.pallas_call(
        functools.partial(feed_backward_kernel, rows, count // 2),
        grid_spec=pltpu.PrefetchScalarGridSpec(
            num_scalar_prefetch=1,
            grid=(count,),
            in_specs=[whole, whole, tall, tall, *weight_specs],
            out_specs=[
                in_half,
                in_half,
                pl.BlockSpec((tile // folds, folds * width), lambda j, p: (p[j], 0)),
                whole,
            ],
            scratch_shapes=[
                pltpu.VMEM((width, row_count), jnp.bfloat16),
                pltpu.VMEM((tile, width), jnp.bfloat16),
            ],
        ),
        out_shape=[
            jax.ShapeDtypeStruct((width // 2, hidden_width), jnp.bfloat16),
            jax.ShapeDtypeStruct((width // 2, hidden_width), jnp.bfloat16),
            jax.ShapeDtypeStruct((hidden_width // folds, folds * width), jnp.bfloat16),
            jax.ShapeDtypeStruct((row_count, width), jnp.float32),
        ],
        compiler_params=pltpu.CompilerParams(vmem_limit_bytes=VMEM_BYTES),
        cost_estimate=SHORT,
        name="feed_backward",
    )(positions, grad_branch, normed, hidden, slope, input_low, output_low)


def weight_gradient_kernel(starts, positions_ref, x_ref, *refs):
    turned = refs[-1]
    send_ref, keep_ref = refs[-3:-1]
    step = pl.program_id(0)

    @pl.when(step == 0)
    def _():
        turn_rows(x_ref, turned, positions_ref)

    half = turned.shape[0] // 2
    for index, grad_ref in enumerate(refs[:-3]):

        @pl.when((step >= starts[index]) & (step < starts[index + 1]))
        def _(grad_ref=grad_ref):
            send_ref[...] = product(turned[:half, :], grad_ref[...]).astype(jnp.bfloat16)
            keep_ref[...] = product(turned[half:, :], grad_ref[...]).astype(jnp.bfloat16)


def weight_gradient(positions, x, grads):
    row_count, width = x.shape
    tile = 512
    starts = [0]
    for grad in grads:
        starts.append(starts[-1] + grad.shape[1] // tile)
    columns = starts[-1] * tile

    def grad_spec(first, last):
        return pl.BlockSpec((row_count, tile), lambda j, p: (0, jnp.clip(j - first, 0, last - first - 1)))

    half = pl.BlockSpec((width // 2, tile), lambda j, p: (0, j))
    return pl.pallas_call(
        functools.partial(weight_gradient_kernel, starts),
        grid_spec=pltpu.PrefetchScalarGridSpec(
            num_scalar_prefetch=1,
            grid=(starts[-1],),
            in_specs=[pl.BlockSpec((row_count, width), lambda j, p: (0, 0))]
            + [grad_spec(starts[i], starts[i + 1]) for i in range(len(grads))],
            out_specs=[half, half],
            scratch_shapes=[pltpu.VMEM((width, row_count), jnp.bfloat16)],
        ),
        out_shape=[jax.ShapeDtypeStruct((width // 2, columns), jnp.bfloat16)] * 2,
        compiler_params=pltpu.CompilerParams(vmem_limit_bytes=VMEM_BYTES),
        cost_estimate=SHORT,
        name="weight_gradient",
    )(positions, x, *grads)


class Order:
    def __init__(self):
        self.last = ()

    def after(self, *values):
        values, _ = lax.optimization_barrier((values, self.last))
        return values if len(values) > 1 else values[0]

    def run(self, work, *values):
        values, _ = lax.optimization_barrier((values, self.last))
        result = work(*values)
        self.last = result
        return result


def place_rows_kernel(counts, rows, table_ref, *refs):
    pieces, out_ref, held, sems_in, sems_out = refs[:-4], *refs[-4:]
    loads, stores = [], []
    for piece, count in zip(pieces, counts):
        for block in range(count):
            at = len(loads)
            start = pl.multiple_of(table_ref[at] * rows, rows)
            loads.append(
                pltpu.make_async_copy(piece.at[pl.ds(block * rows, rows), :], held.at[at], sems_in.at[at])
            )
            stores.append(
                pltpu.make_async_copy(held.at[at], out_ref.at[pl.ds(start, rows), :], sems_out.at[at])
            )
    for load in loads:
        load.start()
    for load, store in zip(loads, stores):
        load.wait()
        store.start()
    for store in stores:
        store.wait()


def place_rows(table, pieces, rows):
    counts = [piece.shape[0] // rows for piece in pieces]
    total, columns = sum(counts), pieces[0].shape[1]
    anywhere = pl.BlockSpec(memory_space=pl.ANY)
    return pl.pallas_call(
        functools.partial(place_rows_kernel, counts, rows),
        grid_spec=pltpu.PrefetchScalarGridSpec(
            num_scalar_prefetch=1,
            grid=(1,),
            in_specs=[anywhere] * len(pieces),
            out_specs=anywhere,
            scratch_shapes=[
                pltpu.VMEM((total, rows, columns), pieces[0].dtype),
                pltpu.SemaphoreType.DMA((total,)),
                pltpu.SemaphoreType.DMA((total,)),
            ],
        ),
        out_shape=jax.ShapeDtypeStruct((total * rows, columns), pieces[0].dtype),
        compiler_params=pltpu.CompilerParams(vmem_limit_bytes=VMEM_BYTES),
        cost_estimate=SHORT,
        name="place_rows",
    )(table, *pieces)


class Links:
    def __init__(self, width):
        self.h_count, self.fsdp_count = lax.axis_size("h"), lax.axis_size("fsdp")
        self.core, self.h, self.fsdp = lax.axis_index("c"), lax.axis_index("h"), lax.axis_index("fsdp")
        dp_count = 2 * self.h_count
        self.pairwise = (
            (self.h_count & (self.h_count - 1)) == 0
            and (self.fsdp_count & (self.fsdp_count - 1)) == 0
            and width == dp_count * LANES
        )
        self.blocks = width // LANES
        self.bits = [1 << b for b in range(self.h_count.bit_length() - 1)]
        self.fsdp_table = (self.fsdp ^ jnp.arange(self.fsdp_count, dtype=jnp.int32)).astype(jnp.int32)

    def order(self, flip):
        return self.bits[::-1] if flip else self.bits

    def swap(self, array, bit):
        return lax.ppermute(array, "h", [(i, i ^ bit) for i in range(self.h_count)])

    def swap_core(self, array):
        return lax.ppermute(array, "c", [(0, 1), (1, 0)])

    def swap_fsdp(self, array, bit):
        return lax.ppermute(array, "fsdp", [(i, i ^ bit) for i in range(self.fsdp_count)])

    def gather(self, shard):
        return lax.all_gather(shard, BOTH, axis=0, tiled=True)

    def spread_fsdp(self, shard):
        return [shard] + [self.swap_fsdp(shard, k) for k in range(1, self.fsdp_count)]

    def place_fsdp(self, parts):
        return place_rows(self.fsdp_table, parts, parts[0].shape[0])

    def spread(self, block, at, flip):
        return jnp.concatenate([block, self.swap(block, self.order(flip)[at])], axis=0)

    def place(self, block, other, flip):
        masks = [0]
        for bit in self.order(flip):
            masks = masks + [mask ^ bit for mask in masks]
        h = self.h ^ jnp.asarray(masks, dtype=jnp.int32)
        table = jnp.concatenate([2 * h + self.core, 2 * h + 1 - self.core]).astype(jnp.int32)
        return place_rows(table, [block, other], block.shape[0] // self.h_count)

    def positions(self, flip=None):
        block = jnp.arange(self.blocks, dtype=jnp.int32)
        if not self.pairwise:
            return block
        place, own = block >> 1, (block & 1) == self.core
        if flip is not None:
            mask, place = place ^ self.h, jnp.zeros_like(place)
            for at, bit in enumerate(self.order(flip)):
                place = place + jnp.where((mask & bit) == 0, 1 << at, 0)
        return (place + jnp.where(own, self.h_count, 0)).astype(jnp.int32)

    def halves(self, rows, flip):
        blocks = rows.reshape(self.blocks, -1, rows.shape[1])
        place = self.positions(flip)
        order = jnp.sum(
            jnp.where(place[:, None] == jnp.arange(self.blocks)[None, :], jnp.arange(self.blocks)[:, None], 0),
            axis=0,
        )
        ordered = [lax.dynamic_index_in_dim(blocks, order[j], 0, keepdims=False) for j in range(self.blocks)]
        half = self.blocks // 2
        return jnp.concatenate(ordered[:half], axis=0), jnp.concatenate(ordered[half:], axis=0)

    def sum_cores(self, keep, other):
        return (keep.astype(jnp.float32) + other.astype(jnp.float32)).astype(jnp.bfloat16)

    def send_fsdp(self, grad):
        return lax.all_to_all(grad, "fsdp", 0, 0, tiled=True)

    def sum_fsdp(self, parts):
        rows = parts.shape[0] // self.fsdp_count
        parts = parts.astype(jnp.float32)
        return sum(parts[k * rows : (k + 1) * rows] for k in range(self.fsdp_count))

    def scatter_whole(self, send, keep):
        grad = jnp.concatenate([send, keep], axis=0).astype(jnp.float32)
        part = lax.psum_scatter(grad, ("h", "c"), scatter_dimension=0, tiled=True)
        return lax.psum_scatter(part, "fsdp", scatter_dimension=0, tiled=True)

    def sum_chips(self, grad):
        return lax.psum_scatter(grad, "h", scatter_dimension=0, tiled=True)

    def first_pair(self, keep, other):
        half = keep.shape[0] // 2
        return self.sum_cores(keep[:half], other[:half]), self.sum_cores(keep[half:], other[half:])

    def bit(self, at, flip):
        return self.order(flip)[::-1][at]


def body(
    unit_states,
    encoder_states,
    cotangent,
    unit_lengths,
    text_lengths,
    self_project,
    self_output,
    cross_project,
    cross_output,
    feed_input,
    feed_output,
    norm_gains,
    norm_biases,
):
    low = jnp.bfloat16
    layer_input = unit_states[0].astype(jnp.float32)
    encoded = encoder_states[0]
    row_count, width = layer_input.shape
    links = Links(width)

    tables = jnp.concatenate([norm_gains, norm_biases], axis=0).T
    tables = jnp.pad(tables, ((0, 0), (0, LANES - tables.shape[1])))
    self_shard = jnp.concatenate([self_project.astype(low), self_output.astype(low), tables], axis=1)
    cross_shard = jnp.concatenate(
        [cross_project[:, width:].astype(low), cross_project[:, :width].astype(low), cross_output.astype(low)],
        axis=1,
    )
    feed_shard = feed_input.astype(low)
    order = Order()
    flips = [False, True]
    split = 2 * width
    if links.pairwise:
        fold_count = feed_input.shape[0]
        folded = [
            feed_output[at : at + fold_count].astype(low) for at in range(0, feed_output.shape[0], fold_count)
        ]
        feed_shard = jnp.concatenate([feed_shard] + folded, axis=1)
        bits = [links.order(flip) for flip in flips]

        def send(sides, at):
            return [links.swap(side, bit[at]) for side, bit in zip(sides, bits)]

        def join(*arrays):
            half = len(arrays) // 2
            return [jnp.concatenate(pair, axis=0) for pair in zip(arrays[:half], arrays[half:])]

        def lay(*arrays):
            half = len(arrays) // 2
            return [links.place(*pair, flip) for pair, flip in zip(zip(arrays[:half], arrays[half:]), flips)]

        def lay_fsdp(*parts):
            return links.place_fsdp(parts)

        gathered = links.gather(jnp.concatenate([feed_shard, cross_shard], axis=1))
        feed_input_low, feed_output_low, cross_whole = gathered, gathered, gathered[:, 8 * width :]
        self_part = order.run(lay_fsdp, *links.spread_fsdp(self_shard))
        self_sides = [self_part[:, :split], self_part[:, split:]]
        self_swaps = send(self_sides, 0)
        self_sides = order.run(join, *self_sides, *self_swaps)
        self_swaps = send(self_sides, 1)
        self_sides = order.run(join, *self_sides, *self_swaps)
        self_others = [links.swap_core(side) for side in self_sides]
        self_first, self_second = order.run(lay, *self_sides, *self_others)
    else:
        fold_count = 0
        self_whole, cross_whole = links.gather(self_shard), links.gather(cross_shard)
        self_first, self_second = self_whole[:, :split], self_whole[:, split:]
        feed_input_low = links.gather(feed_shard)
        feed_output_low = links.gather(feed_output.astype(low))

    self_value, self_output_low = self_second[:, :width], self_second[:, width : 2 * width]
    norm_rows = self_second[:, 2 * width : 2 * width + 8].astype(jnp.float32).T
    gain_table, bias_table = norm_rows[:4], norm_rows[4:]

    def self_projections(layer_input, self_first, self_value, gain_row, bias_row):
        normed_self = layer_norm(layer_input, gain_row, bias_row).astype(low)
        return (
            normed_self,
            product(normed_self, self_first).astype(low),
            product(normed_self, self_value).astype(low),
        )

    normed_self, query_key, self_values = order.run(
        self_projections, layer_input, self_first, self_value, gain_table[0], bias_table[0]
    )
    self_mixed, self_totals = order.run(
        lambda query_key, self_values: attention_forward(
            unit_lengths, query_key, 0, query_key, width // LANES, self_values, 0, True
        ),
        query_key,
        self_values,
    )
    after_self, normed_cross = order.run(
        lambda self_mixed, self_output_low, gain_row, bias_row: (
            lambda after_self: (after_self, layer_norm(after_self, gain_row, bias_row).astype(low))
        )(layer_input + product(self_mixed, self_output_low)),
        self_mixed,
        self_output_low,
        gain_table[1],
        bias_table[1],
    )
    cross_first, cross_second = cross_whole[:, :split], cross_whole[:, split:]
    cross_query, cross_output_low = cross_second[:, :width], cross_second[:, width:]
    cross_queries = product(normed_cross, cross_query).astype(low)
    cross_kv = product(encoded, cross_first).astype(low)
    cross_mixed, cross_totals = attention_forward(
        text_lengths, cross_queries, 0, cross_kv, 0, cross_kv, width // LANES, False
    )
    after_cross = after_self + product(cross_mixed, cross_output_low)
    normed_feed = layer_norm(after_cross, gain_table[2], bias_table[2]).astype(low)
    hidden, slope, after_feed = feed_forward(
        fold_count, normed_feed, feed_input_low, feed_output_low, after_cross
    )
    block_output = layer_norm(after_feed, gain_table[3], bias_table[3]).astype(low)

    row_live = (jnp.arange(row_count, dtype=jnp.int32) < unit_lengths[0]).astype(jnp.float32)
    grad_y = cotangent[0] * row_live[:, None]
    grad_after_feed, grad_gain_3, grad_bias_3 = norm_backward(after_feed, gain_table[3], grad_y)
    positions = links.positions()
    in_send, in_keep, out_grad, grad_normed = order.run(
        lambda *arrays: feed_backward(fold_count, positions, *arrays),
        grad_after_feed.astype(low),
        normed_feed,
        hidden,
        slope,
        feed_input_low,
        feed_output_low,
    )
    if links.pairwise:
        out_half = out_grad.shape[0] // 2
        in_other, out_other = links.swap_core(in_send), links.swap_core(out_grad[:out_half])

    def cross_entry(grad_after_feed, after_cross, grad_normed, gain_row, cross_output_low, cross_mixed):
        grad_input, grad_gain, grad_bias = norm_backward(after_cross, gain_row, grad_normed)
        grad_after_cross = grad_after_feed + grad_input
        cross_branch = grad_after_cross.astype(low)
        return (
            grad_after_cross,
            grad_gain,
            grad_bias,
            times_transposed(cross_branch, cross_output_low).astype(low),
            weight_gradient(links.positions(True), cross_mixed, [cross_branch]),
        )

    grad_after_cross, grad_gain_2, grad_bias_2, grad_cross_mixed, cross_out = order.run(
        cross_entry, grad_after_feed, after_cross, grad_normed, gain_table[2], cross_output_low, cross_mixed
    )
    if links.pairwise:
        feed_sum = order.run(
            lambda *arrays: links.sum_cores(
                jnp.concatenate(arrays[:2], axis=1), jnp.concatenate(arrays[2:], axis=1)
            ),
            in_keep,
            out_grad[out_half:],
            in_other,
            out_other,
        )
        feed_chips = links.sum_chips(feed_sum)
    else:
        feed_in_part = links.scatter_whole(in_send, in_keep)
        feed_out_part = links.scatter_whole(out_grad[: out_grad.shape[0] // 2], out_grad[out_grad.shape[0] // 2 :])

    def cross_middle(cross_queries, cross_kv, cross_mixed, grad_cross_mixed, cross_totals):
        grad_q, grad_k, grad_v = attention_backward(
            text_lengths,
            cross_queries,
            0,
            cross_kv,
            0,
            cross_kv,
            width // LANES,
            cross_mixed,
            grad_cross_mixed,
            cross_totals,
            False,
        )
        return (
            grad_q,
            grad_k,
            grad_v,
            weight_gradient(links.positions(True), normed_cross, [grad_q]),
            weight_gradient(links.positions(False), encoded, [grad_k, grad_v]),
        )

    grad_q, grad_k, grad_v, cross_query_grad, cross_kv_grad = order.run(
        cross_middle, cross_queries, cross_kv, cross_mixed, grad_cross_mixed, cross_totals
    )
    cross_send, cross_keep = [
        [kv, jnp.concatenate([query, out], axis=1)]
        for kv, query, out in zip(cross_kv_grad, cross_query_grad, cross_out)
    ]
    if links.pairwise:
        cross_sides = list(zip(cross_keep, [links.swap_core(side) for side in cross_send]))

        def exchange(sides, at):
            halves = order.run(
                lambda *arrays: [links.first_pair(*arrays[i : i + 2]) for i in range(0, len(arrays), 2)],
                *[array for side in sides for array in side],
            )
            return [
                (stays, links.swap(goes, links.bit(at, flip))) for (goes, stays), flip in zip(halves, flips)
            ]

        def finish(sides):
            arrays = [array for side in sides for array in side]
            return links.send_fsdp(
                order.run(
                    lambda *arrays: jnp.concatenate(
                        [links.sum_cores(*arrays[i : i + 2]) for i in range(0, len(arrays), 2)], axis=1
                    ),
                    *arrays,
                )
            )

    def cross_exit(grad_q, grad_k, grad_v, cross_query, cross_first, after_self, gain_row, grad_after_cross):
        grad_kv = jnp.concatenate([grad_k, grad_v], axis=1)
        grad_normed = times_transposed(grad_q, cross_query)
        grad_encoded = times_transposed(grad_kv, cross_first)
        grad_input, grad_gain, grad_bias = norm_backward(after_self, gain_row, grad_normed)
        grad_after_self = grad_after_cross + grad_input
        return grad_after_self, grad_encoded, grad_gain, grad_bias

    grad_after_self, grad_encoded, grad_gain_1, grad_bias_1 = order.run(
        cross_exit, grad_q, grad_k, grad_v, cross_query, cross_first, after_self, gain_table[1], grad_after_cross
    )
    if links.pairwise:
        cross_sides = exchange(cross_sides, 0)
    else:
        cross_part = links.scatter_whole(*[jnp.concatenate(side, axis=1) for side in (cross_send, cross_keep)])

    def self_entry(grad_after_self, self_output_low, self_mixed):
        self_branch = grad_after_self.astype(low)
        return (
            times_transposed(self_branch, self_output_low).astype(low),
            weight_gradient(links.positions(True), self_mixed, [self_branch]),
        )

    grad_self_mixed, self_out = order.run(self_entry, grad_after_self, self_output_low, self_mixed)
    grad_q, grad_k, grad_v = order.run(
        lambda query_key, self_values, self_mixed, grad_self_mixed, self_totals: attention_backward(
            unit_lengths,
            query_key,
            0,
            query_key,
            width // LANES,
            self_values,
            0,
            self_mixed,
            grad_self_mixed,
            self_totals,
            True,
        ),
        query_key,
        self_values,
        self_mixed,
        grad_self_mixed,
        self_totals,
    )
    if links.pairwise:
        cross_sides = exchange(cross_sides, 1)
        feed_chips = order.after(feed_chips)
        feed_part = lax.psum_scatter(feed_chips, "fsdp", scatter_dimension=0, tiled=True)
    first_send, first_keep = order.run(
        lambda *grads: weight_gradient(links.positions(False), normed_self, list(grads)), grad_q, grad_k
    )
    if links.pairwise:
        first_other = links.swap_core(first_send)
    second_send, second_keep = order.run(
        lambda grad, *out: [
            jnp.concatenate(pair, axis=1)
            for pair in zip(weight_gradient(links.positions(True), normed_self, [grad]), out)
        ],
        grad_v,
        *self_out,
    )
    if links.pairwise:
        self_sides = [(first_keep, first_other), (second_keep, links.swap_core(second_send))]
        cross_parts = finish(cross_sides)
        self_sides = exchange(self_sides, 0)

    def self_exit(grad_q, grad_k, grad_v, self_first, self_value, gain_row, grad_after_self, *others):
        grad_qk = jnp.concatenate([grad_q, grad_k], axis=1)
        grad_normed = times_transposed(grad_qk, self_first) + times_transposed(grad_v, self_value)
        grad_input, grad_gain, grad_bias = norm_backward(layer_input, gain_row, grad_normed)
        grad_tables = jnp.stack([grad_gain, *others[:3], grad_bias, *others[3:]])
        return grad_after_self + grad_input, jnp.pad(grad_tables.T, ((0, 0), (0, LANES - 8))).astype(low)

    grad_states, grad_tables = order.run(
        self_exit,
        grad_q,
        grad_k,
        grad_v,
        self_first,
        self_value,
        gain_table[0],
        grad_after_self,
        grad_gain_1,
        grad_gain_2,
        grad_gain_3,
        grad_bias_1,
        grad_bias_2,
        grad_bias_3,
    )
    table_send, table_keep = links.halves(grad_tables, False)
    if links.pairwise:
        cross_part = order.run(links.sum_fsdp, cross_parts)
        table_goes, table_stays = links.first_pair(table_keep, links.swap_core(table_send))
        table_side = (table_stays, links.swap(table_goes, links.bit(0, False)))
        self_sides = exchange(self_sides, 1)
        feed_part = order.run(lambda part: part.astype(jnp.float32), feed_part)
        table_goes, table_stays = links.first_pair(*table_side)
        table_side = (table_stays, links.swap(table_goes, links.bit(1, False)))
        self_part = links.sum_fsdp(finish(self_sides + [table_side]))
        feed_in_part, feed_out_part = feed_part[:, : 4 * width], feed_part[:, 4 * width :]
        feed_out_part = jnp.concatenate(
            [feed_out_part[:, at * width : (at + 1) * width] for at in range(4)], axis=0
        )
    else:
        self_part = jnp.concatenate(
            [
                links.scatter_whole(*pair)
                for pair in ((first_send, first_keep), (second_send, second_keep), (table_send, table_keep))
            ],
            axis=1,
        )
    self_in_part, self_out_part = self_part[:, : 3 * width], self_part[:, 3 * width : 4 * width]
    table_part = self_part[:, 4 * width :]
    cross_in_part = jnp.concatenate([cross_part[:, split : 3 * width], cross_part[:, :split]], axis=1)
    cross_out_part = cross_part[:, 3 * width :]

    return (
        block_output[None],
        grad_states[None],
        grad_encoded[None],
        self_in_part,
        self_out_part,
        cross_in_part,
        cross_out_part,
        feed_in_part,
        feed_out_part,
        table_part[:, :4].T,
        table_part[:, 4:8].T,
    )


def solution(mesh):
    dp_count, fsdp_count = mesh.shape["dp"], mesh.shape["fsdp"]
    split = Mesh(mesh.devices.reshape(dp_count // 2, 2, fsdp_count), BOTH)
    return jax.shard_map(
        body,
        mesh=split,
        in_specs=(
            P(BOTH, None, None),
            P(BOTH, None, None),
            P(BOTH, None, None),
            P(BOTH),
            P(BOTH),
            P(BOTH, None),
            P(BOTH, None),
            P(BOTH, None),
            P(BOTH, None),
            P(BOTH, None),
            P(BOTH, None),
            P(None, BOTH),
            P(None, BOTH),
        ),
        out_specs=(
            P(BOTH, None, None),
            P(BOTH, None, None),
            P(BOTH, None, None),
            P(BOTH, None),
            P(BOTH, None),
            P(BOTH, None),
            P(BOTH, None),
            P(BOTH, None),
            P(BOTH, None),
            P(None, BOTH),
            P(None, BOTH),
        ),
        check_vma=False,
    )
```

```python
import functools

import jax
import jax.numpy as jnp
from jax import lax
from jax.experimental import pallas as pl
from jax.experimental.pallas import tpu as pltpu
from jax.sharding import Mesh
from jax.sharding import PartitionSpec as P

HEAD = 64
LANES = 128
AHEAD = 1
BOTH = ("h", "c", "fsdp")
VMEM_BYTES = 60 * 1024 * 1024
SHORT = pl.CostEstimate(flops=1024, transcendentals=0, bytes_accessed=1024)


def product(left, right):
    return jnp.dot(left, right, preferred_element_type=jnp.float32)


def contract_rows(left, right):
    return lax.dot_general(
        left, right, (((0,), (0,)), ((), ())), preferred_element_type=jnp.float32
    )


def times_transposed(left, right):
    return lax.dot_general(
        left, right, (((1,), (1,)), ((), ())), preferred_element_type=jnp.float32
    )


def layer_norm(values, gain_row, bias_row):
    centre = values - jnp.mean(values, axis=-1, keepdims=True)
    spread = jnp.mean(centre * centre, axis=-1, keepdims=True)
    return centre * lax.rsqrt(spread + 1e-05) * gain_row + bias_row


def norm_backward(values, gain_row, grad):
    centre = values - jnp.mean(values, axis=-1, keepdims=True)
    rate = lax.rsqrt(jnp.mean(centre * centre, axis=-1, keepdims=True) + 1e-05)
    normed = centre * rate
    scaled = grad * gain_row
    grad_input = rate * (
        scaled
        - jnp.mean(scaled, axis=-1, keepdims=True)
        - normed * jnp.mean(scaled * normed, axis=-1, keepdims=True)
    )
    return grad_input, jnp.sum(grad * normed, axis=0), jnp.sum(grad, axis=0)


def with_bias_lane(matrix, head, bias):
    lane = lax.broadcasted_iota(jnp.int32, matrix.shape, 1)
    own = (lane >= head * HEAD) & (lane < (head + 1) * HEAD)
    rest = jnp.where(lane == (1 - head) * HEAD, bias, 0.0).astype(matrix.dtype)
    return jnp.where(own, matrix, rest)


def key_bias(key_count, key_limit):
    row = lax.broadcasted_iota(jnp.int32, (key_count, LANES), 0)
    return jnp.where(row < key_limit, 0.0, -1e30)


def masked_scores(keys, queries, diagonal_ref):
    scores = times_transposed(keys, queries)
    if diagonal_ref is None:
        return scores
    below = scores.shape[0] - scores.shape[1]
    diagonal = scores[below:, :] + diagonal_ref[...]
    return jnp.concatenate([scores[:below, :], diagonal], axis=0) if below else diagonal


def set_diagonal(diagonal_ref):
    @pl.when(pl.program_id(0) == 0)
    def _():
        row = lax.broadcasted_iota(jnp.int32, diagonal_ref.shape, 0)
        column = lax.broadcasted_iota(jnp.int32, diagonal_ref.shape, 1)
        diagonal_ref[...] = jnp.where(row <= column, 0.0, -1e30)


def query_width(row_count, causal):
    return 256 if causal and row_count % 256 == 0 else row_count


def query_blocks(row_count, key_count, causal):
    width = query_width(row_count, causal)
    return [
        (start, width, start + width if causal else key_count)
        for start in range(0, row_count, width)
    ]


def head_lanes(head, shape):
    lane = lax.broadcasted_iota(jnp.int32, shape, 1)
    return (lane >= head * HEAD) & (lane < (head + 1) * HEAD)


def staggered(items, first, middle, last, ahead):
    begun = [first(item) for item in items[:ahead]]
    waiting = None
    for at, item in enumerate(items):
        if at + ahead < len(items):
            begun.append(first(items[at + ahead]))
        done = middle(item, begun[at])
        begun[at] = None
        if waiting is not None:
            last(*waiting)
        waiting = (item, done)
    last(*waiting)


def attention_forward_kernel(
    causal, limit_ref, q_ref, k_ref, v_ref, mixed_ref, total_ref, mixed_turned, diagonal_ref
):
    row_count, key_count = q_ref.shape[0], k_ref.shape[0]
    bias = key_bias(key_count, limit_ref[0])
    if causal:
        set_diagonal(diagonal_ref)
    else:
        diagonal_ref = None
    values_turned = v_ref[...].T
    ones = jnp.ones((16, key_count), jnp.bfloat16)
    scaled = q_ref[...] * jnp.bfloat16(HEAD**-0.5)
    queries = [with_bias_lane(scaled, head, 1.0) for head in range(2)]
    keys = [with_bias_lane(k_ref[...], head, bias) for head in range(2)]
    lanes = [slice(head * HEAD, (head + 1) * HEAD) for head in range(2)]
    values = [jnp.concatenate([values_turned[at, :], ones], axis=0) for at in lanes]

    def scores_of(item):
        head, (start, width, stop) = item
        return masked_scores(keys[head][:stop, :], queries[head][start : start + width, :], diagonal_ref)

    def expand(item, scores):
        highest = jnp.max(scores, axis=0, keepdims=True)
        return highest, jnp.exp(scores - highest).astype(jnp.bfloat16)

    def mix(item, done):
        head, (start, width, stop) = item
        highest, expanded = done
        mixed = product(values[head][:, :stop], expanded)
        total = mixed[HEAD : HEAD + 1, :]
        mixed_turned[lanes[head], start : start + width] = mixed[:HEAD, :] / total
        total_ref[0, head : head + 1, start : start + width] = highest + jnp.log(total)

    items = [(head, block) for block in query_blocks(row_count, key_count, causal) for head in range(2)]
    staggered(items, scores_of, expand, mix, 2)
    mixed_ref[...] = mixed_turned[...].T.astype(jnp.bfloat16)


def attention_forward(limit, queries, q_at, keys, k_at, values, v_at, causal):
    row_count, key_count = queries.shape[0], keys.shape[0]
    width = 1024
    pairs = width // LANES
    return pl.pallas_call(
        functools.partial(attention_forward_kernel, causal),
        grid_spec=pltpu.PrefetchScalarGridSpec(
            num_scalar_prefetch=1,
            grid=(pairs,),
            in_specs=[
                pl.BlockSpec((row_count, LANES), lambda p, s: (0, q_at + p)),
                pl.BlockSpec((key_count, LANES), lambda p, s: (0, k_at + p)),
                pl.BlockSpec((key_count, LANES), lambda p, s: (0, v_at + p)),
            ],
            out_specs=[
                pl.BlockSpec((row_count, LANES), lambda p, s: (0, p)),
                pl.BlockSpec((1, 2, row_count), lambda p, s: (p, 0, 0)),
            ],
            scratch_shapes=[
                pltpu.VMEM((LANES, row_count), jnp.float32),
                pltpu.VMEM((query_width(row_count, causal),) * 2, jnp.float32),
            ],
        ),
        out_shape=[
            jax.ShapeDtypeStruct((row_count, width), jnp.bfloat16),
            jax.ShapeDtypeStruct((pairs, 2, row_count), jnp.float32),
        ],
        compiler_params=pltpu.CompilerParams(vmem_limit_bytes=VMEM_BYTES),
        cost_estimate=SHORT,
        name="attention_forward",
    )(limit, queries, keys, values)


def attention_backward_kernel(
    causal,
    limit_ref,
    q_ref,
    k_ref,
    v_ref,
    mixed_ref,
    grad_ref,
    total_ref,
    grad_q_ref,
    grad_k_ref,
    grad_v_ref,
    grad_q_turned,
    grad_k_sum,
    grad_v_sum,
    diagonal_ref,
):
    row_count, key_count = q_ref.shape[0], k_ref.shape[0]
    bias = key_bias(key_count, limit_ref[0])
    if causal:
        set_diagonal(diagonal_ref)
    else:
        diagonal_ref = None
    keys_turned = k_ref[...].T
    scaled = q_ref[...] * jnp.bfloat16(HEAD**-0.5)
    grad = grad_ref[...]
    inner_turned = (grad.astype(jnp.float32) * mixed_ref[...].astype(jnp.float32)).T
    grad_k_sum[...] = jnp.zeros_like(grad_k_sum)
    grad_v_sum[...] = jnp.zeros_like(grad_v_sum)
    masks = [head_lanes(head, scaled.shape) for head in range(2)]
    queries = [jnp.where(mask, scaled, jnp.zeros_like(scaled)) for mask in masks]
    grads = [jnp.where(mask, grad, jnp.zeros_like(grad)) for mask in masks]
    biased = [with_bias_lane(scaled, head, 1.0) for head in range(2)]
    keys = [with_bias_lane(k_ref[...], head, bias) for head in range(2)]
    lanes = [slice(head * HEAD, (head + 1) * HEAD) for head in range(2)]
    inner = [jnp.sum(inner_turned[at, :], axis=0, keepdims=True) for at in lanes]

    def scores_of(item):
        head, (start, width, stop) = item
        columns = slice(start, start + width)
        scores = masked_scores(keys[head][:stop, :], biased[head][columns, :], diagonal_ref)
        return scores, times_transposed(v_ref[:stop, :], grads[head][columns, :])

    def differentiate(item, begun):
        head, (start, width, stop) = item
        columns = slice(start, start + width)
        scores, grad_probs = begun
        probs = jnp.exp(scores - total_ref[0, head : head + 1, columns])
        grad_scores = probs * (grad_probs - inner[head][:, columns])
        return probs.astype(jnp.bfloat16), grad_scores.astype(jnp.bfloat16)

    def add(item, done):
        head, (start, width, stop) = item
        columns = slice(start, start + width)
        probs, grad_scores = done
        grad_v_sum[:stop, :] += product(probs, grads[head][columns, :])
        grad_k_sum[:stop, :] += product(grad_scores, queries[head][columns, :])
        grad_q_turned[lanes[head], columns] = product(keys_turned[lanes[head], :stop], grad_scores)

    items = [(head, block) for block in query_blocks(row_count, key_count, causal) for head in range(2)]
    staggered(items, scores_of, differentiate, add, AHEAD)
    grad_q_ref[...] = (grad_q_turned[...].T * HEAD**-0.5).astype(jnp.bfloat16)
    grad_k_ref[...] = grad_k_sum[...].astype(jnp.bfloat16)
    grad_v_ref[...] = grad_v_sum[...].astype(jnp.bfloat16)


def attention_backward(limit, queries, q_at, keys, k_at, values, v_at, mixed, grad_mixed, totals, causal):
    row_count, key_count = queries.shape[0], keys.shape[0]
    width = 1024
    pairs = width // LANES
    row_block = pl.BlockSpec((row_count, LANES), lambda p, s: (0, p))
    key_block = pl.BlockSpec((key_count, LANES), lambda p, s: (0, p))
    return pl.pallas_call(
        functools.partial(attention_backward_kernel, causal),
        grid_spec=pltpu.PrefetchScalarGridSpec(
            num_scalar_prefetch=1,
            grid=(pairs,),
            in_specs=[
                pl.BlockSpec((row_count, LANES), lambda p, s: (0, q_at + p)),
                pl.BlockSpec((key_count, LANES), lambda p, s: (0, k_at + p)),
                pl.BlockSpec((key_count, LANES), lambda p, s: (0, v_at + p)),
                row_block,
                row_block,
                pl.BlockSpec((1, 2, row_count), lambda p, s: (p, 0, 0)),
            ],
            out_specs=[row_block, key_block, key_block],
            scratch_shapes=[
                pltpu.VMEM((LANES, row_count), jnp.float32),
                pltpu.VMEM((key_count, LANES), jnp.float32),
                pltpu.VMEM((key_count, LANES), jnp.float32),
                pltpu.VMEM((query_width(row_count, causal),) * 2, jnp.float32),
            ],
        ),
        out_shape=[
            jax.ShapeDtypeStruct((row_count, width), jnp.bfloat16),
            jax.ShapeDtypeStruct((key_count, width), jnp.bfloat16),
            jax.ShapeDtypeStruct((key_count, width), jnp.bfloat16),
        ],
        compiler_params=pltpu.CompilerParams(vmem_limit_bytes=VMEM_BYTES),
        cost_estimate=SHORT,
        name="attention_backward",
    )(limit, queries, keys, values, mixed, grad_mixed, totals)


def gelu_and_slope(values):
    normal_cdf = 0.5 + 0.5 * lax.erf(values * 2.0 ** (-0.5))
    bell = jnp.exp(-0.5 * values * values) * (2.0 * jnp.pi) ** (-0.5)
    return values * normal_cdf, normal_cdf + values * bell


def unfold_rows(folded_ref, unfolded, rows):
    width = unfolded.shape[1]
    folds = folded_ref.shape[1] // width
    for shard in range(folded_ref.shape[0] // rows):
        for fold in range(folds):
            start = (shard * folds + fold) * rows
            unfolded[start : start + rows, :] = folded_ref[
                shard * rows : (shard + 1) * rows, fold * width : (fold + 1) * width
            ]


def fold_rows(unfolded, folded_ref, rows):
    width = unfolded.shape[1]
    folds = folded_ref.shape[1] // width
    for shard in range(folded_ref.shape[0] // rows):
        for fold in range(folds):
            start = (shard * folds + fold) * rows
            folded_ref[shard * rows : (shard + 1) * rows, fold * width : (fold + 1) * width] = unfolded[
                start : start + rows, :
            ]


def feed_forward_kernel(
    rows, normed_ref, input_ref, output_ref, base_ref, hidden_ref, slope_ref, after_ref, unfolded
):
    if rows:
        unfold_rows(output_ref, unfolded, rows)
        output_ref = unfolded

    @pl.when(pl.program_id(0) == 0)
    def _():
        after_ref[...] = base_ref[...]

    row_count = normed_ref.shape[0]
    step = 256 if row_count % 256 == 0 else row_count
    blocks = [slice(start, start + step) for start in range(0, row_count, step)]
    hidden_pre = product(normed_ref[blocks[0], :], input_ref[...])
    ready = None
    for at, rows_at in enumerate(blocks):
        following = product(normed_ref[blocks[at + 1], :], input_ref[...]) if at + 1 < len(blocks) else None
        hidden, slope = gelu_and_slope(hidden_pre)
        hidden = hidden.astype(jnp.bfloat16)
        hidden_ref[rows_at, :] = hidden
        slope_ref[rows_at, :] = slope.astype(jnp.bfloat16)
        if ready is not None:
            after_ref[blocks[at - 1], :] += product(ready, output_ref[...])
        hidden_pre, ready = following, hidden
    after_ref[blocks[-1], :] += product(ready, output_ref[...])


FEED_TILE = 512


def feed_weight_specs(folds, width, tile, index):
    first = pl.BlockSpec((width, tile), lambda *at: (0, index(*at)))
    if folds:
        return first, pl.BlockSpec((tile // folds, folds * width), lambda *at: (index(*at), 1))
    return first, pl.BlockSpec((tile, width), lambda *at: (index(*at), 0))


def feed_forward(rows, normed, input_low, output_low, after_cross):
    row_count, width = normed.shape
    hidden_width = 4 * width
    tile = FEED_TILE
    whole = pl.BlockSpec((row_count, width), lambda j: (0, 0))
    tall = pl.BlockSpec((row_count, tile), lambda j: (0, j))
    weight_specs = feed_weight_specs(hidden_width // width if rows else 0, width, tile, lambda j: j)
    return pl.pallas_call(
        functools.partial(feed_forward_kernel, rows),
        grid=(hidden_width // tile,),
        in_specs=[whole, *weight_specs, whole],
        out_specs=[tall, tall, whole],
        out_shape=[
            jax.ShapeDtypeStruct((row_count, hidden_width), jnp.bfloat16),
            jax.ShapeDtypeStruct((row_count, hidden_width), jnp.bfloat16),
            jax.ShapeDtypeStruct((row_count, width), jnp.float32),
        ],
        scratch_shapes=[pltpu.VMEM((tile, width), jnp.bfloat16)],
        compiler_params=pltpu.CompilerParams(vmem_limit_bytes=VMEM_BYTES),
        cost_estimate=SHORT,
        name="feed_forward",
    )(normed, input_low, output_low, after_cross)


def turn_rows(x_ref, turned, positions_ref):
    for j in range(x_ref.shape[1] // LANES):
        start = pl.multiple_of(positions_ref[j] * LANES, LANES)
        turned[pl.ds(start, LANES), :] = x_ref[:, j * LANES : (j + 1) * LANES].T


def feed_backward_kernel(
    rows,
    half_blocks,
    positions_ref,
    grad_ref,
    normed_ref,
    hidden_ref,
    slope_ref,
    input_ref,
    output_ref,
    in_send_ref,
    in_keep_ref,
    out_ref,
    grad_normed_ref,
    turned,
    unfolded,
):
    step = pl.program_id(0)
    if rows:
        unfold_rows(output_ref, unfolded, rows)
        output_ref = unfolded

    @pl.when(step == 0)
    def _():
        grad_normed_ref[...] = jnp.zeros_like(grad_normed_ref)
        turn_rows(normed_ref, turned, positions_ref)

    grad_hidden = times_transposed(grad_ref[...], output_ref[...])
    grad_pre = (grad_hidden * slope_ref[...].astype(jnp.float32)).astype(jnp.bfloat16)
    grad_out = contract_rows(hidden_ref[...], grad_ref[...]).astype(jnp.bfloat16)
    if rows:
        fold_rows(grad_out, out_ref, rows)
    else:
        out_ref[...] = grad_out
    half = turned.shape[0] // 2
    in_send_ref[...] = product(turned[:half, :], grad_pre).astype(jnp.bfloat16)
    in_keep_ref[...] = product(turned[half:, :], grad_pre).astype(jnp.bfloat16)
    grad_normed_ref[...] += times_transposed(grad_pre, input_ref[...])


def feed_backward(rows, positions, grad_branch, normed, hidden, slope, input_low, output_low):
    row_count, width = grad_branch.shape
    hidden_width = hidden.shape[1]
    count = positions.shape[0]
    tile = hidden_width // count
    whole = pl.BlockSpec((row_count, width), lambda j, p: (0, 0))
    tall = pl.BlockSpec((row_count, tile), lambda j, p: (0, j))
    in_half = pl.BlockSpec((width // 2, tile), lambda j, p: (0, j))
    folds = hidden_width // width if rows else 1
    weight_specs = feed_weight_specs(folds if rows else 0, width, tile, lambda j, p: j)
    return pl.pallas_call(
        functools.partial(feed_backward_kernel, rows, count // 2),
        grid_spec=pltpu.PrefetchScalarGridSpec(
            num_scalar_prefetch=1,
            grid=(count,),
            in_specs=[whole, whole, tall, tall, *weight_specs],
            out_specs=[
                in_half,
                in_half,
                pl.BlockSpec((tile // folds, folds * width), lambda j, p: (p[j], 0)),
                whole,
            ],
            scratch_shapes=[
                pltpu.VMEM((width, row_count), jnp.bfloat16),
                pltpu.VMEM((tile, width), jnp.bfloat16),
            ],
        ),
        out_shape=[
            jax.ShapeDtypeStruct((width // 2, hidden_width), jnp.bfloat16),
            jax.ShapeDtypeStruct((width // 2, hidden_width), jnp.bfloat16),
            jax.ShapeDtypeStruct((hidden_width // folds, folds * width), jnp.bfloat16),
            jax.ShapeDtypeStruct((row_count, width), jnp.float32),
        ],
        compiler_params=pltpu.CompilerParams(vmem_limit_bytes=VMEM_BYTES),
        cost_estimate=SHORT,
        name="feed_backward",
    )(positions, grad_branch, normed, hidden, slope, input_low, output_low)


def weight_gradient_kernel(starts, positions_ref, x_ref, *refs):
    turned = refs[-1]
    send_ref, keep_ref = refs[-3:-1]
    step = pl.program_id(0)

    @pl.when(step == 0)
    def _():
        turn_rows(x_ref, turned, positions_ref)

    half = turned.shape[0] // 2
    for index, grad_ref in enumerate(refs[:-3]):

        @pl.when((step >= starts[index]) & (step < starts[index + 1]))
        def _(grad_ref=grad_ref):
            send_ref[...] = product(turned[:half, :], grad_ref[...]).astype(jnp.bfloat16)
            keep_ref[...] = product(turned[half:, :], grad_ref[...]).astype(jnp.bfloat16)


def weight_gradient(positions, x, grads):
    row_count, width = x.shape
    tile = 512
    starts = [0]
    for grad in grads:
        starts.append(starts[-1] + grad.shape[1] // tile)
    columns = starts[-1] * tile

    def grad_spec(first, last):
        return pl.BlockSpec((row_count, tile), lambda j, p: (0, jnp.clip(j - first, 0, last - first - 1)))

    half = pl.BlockSpec((width // 2, tile), lambda j, p: (0, j))
    return pl.pallas_call(
        functools.partial(weight_gradient_kernel, starts),
        grid_spec=pltpu.PrefetchScalarGridSpec(
            num_scalar_prefetch=1,
            grid=(starts[-1],),
            in_specs=[pl.BlockSpec((row_count, width), lambda j, p: (0, 0))]
            + [grad_spec(starts[i], starts[i + 1]) for i in range(len(grads))],
            out_specs=[half, half],
            scratch_shapes=[pltpu.VMEM((width, row_count), jnp.bfloat16)],
        ),
        out_shape=[jax.ShapeDtypeStruct((width // 2, columns), jnp.bfloat16)] * 2,
        compiler_params=pltpu.CompilerParams(vmem_limit_bytes=VMEM_BYTES),
        cost_estimate=SHORT,
        name="weight_gradient",
    )(positions, x, *grads)


class Order:
    def __init__(self):
        self.last = ()

    def after(self, *values):
        values, _ = lax.optimization_barrier((values, self.last))
        return values if len(values) > 1 else values[0]

    def run(self, work, *values):
        values, _ = lax.optimization_barrier((values, self.last))
        result = work(*values)
        self.last = result
        return result


def place_rows_kernel(counts, rows, table_ref, *refs):
    pieces, out_ref, held, sems_in, sems_out = refs[:-4], *refs[-4:]
    loads, stores = [], []
    for piece, count in zip(pieces, counts):
        for block in range(count):
            at = len(loads)
            start = pl.multiple_of(table_ref[at] * rows, rows)
            loads.append(
                pltpu.make_async_copy(piece.at[pl.ds(block * rows, rows), :], held.at[at], sems_in.at[at])
            )
            stores.append(
                pltpu.make_async_copy(held.at[at], out_ref.at[pl.ds(start, rows), :], sems_out.at[at])
            )
    for load in loads:
        load.start()
    for load, store in zip(loads, stores):
        load.wait()
        store.start()
    for store in stores:
        store.wait()


def place_rows(table, pieces, rows):
    counts = [piece.shape[0] // rows for piece in pieces]
    total, columns = sum(counts), pieces[0].shape[1]
    anywhere = pl.BlockSpec(memory_space=pl.ANY)
    return pl.pallas_call(
        functools.partial(place_rows_kernel, counts, rows),
        grid_spec=pltpu.PrefetchScalarGridSpec(
            num_scalar_prefetch=1,
            grid=(1,),
            in_specs=[anywhere] * len(pieces),
            out_specs=anywhere,
            scratch_shapes=[
                pltpu.VMEM((total, rows, columns), pieces[0].dtype),
                pltpu.SemaphoreType.DMA((total,)),
                pltpu.SemaphoreType.DMA((total,)),
            ],
        ),
        out_shape=jax.ShapeDtypeStruct((total * rows, columns), pieces[0].dtype),
        compiler_params=pltpu.CompilerParams(vmem_limit_bytes=VMEM_BYTES),
        cost_estimate=SHORT,
        name="place_rows",
    )(table, *pieces)


class Links:
    def __init__(self, width):
        self.h_count, self.fsdp_count = lax.axis_size("h"), lax.axis_size("fsdp")
        self.core, self.h, self.fsdp = lax.axis_index("c"), lax.axis_index("h"), lax.axis_index("fsdp")
        dp_count = 2 * self.h_count
        self.pairwise = (
            (self.h_count & (self.h_count - 1)) == 0
            and (self.fsdp_count & (self.fsdp_count - 1)) == 0
            and width == dp_count * LANES
        )
        self.blocks = width // LANES
        self.bits = [1 << b for b in range(self.h_count.bit_length() - 1)]
        self.fsdp_table = (self.fsdp ^ jnp.arange(self.fsdp_count, dtype=jnp.int32)).astype(jnp.int32)

    def order(self, flip):
        return self.bits[::-1] if flip else self.bits

    def swap(self, array, bit):
        return lax.ppermute(array, "h", [(i, i ^ bit) for i in range(self.h_count)])

    def swap_core(self, array):
        return lax.ppermute(array, "c", [(0, 1), (1, 0)])

    def swap_fsdp(self, array, bit):
        return lax.ppermute(array, "fsdp", [(i, i ^ bit) for i in range(self.fsdp_count)])

    def gather(self, shard):
        return lax.all_gather(shard, BOTH, axis=0, tiled=True)

    def spread_fsdp(self, shard):
        return [shard] + [self.swap_fsdp(shard, k) for k in range(1, self.fsdp_count)]

    def place_fsdp(self, parts):
        return place_rows(self.fsdp_table, parts, parts[0].shape[0])

    def spread(self, block, at, flip):
        return jnp.concatenate([block, self.swap(block, self.order(flip)[at])], axis=0)

    def place(self, block, other, flip):
        masks = [0]
        for bit in self.order(flip):
            masks = masks + [mask ^ bit for mask in masks]
        h = self.h ^ jnp.asarray(masks, dtype=jnp.int32)
        table = jnp.concatenate([2 * h + self.core, 2 * h + 1 - self.core]).astype(jnp.int32)
        return place_rows(table, [block, other], block.shape[0] // self.h_count)

    def positions(self, flip=None):
        block = jnp.arange(self.blocks, dtype=jnp.int32)
        if not self.pairwise:
            return block
        place, own = block >> 1, (block & 1) == self.core
        if flip is not None:
            mask, place = place ^ self.h, jnp.zeros_like(place)
            for at, bit in enumerate(self.order(flip)):
                place = place + jnp.where((mask & bit) == 0, 1 << at, 0)
        return (place + jnp.where(own, self.h_count, 0)).astype(jnp.int32)

    def halves(self, rows, flip):
        blocks = rows.reshape(self.blocks, -1, rows.shape[1])
        place = self.positions(flip)
        order = jnp.sum(
            jnp.where(place[:, None] == jnp.arange(self.blocks)[None, :], jnp.arange(self.blocks)[:, None], 0),
            axis=0,
        )
        ordered = [lax.dynamic_index_in_dim(blocks, order[j], 0, keepdims=False) for j in range(self.blocks)]
        half = self.blocks // 2
        return jnp.concatenate(ordered[:half], axis=0), jnp.concatenate(ordered[half:], axis=0)

    def sum_cores(self, keep, other):
        return (keep.astype(jnp.float32) + other.astype(jnp.float32)).astype(jnp.bfloat16)

    def send_fsdp(self, grad):
        return lax.all_to_all(grad, "fsdp", 0, 0, tiled=True)

    def sum_fsdp(self, parts):
        rows = parts.shape[0] // self.fsdp_count
        parts = parts.astype(jnp.float32)
        return sum(parts[k * rows : (k + 1) * rows] for k in range(self.fsdp_count))

    def scatter_whole(self, send, keep):
        grad = jnp.concatenate([send, keep], axis=0).astype(jnp.float32)
        part = lax.psum_scatter(grad, ("h", "c"), scatter_dimension=0, tiled=True)
        return lax.psum_scatter(part, "fsdp", scatter_dimension=0, tiled=True)

    def sum_chips(self, grad):
        return lax.psum_scatter(grad, "h", scatter_dimension=0, tiled=True)

    def first_pair(self, keep, other):
        half = keep.shape[0] // 2
        return self.sum_cores(keep[:half], other[:half]), self.sum_cores(keep[half:], other[half:])

    def bit(self, at, flip):
        return self.order(flip)[::-1][at]


def body(
    unit_states,
    encoder_states,
    cotangent,
    unit_lengths,
    text_lengths,
    self_project,
    self_output,
    cross_project,
    cross_output,
    feed_input,
    feed_output,
    norm_gains,
    norm_biases,
):
    low = jnp.bfloat16
    layer_input = unit_states[0].astype(jnp.float32)
    encoded = encoder_states[0]
    row_count, width = layer_input.shape
    links = Links(width)

    tables = jnp.concatenate([norm_gains, norm_biases], axis=0).T
    tables = jnp.pad(tables, ((0, 0), (0, LANES - tables.shape[1])))
    self_shard = jnp.concatenate([self_project.astype(low), self_output.astype(low), tables], axis=1)
    cross_shard = jnp.concatenate(
        [cross_project[:, width:].astype(low), cross_project[:, :width].astype(low), cross_output.astype(low)],
        axis=1,
    )
    feed_shard = feed_input.astype(low)
    order = Order()
    flips = [False, True]
    split = 2 * width
    if links.pairwise:
        fold_count = feed_input.shape[0]
        folded = [
            feed_output[at : at + fold_count].astype(low) for at in range(0, feed_output.shape[0], fold_count)
        ]
        feed_shard = jnp.concatenate([feed_shard] + folded, axis=1)
        bits = [links.order(flip) for flip in flips]

        def send(sides, at):
            return [links.swap(side, bit[at]) for side, bit in zip(sides, bits)]

        def join(*arrays):
            half = len(arrays) // 2
            return [jnp.concatenate(pair, axis=0) for pair in zip(arrays[:half], arrays[half:])]

        def lay(*arrays):
            half = len(arrays) // 2
            return [links.place(*pair, flip) for pair, flip in zip(zip(arrays[:half], arrays[half:]), flips)]

        def lay_fsdp(*parts):
            return links.place_fsdp(parts)

        gathered = links.gather(jnp.concatenate([feed_shard, cross_shard], axis=1))
        feed_input_low, feed_output_low, cross_whole = gathered, gathered, gathered[:, 8 * width :]
        self_part = order.run(lay_fsdp, *links.spread_fsdp(self_shard))
        self_sides = [self_part[:, :split], self_part[:, split:]]
        self_swaps = send(self_sides, 0)
        self_sides = order.run(join, *self_sides, *self_swaps)
        self_swaps = send(self_sides, 1)
        self_sides = order.run(join, *self_sides, *self_swaps)
        self_others = [links.swap_core(side) for side in self_sides]
        self_first, self_second = order.run(lay, *self_sides, *self_others)
    else:
        fold_count = 0
        self_whole, cross_whole = links.gather(self_shard), links.gather(cross_shard)
        self_first, self_second = self_whole[:, :split], self_whole[:, split:]
        feed_input_low = links.gather(feed_shard)
        feed_output_low = links.gather(feed_output.astype(low))

    self_value, self_output_low = self_second[:, :width], self_second[:, width : 2 * width]
    norm_rows = self_second[:, 2 * width : 2 * width + 8].astype(jnp.float32).T
    gain_table, bias_table = norm_rows[:4], norm_rows[4:]

    def self_projections(layer_input, self_first, self_value, gain_row, bias_row):
        normed_self = layer_norm(layer_input, gain_row, bias_row).astype(low)
        return (
            normed_self,
            product(normed_self, self_first).astype(low),
            product(normed_self, self_value).astype(low),
        )

    normed_self, query_key, self_values = order.run(
        self_projections, layer_input, self_first, self_value, gain_table[0], bias_table[0]
    )
    self_mixed, self_totals = order.run(
        lambda query_key, self_values: attention_forward(
            unit_lengths, query_key, 0, query_key, width // LANES, self_values, 0, True
        ),
        query_key,
        self_values,
    )
    after_self, normed_cross = order.run(
        lambda self_mixed, self_output_low, gain_row, bias_row: (
            lambda after_self: (after_self, layer_norm(after_self, gain_row, bias_row).astype(low))
        )(layer_input + product(self_mixed, self_output_low)),
        self_mixed,
        self_output_low,
        gain_table[1],
        bias_table[1],
    )
    cross_first, cross_second = cross_whole[:, :split], cross_whole[:, split:]
    cross_query, cross_output_low = cross_second[:, :width], cross_second[:, width:]
    cross_queries = product(normed_cross, cross_query).astype(low)
    cross_kv = product(encoded, cross_first).astype(low)
    cross_mixed, cross_totals = attention_forward(
        text_lengths, cross_queries, 0, cross_kv, 0, cross_kv, width // LANES, False
    )
    after_cross = after_self + product(cross_mixed, cross_output_low)
    normed_feed = layer_norm(after_cross, gain_table[2], bias_table[2]).astype(low)
    hidden, slope, after_feed = feed_forward(
        fold_count, normed_feed, feed_input_low, feed_output_low, after_cross
    )
    block_output = layer_norm(after_feed, gain_table[3], bias_table[3]).astype(low)

    row_live = (jnp.arange(row_count, dtype=jnp.int32) < unit_lengths[0]).astype(jnp.float32)
    grad_y = cotangent[0] * row_live[:, None]
    grad_after_feed, grad_gain_3, grad_bias_3 = norm_backward(after_feed, gain_table[3], grad_y)
    positions = links.positions()
    in_send, in_keep, out_grad, grad_normed = order.run(
        lambda *arrays: feed_backward(fold_count, positions, *arrays),
        grad_after_feed.astype(low),
        normed_feed,
        hidden,
        slope,
        feed_input_low,
        feed_output_low,
    )
    if links.pairwise:
        out_half = out_grad.shape[0] // 2
        in_other, out_other = links.swap_core(in_send), links.swap_core(out_grad[:out_half])

    def cross_entry(grad_after_feed, after_cross, grad_normed, gain_row, cross_output_low, cross_mixed):
        grad_input, grad_gain, grad_bias = norm_backward(after_cross, gain_row, grad_normed)
        grad_after_cross = grad_after_feed + grad_input
        cross_branch = grad_after_cross.astype(low)
        return (
            grad_after_cross,
            grad_gain,
            grad_bias,
            times_transposed(cross_branch, cross_output_low).astype(low),
            weight_gradient(links.positions(True), cross_mixed, [cross_branch]),
        )

    grad_after_cross, grad_gain_2, grad_bias_2, grad_cross_mixed, cross_out = order.run(
        cross_entry, grad_after_feed, after_cross, grad_normed, gain_table[2], cross_output_low, cross_mixed
    )
    if links.pairwise:
        feed_sum = order.run(
            lambda *arrays: links.sum_cores(
                jnp.concatenate(arrays[:2], axis=1), jnp.concatenate(arrays[2:], axis=1)
            ),
            in_keep,
            out_grad[out_half:],
            in_other,
            out_other,
        )
        feed_chips = links.sum_chips(feed_sum)
    else:
        feed_in_part = links.scatter_whole(in_send, in_keep)
        feed_out_part = links.scatter_whole(out_grad[: out_grad.shape[0] // 2], out_grad[out_grad.shape[0] // 2 :])

    def cross_middle(cross_queries, cross_kv, cross_mixed, grad_cross_mixed, cross_totals):
        grad_q, grad_k, grad_v = attention_backward(
            text_lengths,
            cross_queries,
            0,
            cross_kv,
            0,
            cross_kv,
            width // LANES,
            cross_mixed,
            grad_cross_mixed,
            cross_totals,
            False,
        )
        return (
            grad_q,
            grad_k,
            grad_v,
            weight_gradient(links.positions(True), normed_cross, [grad_q]),
            weight_gradient(links.positions(False), encoded, [grad_k, grad_v]),
        )

    grad_q, grad_k, grad_v, cross_query_grad, cross_kv_grad = order.run(
        cross_middle, cross_queries, cross_kv, cross_mixed, grad_cross_mixed, cross_totals
    )
    cross_send, cross_keep = [
        [kv, jnp.concatenate([query, out], axis=1)]
        for kv, query, out in zip(cross_kv_grad, cross_query_grad, cross_out)
    ]
    if links.pairwise:
        cross_sides = list(zip(cross_keep, [links.swap_core(side) for side in cross_send]))

        def exchange(sides, at):
            halves = order.run(
                lambda *arrays: [links.first_pair(*arrays[i : i + 2]) for i in range(0, len(arrays), 2)],
                *[array for side in sides for array in side],
            )
            return [
                (stays, links.swap(goes, links.bit(at, flip))) for (goes, stays), flip in zip(halves, flips)
            ]

        def finish(sides):
            arrays = [array for side in sides for array in side]
            return links.send_fsdp(
                order.run(
                    lambda *arrays: jnp.concatenate(
                        [links.sum_cores(*arrays[i : i + 2]) for i in range(0, len(arrays), 2)], axis=1
                    ),
                    *arrays,
                )
            )

    def cross_exit(grad_q, grad_k, grad_v, cross_query, cross_first, after_self, gain_row, grad_after_cross):
        grad_kv = jnp.concatenate([grad_k, grad_v], axis=1)
        grad_normed = times_transposed(grad_q, cross_query)
        grad_encoded = times_transposed(grad_kv, cross_first)
        grad_input, grad_gain, grad_bias = norm_backward(after_self, gain_row, grad_normed)
        grad_after_self = grad_after_cross + grad_input
        return grad_after_self, grad_encoded, grad_gain, grad_bias

    grad_after_self, grad_encoded, grad_gain_1, grad_bias_1 = order.run(
        cross_exit, grad_q, grad_k, grad_v, cross_query, cross_first, after_self, gain_table[1], grad_after_cross
    )
    if links.pairwise:
        cross_sides = exchange(cross_sides, 0)
    else:
        cross_part = links.scatter_whole(*[jnp.concatenate(side, axis=1) for side in (cross_send, cross_keep)])

    def self_entry(grad_after_self, self_output_low, self_mixed):
        self_branch = grad_after_self.astype(low)
        return (
            times_transposed(self_branch, self_output_low).astype(low),
            weight_gradient(links.positions(True), self_mixed, [self_branch]),
        )

    grad_self_mixed, self_out = order.run(self_entry, grad_after_self, self_output_low, self_mixed)
    grad_q, grad_k, grad_v = order.run(
        lambda query_key, self_values, self_mixed, grad_self_mixed, self_totals: attention_backward(
            unit_lengths,
            query_key,
            0,
            query_key,
            width // LANES,
            self_values,
            0,
            self_mixed,
            grad_self_mixed,
            self_totals,
            True,
        ),
        query_key,
        self_values,
        self_mixed,
        grad_self_mixed,
        self_totals,
    )
    if links.pairwise:
        cross_sides = exchange(cross_sides, 1)
        feed_chips = order.after(feed_chips)
        feed_part = lax.psum_scatter(feed_chips, "fsdp", scatter_dimension=0, tiled=True)
    first_send, first_keep = order.run(
        lambda *grads: weight_gradient(links.positions(False), normed_self, list(grads)), grad_q, grad_k
    )
    if links.pairwise:
        first_other = links.swap_core(first_send)
    second_send, second_keep = order.run(
        lambda grad, *out: [
            jnp.concatenate(pair, axis=1)
            for pair in zip(weight_gradient(links.positions(True), normed_self, [grad]), out)
        ],
        grad_v,
        *self_out,
    )
    if links.pairwise:
        self_sides = [(first_keep, first_other), (second_keep, links.swap_core(second_send))]
        cross_parts = finish(cross_sides)
        self_sides = exchange(self_sides, 0)

    def self_exit(grad_q, grad_k, grad_v, self_first, self_value, gain_row, grad_after_self, *others):
        grad_qk = jnp.concatenate([grad_q, grad_k], axis=1)
        grad_normed = times_transposed(grad_qk, self_first) + times_transposed(grad_v, self_value)
        grad_input, grad_gain, grad_bias = norm_backward(layer_input, gain_row, grad_normed)
        grad_tables = jnp.stack([grad_gain, *others[:3], grad_bias, *others[3:]])
        return grad_after_self + grad_input, jnp.pad(grad_tables.T, ((0, 0), (0, LANES - 8))).astype(low)

    grad_states, grad_tables = order.run(
        self_exit,
        grad_q,
        grad_k,
        grad_v,
        self_first,
        self_value,
        gain_table[0],
        grad_after_self,
        grad_gain_1,
        grad_gain_2,
        grad_gain_3,
        grad_bias_1,
        grad_bias_2,
        grad_bias_3,
    )
    table_send, table_keep = links.halves(grad_tables, False)
    if links.pairwise:
        cross_part = order.run(links.sum_fsdp, cross_parts)
        table_goes, table_stays = links.first_pair(table_keep, links.swap_core(table_send))
        table_side = (table_stays, links.swap(table_goes, links.bit(0, False)))
        self_sides = exchange(self_sides, 1)
        feed_part = order.run(lambda part: part.astype(jnp.float32), feed_part)
        table_goes, table_stays = links.first_pair(*table_side)
        table_side = (table_stays, links.swap(table_goes, links.bit(1, False)))
        self_part = links.sum_fsdp(finish(self_sides + [table_side]))
        feed_in_part, feed_out_part = feed_part[:, : 4 * width], feed_part[:, 4 * width :]
        feed_out_part = jnp.concatenate(
            [feed_out_part[:, at * width : (at + 1) * width] for at in range(4)], axis=0
        )
    else:
        self_part = jnp.concatenate(
            [
                links.scatter_whole(*pair)
                for pair in ((first_send, first_keep), (second_send, second_keep), (table_send, table_keep))
            ],
            axis=1,
        )
    self_in_part, self_out_part = self_part[:, : 3 * width], self_part[:, 3 * width : 4 * width]
    table_part = self_part[:, 4 * width :]
    cross_in_part = jnp.concatenate([cross_part[:, split : 3 * width], cross_part[:, :split]], axis=1)
    cross_out_part = cross_part[:, 3 * width :]

    return (
        block_output[None],
        grad_states[None],
        grad_encoded[None],
        self_in_part,
        self_out_part,
        cross_in_part,
        cross_out_part,
        feed_in_part,
        feed_out_part,
        table_part[:, :4].T,
        table_part[:, 4:8].T,
    )


def solution(mesh):
    dp_count, fsdp_count = mesh.shape["dp"], mesh.shape["fsdp"]
    split = Mesh(mesh.devices.reshape(dp_count // 2, 2, fsdp_count), BOTH)
    return jax.shard_map(
        body,
        mesh=split,
        in_specs=(
            P(BOTH, None, None),
            P(BOTH, None, None),
            P(BOTH, None, None),
            P(BOTH),
            P(BOTH),
            P(BOTH, None),
            P(BOTH, None),
            P(BOTH, None),
            P(BOTH, None),
            P(BOTH, None),
            P(BOTH, None),
            P(None, BOTH),
            P(None, BOTH),
        ),
        out_specs=(
            P(BOTH, None, None),
            P(BOTH, None, None),
            P(BOTH, None, None),
            P(BOTH, None),
            P(BOTH, None),
            P(BOTH, None),
            P(BOTH, None),
            P(BOTH, None),
            P(BOTH, None),
            P(None, BOTH),
            P(None, BOTH),
        ),
        check_vma=False,
    )
```

```python
import functools

import jax
import jax.numpy as jnp
from jax import lax
from jax.experimental import pallas as pl
from jax.experimental.pallas import tpu as pltpu
from jax.sharding import Mesh
from jax.sharding import PartitionSpec as P

HEAD = 64
LANES = 128
AHEAD = 1
BOTH = ("h", "c", "fsdp")
VMEM_BYTES = 60 * 1024 * 1024
SHORT = pl.CostEstimate(flops=1024, transcendentals=0, bytes_accessed=1024)


def product(left, right):
    return jnp.dot(left, right, preferred_element_type=jnp.float32)


def contract_rows(left, right):
    return lax.dot_general(
        left, right, (((0,), (0,)), ((), ())), preferred_element_type=jnp.float32
    )


def times_transposed(left, right):
    return lax.dot_general(
        left, right, (((1,), (1,)), ((), ())), preferred_element_type=jnp.float32
    )


def layer_norm(values, gain_row, bias_row):
    centre = values - jnp.mean(values, axis=-1, keepdims=True)
    spread = jnp.mean(centre * centre, axis=-1, keepdims=True)
    return centre * lax.rsqrt(spread + 1e-05) * gain_row + bias_row


def row_blocks(row_count, step):
    step = step if row_count % step == 0 else row_count
    return [slice(start, start + step) for start in range(0, row_count, step)]


def norm_backward_rows(norm, values_ref, grad_of, base_ref, rows_ref, grad_ref, low_ref, sums_ref, normed_ref=None):
    gain, bias = rows_ref[norm : norm + 1, :], rows_ref[4 + norm : 5 + norm, :]
    gain_sum, bias_sum = jnp.zeros_like(gain), jnp.zeros_like(gain)
    for rows in row_blocks(values_ref.shape[0], LANES):
        values = values_ref[rows, :].astype(jnp.float32)
        grad = grad_of(rows)
        centre = values - jnp.mean(values, axis=-1, keepdims=True)
        rate = lax.rsqrt(jnp.mean(centre * centre, axis=-1, keepdims=True) + 1e-05)
        normed = centre * rate
        if normed_ref is not None:
            normed_ref[rows, :] = (normed * gain + bias).astype(normed_ref.dtype)
        scaled = grad * gain
        total = rate * (
            scaled
            - jnp.mean(scaled, axis=-1, keepdims=True)
            - normed * jnp.mean(scaled * normed, axis=-1, keepdims=True)
        )
        if base_ref is not None:
            total = base_ref[rows, :] + total
        grad_ref[rows, :] = total
        if low_ref is not None:
            low_ref[rows, :] = total.astype(jnp.bfloat16)
        gain_sum += jnp.sum(grad * normed, axis=0, keepdims=True)
        bias_sum += jnp.sum(grad, axis=0, keepdims=True)
    sums_ref[0:1, :] = gain_sum
    sums_ref[1:2, :] = bias_sum


def with_bias_lane(matrix, head, bias):
    lane = lax.broadcasted_iota(jnp.int32, matrix.shape, 1)
    own = (lane >= head * HEAD) & (lane < (head + 1) * HEAD)
    rest = jnp.where(lane == (1 - head) * HEAD, bias, 0.0).astype(matrix.dtype)
    return jnp.where(own, matrix, rest)


def key_bias(key_count, key_limit):
    row = lax.broadcasted_iota(jnp.int32, (key_count, LANES), 0)
    return jnp.where(row < key_limit, 0.0, -1e30)


def masked_scores(keys, queries, diagonal_ref):
    scores = times_transposed(keys, queries)
    if diagonal_ref is None:
        return scores
    below = scores.shape[0] - scores.shape[1]
    diagonal = scores[below:, :] + diagonal_ref[...]
    return jnp.concatenate([scores[:below, :], diagonal], axis=0) if below else diagonal


def set_diagonal(diagonal_ref):
    @pl.when(pl.program_id(0) == 0)
    def _():
        row = lax.broadcasted_iota(jnp.int32, diagonal_ref.shape, 0)
        column = lax.broadcasted_iota(jnp.int32, diagonal_ref.shape, 1)
        diagonal_ref[...] = jnp.where(row <= column, 0.0, -1e30)


def query_width(row_count, causal):
    return 256 if causal and row_count % 256 == 0 else row_count


def query_blocks(row_count, key_count, causal):
    width = query_width(row_count, causal)
    return [
        (start, width, start + width if causal else key_count)
        for start in range(0, row_count, width)
    ]


def head_lanes(head, shape):
    lane = lax.broadcasted_iota(jnp.int32, shape, 1)
    return (lane >= head * HEAD) & (lane < (head + 1) * HEAD)


def staggered(items, first, middle, last, ahead):
    begun = [first(item) for item in items[:ahead]]
    waiting = None
    for at, item in enumerate(items):
        if at + ahead < len(items):
            begun.append(first(items[at + ahead]))
        done = middle(item, begun[at])
        begun[at] = None
        if waiting is not None:
            last(*waiting)
        waiting = (item, done)
    last(*waiting)


def attention_forward_kernel(
    causal, limit_ref, q_ref, k_ref, v_ref, mixed_ref, total_ref, mixed_turned, diagonal_ref
):
    row_count, key_count = q_ref.shape[0], k_ref.shape[0]
    bias = key_bias(key_count, limit_ref[0])
    if causal:
        set_diagonal(diagonal_ref)
    else:
        diagonal_ref = None
    values_turned = v_ref[...].T
    ones = jnp.ones((16, key_count), jnp.bfloat16)
    scaled = q_ref[...] * jnp.bfloat16(HEAD**-0.5)
    queries = [with_bias_lane(scaled, head, 1.0) for head in range(2)]
    keys = [with_bias_lane(k_ref[...], head, bias) for head in range(2)]
    lanes = [slice(head * HEAD, (head + 1) * HEAD) for head in range(2)]
    values = [jnp.concatenate([values_turned[at, :], ones], axis=0) for at in lanes]

    def scores_of(item):
        head, (start, width, stop) = item
        return masked_scores(keys[head][:stop, :], queries[head][start : start + width, :], diagonal_ref)

    def expand(item, scores):
        highest = jnp.max(scores, axis=0, keepdims=True)
        return highest, jnp.exp(scores - highest).astype(jnp.bfloat16)

    def mix(item, done):
        head, (start, width, stop) = item
        highest, expanded = done
        mixed = product(values[head][:, :stop], expanded)
        total = mixed[HEAD : HEAD + 1, :]
        mixed_turned[lanes[head], start : start + width] = mixed[:HEAD, :] / total
        total_ref[0, head : head + 1, start : start + width] = highest + jnp.log(total)

    items = [(head, block) for block in query_blocks(row_count, key_count, causal) for head in range(2)]
    staggered(items, scores_of, expand, mix, 2)
    mixed_ref[...] = mixed_turned[...].T.astype(jnp.bfloat16)


def attention_forward(limit, queries, q_at, keys, k_at, values, v_at, causal):
    row_count, key_count = queries.shape[0], keys.shape[0]
    width = 1024
    pairs = width // LANES
    return pl.pallas_call(
        functools.partial(attention_forward_kernel, causal),
        grid_spec=pltpu.PrefetchScalarGridSpec(
            num_scalar_prefetch=1,
            grid=(pairs,),
            in_specs=[
                pl.BlockSpec((row_count, LANES), lambda p, s: (0, q_at + p)),
                pl.BlockSpec((key_count, LANES), lambda p, s: (0, k_at + p)),
                pl.BlockSpec((key_count, LANES), lambda p, s: (0, v_at + p)),
            ],
            out_specs=[
                pl.BlockSpec((row_count, LANES), lambda p, s: (0, p)),
                pl.BlockSpec((1, 2, row_count), lambda p, s: (p, 0, 0)),
            ],
            scratch_shapes=[
                pltpu.VMEM((LANES, row_count), jnp.float32),
                pltpu.VMEM((query_width(row_count, causal),) * 2, jnp.float32),
            ],
        ),
        out_shape=[
            jax.ShapeDtypeStruct((row_count, width), jnp.bfloat16),
            jax.ShapeDtypeStruct((pairs, 2, row_count), jnp.float32),
        ],
        compiler_params=pltpu.CompilerParams(vmem_limit_bytes=VMEM_BYTES),
        cost_estimate=SHORT,
        name="attention_forward",
    )(limit, queries, keys, values)


def attention_backward_kernel(
    causal,
    limit_ref,
    q_ref,
    k_ref,
    v_ref,
    mixed_ref,
    grad_ref,
    total_ref,
    grad_q_ref,
    grad_k_ref,
    grad_v_ref,
    grad_q_turned,
    grad_k_sum,
    grad_v_sum,
    diagonal_ref,
):
    row_count, key_count = q_ref.shape[0], k_ref.shape[0]
    bias = key_bias(key_count, limit_ref[0])
    if causal:
        set_diagonal(diagonal_ref)
    else:
        diagonal_ref = None
    keys_turned = k_ref[...].T
    scaled = q_ref[...] * jnp.bfloat16(HEAD**-0.5)
    grad = grad_ref[...]
    inner_turned = (grad.astype(jnp.float32) * mixed_ref[...].astype(jnp.float32)).T
    grad_k_sum[...] = jnp.zeros_like(grad_k_sum)
    grad_v_sum[...] = jnp.zeros_like(grad_v_sum)
    masks = [head_lanes(head, scaled.shape) for head in range(2)]
    queries = [jnp.where(mask, scaled, jnp.zeros_like(scaled)) for mask in masks]
    grads = [jnp.where(mask, grad, jnp.zeros_like(grad)) for mask in masks]
    biased = [with_bias_lane(scaled, head, 1.0) for head in range(2)]
    keys = [with_bias_lane(k_ref[...], head, bias) for head in range(2)]
    lanes = [slice(head * HEAD, (head + 1) * HEAD) for head in range(2)]
    inner = [jnp.sum(inner_turned[at, :], axis=0, keepdims=True) for at in lanes]

    def scores_of(item):
        head, (start, width, stop) = item
        columns = slice(start, start + width)
        scores = masked_scores(keys[head][:stop, :], biased[head][columns, :], diagonal_ref)
        return scores, times_transposed(v_ref[:stop, :], grads[head][columns, :])

    def differentiate(item, begun):
        head, (start, width, stop) = item
        columns = slice(start, start + width)
        scores, grad_probs = begun
        probs = jnp.exp(scores - total_ref[0, head : head + 1, columns])
        grad_scores = probs * (grad_probs - inner[head][:, columns])
        return probs.astype(jnp.bfloat16), grad_scores.astype(jnp.bfloat16)

    def add(item, done):
        head, (start, width, stop) = item
        columns = slice(start, start + width)
        probs, grad_scores = done
        grad_v_sum[:stop, :] += product(probs, grads[head][columns, :])
        grad_k_sum[:stop, :] += product(grad_scores, queries[head][columns, :])
        grad_q_turned[lanes[head], columns] = product(keys_turned[lanes[head], :stop], grad_scores)

    items = [(head, block) for block in query_blocks(row_count, key_count, causal) for head in range(2)]
    staggered(items, scores_of, differentiate, add, AHEAD)
    grad_q_ref[...] = (grad_q_turned[...].T * HEAD**-0.5).astype(jnp.bfloat16)
    grad_k_ref[...] = grad_k_sum[...].astype(jnp.bfloat16)
    grad_v_ref[...] = grad_v_sum[...].astype(jnp.bfloat16)


def attention_backward(limit, queries, q_at, keys, k_at, values, v_at, mixed, grad_mixed, totals, causal):
    row_count, key_count = queries.shape[0], keys.shape[0]
    width = 1024
    pairs = width // LANES
    row_block = pl.BlockSpec((row_count, LANES), lambda p, s: (0, p))
    key_block = pl.BlockSpec((key_count, LANES), lambda p, s: (0, p))
    return pl.pallas_call(
        functools.partial(attention_backward_kernel, causal),
        grid_spec=pltpu.PrefetchScalarGridSpec(
            num_scalar_prefetch=1,
            grid=(pairs,),
            in_specs=[
                pl.BlockSpec((row_count, LANES), lambda p, s: (0, q_at + p)),
                pl.BlockSpec((key_count, LANES), lambda p, s: (0, k_at + p)),
                pl.BlockSpec((key_count, LANES), lambda p, s: (0, v_at + p)),
                row_block,
                row_block,
                pl.BlockSpec((1, 2, row_count), lambda p, s: (p, 0, 0)),
            ],
            out_specs=[row_block, key_block, key_block],
            scratch_shapes=[
                pltpu.VMEM((LANES, row_count), jnp.float32),
                pltpu.VMEM((key_count, LANES), jnp.float32),
                pltpu.VMEM((key_count, LANES), jnp.float32),
                pltpu.VMEM((query_width(row_count, causal),) * 2, jnp.float32),
            ],
        ),
        out_shape=[
            jax.ShapeDtypeStruct((row_count, width), jnp.bfloat16),
            jax.ShapeDtypeStruct((key_count, width), jnp.bfloat16),
            jax.ShapeDtypeStruct((key_count, width), jnp.bfloat16),
        ],
        compiler_params=pltpu.CompilerParams(vmem_limit_bytes=VMEM_BYTES),
        cost_estimate=SHORT,
        name="attention_backward",
    )(limit, queries, keys, values, mixed, grad_mixed, totals)


def gelu_and_slope(values):
    normal_cdf = 0.5 + 0.5 * lax.erf(values * 2.0 ** (-0.5))
    bell = jnp.exp(-0.5 * values * values) * (2.0 * jnp.pi) ** (-0.5)
    return values * normal_cdf, normal_cdf + values * bell


def unfold_rows(folded_ref, unfolded, rows):
    width = unfolded.shape[1]
    folds = folded_ref.shape[1] // width
    for shard in range(folded_ref.shape[0] // rows):
        for fold in range(folds):
            start = (shard * folds + fold) * rows
            unfolded[start : start + rows, :] = folded_ref[
                shard * rows : (shard + 1) * rows, fold * width : (fold + 1) * width
            ]


def fold_rows(unfolded, folded_ref, rows):
    width = unfolded.shape[1]
    folds = folded_ref.shape[1] // width
    for shard in range(folded_ref.shape[0] // rows):
        for fold in range(folds):
            start = (shard * folds + fold) * rows
            folded_ref[shard * rows : (shard + 1) * rows, fold * width : (fold + 1) * width] = unfolded[
                start : start + rows, :
            ]


def feed_forward_kernel(
    rows,
    limit_ref,
    normed_ref,
    input_ref,
    output_ref,
    base_ref,
    cotangent_ref,
    rows_ref,
    hidden_ref,
    slope_ref,
    block_ref,
    grad_ref,
    low_ref,
    sums_ref,
    after_ref,
    unfolded,
):
    if rows:
        unfold_rows(output_ref, unfolded, rows)
        output_ref = unfolded

    @pl.when(pl.program_id(0) == 0)
    def _():
        after_ref[...] = base_ref[...]

    row_count = normed_ref.shape[0]
    step = 256 if row_count % 256 == 0 else row_count
    blocks = [slice(start, start + step) for start in range(0, row_count, step)]
    hidden_pre = product(normed_ref[blocks[0], :], input_ref[...])
    ready = None
    for at, rows_at in enumerate(blocks):
        following = product(normed_ref[blocks[at + 1], :], input_ref[...]) if at + 1 < len(blocks) else None
        hidden, slope = gelu_and_slope(hidden_pre)
        hidden = hidden.astype(jnp.bfloat16)
        hidden_ref[rows_at, :] = hidden
        slope_ref[rows_at, :] = slope.astype(jnp.bfloat16)
        if ready is not None:
            after_ref[blocks[at - 1], :] += product(ready, output_ref[...])
        hidden_pre, ready = following, hidden
    after_ref[blocks[-1], :] += product(ready, output_ref[...])

    @pl.when(pl.program_id(0) == pl.num_programs(0) - 1)
    def _():
        def live_grad(rows_at):
            shape = (rows_at.stop - rows_at.start, after_ref.shape[1])
            row = rows_at.start + lax.broadcasted_iota(jnp.int32, shape, 0)
            return jnp.where(row < limit_ref[0], cotangent_ref[rows_at, :], 0.0)

        norm_backward_rows(3, after_ref, live_grad, None, rows_ref, grad_ref, low_ref, sums_ref, block_ref)


FEED_TILE = 512


def feed_weight_specs(folds, width, tile, index):
    first = pl.BlockSpec((width, tile), lambda *at: (0, index(*at)))
    if folds:
        return first, pl.BlockSpec((tile // folds, folds * width), lambda *at: (index(*at), 1))
    return first, pl.BlockSpec((tile, width), lambda *at: (index(*at), 0))


def feed_forward(rows, limit, normed, input_low, output_low, after_cross, cotangent, norm_rows):
    row_count, width = normed.shape
    hidden_width = 4 * width
    tile = FEED_TILE
    whole = pl.BlockSpec((row_count, width), lambda j, s: (0, 0))
    tall = pl.BlockSpec((row_count, tile), lambda j, s: (0, j))
    weight_specs = feed_weight_specs(hidden_width // width if rows else 0, width, tile, lambda j, s: j)
    return pl.pallas_call(
        functools.partial(feed_forward_kernel, rows),
        grid_spec=pltpu.PrefetchScalarGridSpec(
            num_scalar_prefetch=1,
            grid=(hidden_width // tile,),
            in_specs=[whole, *weight_specs, whole, whole, pl.BlockSpec((8, width), lambda j, s: (0, 0))],
            out_specs=[tall, tall, whole, whole, whole, pl.BlockSpec((2, width), lambda j, s: (0, 0))],
            scratch_shapes=[pltpu.VMEM((row_count, width), jnp.float32), pltpu.VMEM((tile, width), jnp.bfloat16)],
        ),
        out_shape=[
            jax.ShapeDtypeStruct((row_count, hidden_width), jnp.bfloat16),
            jax.ShapeDtypeStruct((row_count, hidden_width), jnp.bfloat16),
            jax.ShapeDtypeStruct((row_count, width), jnp.bfloat16),
            jax.ShapeDtypeStruct((row_count, width), jnp.float32),
            jax.ShapeDtypeStruct((row_count, width), jnp.bfloat16),
            jax.ShapeDtypeStruct((2, width), jnp.float32),
        ],
        compiler_params=pltpu.CompilerParams(vmem_limit_bytes=VMEM_BYTES),
        cost_estimate=SHORT,
        name="feed_forward",
    )(limit, normed, input_low, output_low, after_cross, cotangent, norm_rows)


def turn_rows(x_ref, turned, positions_ref):
    for j in range(x_ref.shape[1] // LANES):
        start = pl.multiple_of(positions_ref[j] * LANES, LANES)
        turned[pl.ds(start, LANES), :] = x_ref[:, j * LANES : (j + 1) * LANES].T


def feed_backward_kernel(
    rows,
    tiles_ref,
    positions_ref,
    grad_ref,
    normed_ref,
    hidden_ref,
    slope_ref,
    input_ref,
    output_ref,
    values_ref,
    base_ref,
    rows_ref,
    in_send_ref,
    in_keep_ref,
    out_send_ref,
    out_keep_ref,
    total_ref,
    low_ref,
    sums_ref,
    grad_normed_ref,
    turned,
    unfolded,
):
    step = pl.program_id(0)
    if rows:
        unfold_rows(output_ref, unfolded, rows)
        output_ref = unfolded

    @pl.when(step == 0)
    def _():
        grad_normed_ref[...] = jnp.zeros_like(grad_normed_ref)
        turn_rows(normed_ref, turned, positions_ref)

    grad_hidden = times_transposed(grad_ref[...], output_ref[...])
    grad_pre = (grad_hidden * slope_ref[...].astype(jnp.float32)).astype(jnp.bfloat16)
    grad_out = contract_rows(hidden_ref[...], grad_ref[...]).astype(jnp.bfloat16)
    for out_ref, first in ((out_send_ref, True), (out_keep_ref, False)):

        @pl.when((step < pl.num_programs(0) // 2) == first)
        def _(out_ref=out_ref):
            if rows:
                fold_rows(grad_out, out_ref, rows)
            else:
                out_ref[...] = grad_out

    half = turned.shape[0] // 2
    in_send_ref[...] = product(turned[:half, :], grad_pre).astype(jnp.bfloat16)
    in_keep_ref[...] = product(turned[half:, :], grad_pre).astype(jnp.bfloat16)
    grad_normed_ref[...] += times_transposed(grad_pre, input_ref[...])

    @pl.when(step == pl.num_programs(0) - 1)
    def _():
        norm_backward_rows(
            2,
            values_ref,
            lambda rows_at: grad_normed_ref[rows_at, :],
            base_ref,
            rows_ref,
            total_ref,
            low_ref,
            sums_ref,
        )


def feed_backward(
    rows, tiles, positions, grad_branch, normed, hidden, slope, input_low, output_low, after_cross, grad_after, norm_rows
):
    row_count, width = grad_branch.shape
    hidden_width = hidden.shape[1]
    count = tiles.shape[0]
    half = count // 2
    tile = hidden_width // count
    whole = pl.BlockSpec((row_count, width), lambda j, t, p: (0, 0))
    tall = pl.BlockSpec((row_count, tile), lambda j, t, p: (0, t[j]))
    in_half = pl.BlockSpec((width // 2, tile), lambda j, t, p: (0, t[j]))
    folds = hidden_width // width if rows else 1
    weight_specs = feed_weight_specs(folds if rows else 0, width, tile, lambda j, t, p: t[j])
    return pl.pallas_call(
        functools.partial(feed_backward_kernel, rows),
        grid_spec=pltpu.PrefetchScalarGridSpec(
            num_scalar_prefetch=2,
            grid=(count,),
            in_specs=[
                whole,
                whole,
                tall,
                tall,
                *weight_specs,
                whole,
                whole,
                pl.BlockSpec((8, width), lambda j, t, p: (0, 0)),
            ],
            out_specs=[
                in_half,
                in_half,
                pl.BlockSpec((tile // folds, folds * width), lambda j, t, p: (jnp.minimum(j, half - 1), 0)),
                pl.BlockSpec((tile // folds, folds * width), lambda j, t, p: (jnp.maximum(j - half, 0), 0)),
                whole,
                whole,
                pl.BlockSpec((2, width), lambda j, t, p: (0, 0)),
            ],
            scratch_shapes=[
                pltpu.VMEM((row_count, width), jnp.float32),
                pltpu.VMEM((width, row_count), jnp.bfloat16),
                pltpu.VMEM((tile, width), jnp.bfloat16),
            ],
        ),
        out_shape=[
            jax.ShapeDtypeStruct((width // 2, hidden_width), jnp.bfloat16),
            jax.ShapeDtypeStruct((width // 2, hidden_width), jnp.bfloat16),
            jax.ShapeDtypeStruct((hidden_width // folds // 2, folds * width), jnp.bfloat16),
            jax.ShapeDtypeStruct((hidden_width // folds // 2, folds * width), jnp.bfloat16),
            jax.ShapeDtypeStruct((row_count, width), jnp.float32),
            jax.ShapeDtypeStruct((row_count, width), jnp.bfloat16),
            jax.ShapeDtypeStruct((2, width), jnp.float32),
        ],
        compiler_params=pltpu.CompilerParams(vmem_limit_bytes=VMEM_BYTES),
        cost_estimate=SHORT,
        name="feed_backward",
    )(
        tiles, positions, grad_branch, normed, hidden, slope, input_low, output_low, after_cross, grad_after, norm_rows
    )


WEIGHT_TILE = 512


def tile_starts(arrays):
    starts = [0]
    for array in arrays:
        starts.append(starts[-1] + array.shape[1] // WEIGHT_TILE)
    return starts


def tile_spec(rows, first, last, offset=0):
    return pl.BlockSpec(
        (rows, WEIGHT_TILE), lambda j, *_: (0, offset + jnp.clip(j - first, 0, last - first - 1))
    )


def weight_gradient_kernel(starts, groups, crossed, positions_ref, x_ref, *refs):
    grads, outs, turned = refs[: len(starts) - 1], refs[len(starts) - 1 : -1], refs[-1]
    step = pl.program_id(0)

    @pl.when(step == 0)
    def _():
        turn_rows(x_ref, turned, positions_ref)

    half = turned.shape[0] // 2
    for index, grad_ref in enumerate(grads):
        group = groups[index]

        @pl.when((step >= starts[index]) & (step < starts[index + 1]))
        def _(grad_ref=grad_ref, group=group):
            for out_ref, rows in ((outs[2 * group], slice(0, half)), (outs[2 * group + 1], slice(half, 2 * half))):
                result = product(turned[rows, :], grad_ref[...]).astype(jnp.bfloat16)
                if crossed[group]:
                    for block, place in enumerate((0, 2, 1, 3)):
                        out_ref[place * LANES : (place + 1) * LANES, :] = result[
                            block * LANES : (block + 1) * LANES, :
                        ]
                else:
                    out_ref[...] = result


def weight_gradient(positions, x, *groups):
    row_count, width = x.shape
    grads = [grad for group, _ in groups for grad in group]
    group_of = [index for index, (group, _) in enumerate(groups) for _ in group]
    starts = tile_starts(grads)
    half = width // 2
    out_specs, out_shape = [], []
    for index in range(len(groups)):
        own = [at for at, group in enumerate(group_of) if group == index]
        first, last = starts[own[0]], starts[own[-1] + 1]
        out_specs += [tile_spec(half, first, last)] * 2
        out_shape += [jax.ShapeDtypeStruct((half, (last - first) * WEIGHT_TILE), jnp.bfloat16)] * 2
    return pl.pallas_call(
        functools.partial(weight_gradient_kernel, starts, group_of, [crossed for _, crossed in groups]),
        grid_spec=pltpu.PrefetchScalarGridSpec(
            num_scalar_prefetch=1,
            grid=(starts[-1],),
            in_specs=[pl.BlockSpec((row_count, width), lambda j, p: (0, 0))]
            + [tile_spec(row_count, starts[i], starts[i + 1]) for i in range(len(grads))],
            out_specs=out_specs,
            scratch_shapes=[pltpu.VMEM((width, row_count), jnp.bfloat16)],
        ),
        out_shape=out_shape,
        compiler_params=pltpu.CompilerParams(vmem_limit_bytes=VMEM_BYTES),
        cost_estimate=SHORT,
        name="weight_gradient",
    )(positions, x, *grads)


def input_gradient_kernel(norm, starts, has_low, *refs):
    count = len(starts) - 1
    grads, weights = refs[:count], refs[count : 2 * count]
    values_ref, base_ref, rows_ref, total_ref = refs[2 * count : 2 * count + 4]
    low_ref = refs[2 * count + 4] if has_low else None
    sums_ref, summed = refs[-2:]
    step = pl.program_id(0)

    @pl.when(step == 0)
    def _():
        summed[...] = jnp.zeros_like(summed)

    for index in range(count):

        @pl.when((step >= starts[index]) & (step < starts[index + 1]))
        def _(index=index):
            summed[...] += times_transposed(grads[index][...], weights[index][...])

    @pl.when(step == starts[-1] - 1)
    def _():
        norm_backward_rows(
            norm, values_ref, lambda rows: summed[rows, :], base_ref, rows_ref, total_ref, low_ref, sums_ref
        )


def input_gradient(norm, grads, weights, values, base, norm_rows, has_low):
    row_count, width = values.shape
    starts = tile_starts(grads)
    whole = pl.BlockSpec((row_count, width), lambda j: (0, 0))
    spans = [(starts[i], starts[i + 1]) for i in range(len(grads))]
    lows = [jax.ShapeDtypeStruct((row_count, width), jnp.bfloat16)] if has_low else []
    return pl.pallas_call(
        functools.partial(input_gradient_kernel, norm, starts, has_low),
        grid=(starts[-1],),
        in_specs=[tile_spec(row_count, *span) for span in spans]
        + [
            tile_spec(width, *span, offset=column // WEIGHT_TILE) for span, (_, column) in zip(spans, weights)
        ]
        + [whole, whole, pl.BlockSpec((8, width), lambda j: (0, 0))],
        out_specs=[whole] * (1 + len(lows)) + [pl.BlockSpec((2, width), lambda j: (0, 0))],
        out_shape=[jax.ShapeDtypeStruct((row_count, width), jnp.float32)]
        + lows
        + [jax.ShapeDtypeStruct((2, width), jnp.float32)],
        scratch_shapes=[pltpu.VMEM((row_count, width), jnp.float32)],
        compiler_params=pltpu.CompilerParams(vmem_limit_bytes=VMEM_BYTES),
        cost_estimate=SHORT,
        name="input_gradient",
    )(*grads, *[array for array, _ in weights], values, base, norm_rows)


class Order:
    def __init__(self):
        self.last = ()

    def after(self, *values):
        values, _ = lax.optimization_barrier((values, self.last))
        return values if len(values) > 1 else values[0]

    def run(self, work, *values):
        values, _ = lax.optimization_barrier((values, self.last))
        result = work(*values)
        self.last = result
        return result


def place_rows_kernel(counts, rows, table_ref, *refs):
    pieces, out_ref, held, sems_in, sems_out = refs[:-4], *refs[-4:]
    loads, stores = [], []
    for piece, count in zip(pieces, counts):
        for block in range(count):
            at = len(loads)
            start = pl.multiple_of(table_ref[at] * rows, rows)
            loads.append(
                pltpu.make_async_copy(piece.at[pl.ds(block * rows, rows), :], held.at[at], sems_in.at[at])
            )
            stores.append(
                pltpu.make_async_copy(held.at[at], out_ref.at[pl.ds(start, rows), :], sems_out.at[at])
            )
    for load in loads:
        load.start()
    for load, store in zip(loads, stores):
        load.wait()
        store.start()
    for store in stores:
        store.wait()


def place_rows(table, pieces, rows):
    counts = [piece.shape[0] // rows for piece in pieces]
    total, columns = sum(counts), pieces[0].shape[1]
    anywhere = pl.BlockSpec(memory_space=pl.ANY)
    return pl.pallas_call(
        functools.partial(place_rows_kernel, counts, rows),
        grid_spec=pltpu.PrefetchScalarGridSpec(
            num_scalar_prefetch=1,
            grid=(1,),
            in_specs=[anywhere] * len(pieces),
            out_specs=anywhere,
            scratch_shapes=[
                pltpu.VMEM((total, rows, columns), pieces[0].dtype),
                pltpu.SemaphoreType.DMA((total,)),
                pltpu.SemaphoreType.DMA((total,)),
            ],
        ),
        out_shape=jax.ShapeDtypeStruct((total * rows, columns), pieces[0].dtype),
        compiler_params=pltpu.CompilerParams(vmem_limit_bytes=VMEM_BYTES),
        cost_estimate=SHORT,
        name="place_rows",
    )(table, *pieces)


class Links:
    def __init__(self, width):
        self.h_count, self.fsdp_count = lax.axis_size("h"), lax.axis_size("fsdp")
        self.core, self.h, self.fsdp = lax.axis_index("c"), lax.axis_index("h"), lax.axis_index("fsdp")
        dp_count = 2 * self.h_count
        self.pairwise = (
            (self.h_count & (self.h_count - 1)) == 0
            and (self.fsdp_count & (self.fsdp_count - 1)) == 0
            and width == dp_count * LANES
        )
        self.blocks = width // LANES
        self.bits = [1 << b for b in range(self.h_count.bit_length() - 1)]
        self.fsdp_table = (self.fsdp ^ jnp.arange(self.fsdp_count, dtype=jnp.int32)).astype(jnp.int32)

    def order(self, flip):
        return self.bits[::-1] if flip else self.bits

    def swap(self, array, bit):
        return lax.ppermute(array, "h", [(i, i ^ bit) for i in range(self.h_count)])

    def swap_core(self, array):
        return lax.ppermute(array, "c", [(0, 1), (1, 0)])

    def swap_fsdp(self, array, bit):
        return lax.ppermute(array, "fsdp", [(i, i ^ bit) for i in range(self.fsdp_count)])

    def gather(self, shard):
        return lax.all_gather(shard, BOTH, axis=0, tiled=True)

    def spread_fsdp(self, shard):
        return [shard] + [self.swap_fsdp(shard, k) for k in range(1, self.fsdp_count)]

    def place_fsdp(self, parts):
        return place_rows(self.fsdp_table, parts, parts[0].shape[0])

    def spread(self, block, at, flip):
        return jnp.concatenate([block, self.swap(block, self.order(flip)[at])], axis=0)

    def place(self, block, other, flip):
        masks = [0]
        for bit in self.order(flip):
            masks = masks + [mask ^ bit for mask in masks]
        h = self.h ^ jnp.asarray(masks, dtype=jnp.int32)
        table = jnp.concatenate([2 * h + self.core, 2 * h + 1 - self.core]).astype(jnp.int32)
        return place_rows(table, [block, other], block.shape[0] // self.h_count)

    def tiles(self):
        if not self.pairwise:
            return jnp.arange(self.blocks, dtype=jnp.int32)
        h = 2 * jnp.arange(self.h_count, dtype=jnp.int32)
        return jnp.concatenate([h + 1 - self.core, h + self.core]).astype(jnp.int32)

    def positions(self, flip=None):
        block = jnp.arange(self.blocks, dtype=jnp.int32)
        if not self.pairwise:
            return block
        place, own = block >> 1, (block & 1) == self.core
        if flip is not None:
            mask, place = place ^ self.h, jnp.zeros_like(place)
            for at, bit in enumerate(self.order(flip)):
                place = place + jnp.where((mask & bit) == 0, 1 << at, 0)
        return (place + jnp.where(own, self.h_count, 0)).astype(jnp.int32)

    def halves(self, rows, flip):
        ordered = place_rows(self.positions(flip), [rows], rows.shape[0] // self.blocks)
        half = rows.shape[0] // 2
        return ordered[:half], ordered[half:]

    def sum_cores(self, keep, other):
        return (keep.astype(jnp.float32) + other.astype(jnp.float32)).astype(jnp.bfloat16)

    def send_fsdp(self, grad):
        return lax.all_to_all(grad, "fsdp", 0, 0, tiled=True)

    def sum_fsdp(self, parts):
        rows = parts.shape[0] // self.fsdp_count
        parts = parts.astype(jnp.float32)
        return sum(parts[k * rows : (k + 1) * rows] for k in range(self.fsdp_count))

    def sum_all_fsdp(self, grad):
        grad = grad.astype(jnp.float32)
        for bit in range(self.fsdp_count.bit_length() - 1):
            grad = grad + self.swap_fsdp(grad, 1 << bit)
        rows = grad.shape[0] // self.fsdp_count
        return lax.dynamic_slice_in_dim(grad, self.fsdp * rows, rows, 0)

    def scatter_whole(self, send, keep):
        grad = jnp.concatenate([send, keep], axis=0).astype(jnp.float32)
        part = lax.psum_scatter(grad, ("h", "c"), scatter_dimension=0, tiled=True)
        return lax.psum_scatter(part, "fsdp", scatter_dimension=0, tiled=True)

    def sum_chips(self, grad):
        return lax.psum_scatter(grad, "h", scatter_dimension=0, tiled=True)

    def first_pair(self, keep, other):
        half = keep.shape[0] // 2
        return self.sum_cores(keep[:half], other[:half]), self.sum_cores(keep[half:], other[half:])

    def bit(self, at, flip):
        return self.order(flip)[::-1][at]


def body(
    unit_states,
    encoder_states,
    cotangent,
    unit_lengths,
    text_lengths,
    self_project,
    self_output,
    cross_project,
    cross_output,
    feed_input,
    feed_output,
    norm_gains,
    norm_biases,
):
    low = jnp.bfloat16
    layer_input = unit_states[0].astype(jnp.float32)
    encoded = encoder_states[0]
    row_count, width = layer_input.shape
    links = Links(width)

    tables = jnp.concatenate([norm_gains, norm_biases], axis=0).T
    tables = jnp.pad(tables, ((0, 0), (0, LANES - tables.shape[1])))
    self_shard = jnp.concatenate([self_project.astype(low), self_output.astype(low), tables], axis=1)
    cross_shard = jnp.concatenate(
        [cross_project[:, width:].astype(low), cross_project[:, :width].astype(low), cross_output.astype(low)],
        axis=1,
    )
    feed_shard = feed_input.astype(low)
    order = Order()
    flips = [False, True]
    split = 2 * width
    if links.pairwise:
        fold_count = feed_input.shape[0]
        folded = [
            feed_output[at : at + fold_count].astype(low) for at in range(0, feed_output.shape[0], fold_count)
        ]
        feed_shard = jnp.concatenate([feed_shard] + folded, axis=1)
        bits = [links.order(flip) for flip in flips]

        def send(sides, at):
            return [links.swap(side, bit[at]) for side, bit in zip(sides, bits)]

        def join(*arrays):
            half = len(arrays) // 2
            return [jnp.concatenate(pair, axis=0) for pair in zip(arrays[:half], arrays[half:])]

        def lay(*arrays):
            half = len(arrays) // 2
            return [links.place(*pair, flip) for pair, flip in zip(zip(arrays[:half], arrays[half:]), flips)]

        def lay_fsdp(*parts):
            return links.place_fsdp(parts)

        gathered = links.gather(jnp.concatenate([feed_shard, cross_shard], axis=1))
        feed_input_low, feed_output_low, cross_whole = gathered, gathered, gathered[:, 8 * width :]
        cross_held, cross_at = gathered, 8 * width
        self_part = order.run(lay_fsdp, *links.spread_fsdp(self_shard))
        self_sides = [self_part[:, :split], self_part[:, split:]]
        self_swaps = send(self_sides, 0)
        self_sides = order.run(join, *self_sides, *self_swaps)
        self_swaps = send(self_sides, 1)
        self_sides = order.run(join, *self_sides, *self_swaps)
        self_others = [links.swap_core(side) for side in self_sides]
        self_first, self_second = order.run(lay, *self_sides, *self_others)
    else:
        fold_count = 0
        self_whole, cross_whole = links.gather(self_shard), links.gather(cross_shard)
        self_first, self_second = self_whole[:, :split], self_whole[:, split:]
        cross_held, cross_at = cross_whole, 0
        feed_input_low = links.gather(feed_shard)
        feed_output_low = links.gather(feed_output.astype(low))

    self_value, self_output_low = self_second[:, :width], self_second[:, width : 2 * width]
    norm_rows = self_second[:, 2 * width : 2 * width + 8].astype(jnp.float32).T
    gain_table, bias_table = norm_rows[:4], norm_rows[4:]

    def self_projections(layer_input, self_first, self_value, gain_row, bias_row):
        normed_self = layer_norm(layer_input, gain_row, bias_row).astype(low)
        return (
            normed_self,
            product(normed_self, self_first).astype(low),
            product(normed_self, self_value).astype(low),
        )

    normed_self, query_key, self_values = order.run(
        self_projections, layer_input, self_first, self_value, gain_table[0], bias_table[0]
    )
    self_mixed, self_totals = order.run(
        lambda query_key, self_values: attention_forward(
            unit_lengths, query_key, 0, query_key, width // LANES, self_values, 0, True
        ),
        query_key,
        self_values,
    )
    after_self, normed_cross = order.run(
        lambda self_mixed, self_output_low, gain_row, bias_row: (
            lambda after_self: (after_self, layer_norm(after_self, gain_row, bias_row).astype(low))
        )(layer_input + product(self_mixed, self_output_low)),
        self_mixed,
        self_output_low,
        gain_table[1],
        bias_table[1],
    )
    cross_first, cross_second = cross_whole[:, :split], cross_whole[:, split:]
    cross_query, cross_output_low = cross_second[:, :width], cross_second[:, width:]
    cross_queries = product(normed_cross, cross_query).astype(low)
    cross_kv = product(encoded, cross_first).astype(low)
    cross_mixed, cross_totals = attention_forward(
        text_lengths, cross_queries, 0, cross_kv, 0, cross_kv, width // LANES, False
    )
    after_cross = after_self + product(cross_mixed, cross_output_low)
    normed_feed = layer_norm(after_cross, gain_table[2], bias_table[2]).astype(low)
    hidden, slope, block_output, grad_after_feed, feed_branch, sums_3 = feed_forward(
        fold_count,
        unit_lengths,
        normed_feed,
        feed_input_low,
        feed_output_low,
        after_cross,
        cotangent[0],
        norm_rows,
    )

    positions = links.positions()
    in_send, in_keep, down_send, down_keep, grad_after_cross, cross_branch, sums_2 = order.run(
        lambda *arrays: feed_backward(fold_count, links.tiles(), positions, *arrays),
        feed_branch,
        normed_feed,
        hidden,
        slope,
        feed_input_low,
        feed_output_low,
        after_cross,
        grad_after_feed,
        norm_rows,
    )
    if links.pairwise:
        in_other, down_other = links.swap_core(in_send), links.swap_core(down_send)

    crossed, straight = links.positions(True), links.positions(False)
    grad_cross_mixed, cross_out = order.run(
        lambda branch, weights, mixed: (
            times_transposed(branch, weights).astype(low),
            weight_gradient(crossed, mixed, ([branch], False)),
        ),
        cross_branch,
        cross_output_low,
        cross_mixed,
    )
    if links.pairwise:
        feed_sum = order.run(
            lambda *arrays: links.sum_cores(
                jnp.concatenate(arrays[:2], axis=1), jnp.concatenate(arrays[2:], axis=1)
            ),
            in_keep,
            down_keep,
            in_other,
            down_other,
        )
        feed_chips = links.sum_chips(feed_sum)
    else:
        feed_in_part = links.scatter_whole(in_send, in_keep)
        feed_out_part = links.scatter_whole(down_send, down_keep)

    def cross_middle(cross_queries, cross_kv, cross_mixed, grad_cross_mixed, cross_totals):
        grad_q, grad_k, grad_v = attention_backward(
            text_lengths,
            cross_queries,
            0,
            cross_kv,
            0,
            cross_kv,
            width // LANES,
            cross_mixed,
            grad_cross_mixed,
            cross_totals,
            False,
        )
        return (
            grad_q,
            grad_k,
            grad_v,
            weight_gradient(crossed, normed_cross, ([grad_q], False)),
            weight_gradient(straight, encoded, ([grad_k, grad_v], False)),
        )

    grad_q, grad_k, grad_v, cross_query_grad, cross_kv_grad = order.run(
        cross_middle, cross_queries, cross_kv, cross_mixed, grad_cross_mixed, cross_totals
    )
    cross_send, cross_keep = [
        [kv, jnp.concatenate([query, out], axis=1)]
        for kv, query, out in zip(cross_kv_grad, cross_query_grad, cross_out)
    ]
    if links.pairwise:
        cross_sides = list(zip(cross_keep, [links.swap_core(side) for side in cross_send]))

        def exchange(sides, ats, flips):
            halves = order.run(
                lambda *arrays: [links.first_pair(*arrays[i : i + 2]) for i in range(0, len(arrays), 2)],
                *[array for side in sides for array in side],
            )
            return [
                (stays, links.swap(goes, links.bit(at, flip)))
                for (goes, stays), at, flip in zip(halves, ats, flips)
            ]

        def finish(sides):
            arrays = [array for side in sides for array in side]
            return links.send_fsdp(
                order.run(
                    lambda *arrays: jnp.concatenate(
                        [links.sum_cores(*arrays[i : i + 2]) for i in range(0, len(arrays), 2)], axis=1
                    ),
                    *arrays,
                )
            )

    grad_after_self, self_branch, sums_1 = order.run(
        lambda grad_q, held, *arrays: input_gradient(1, [grad_q], [(held, cross_at + split)], *arrays, True),
        grad_q,
        cross_held,
        after_self,
        grad_after_cross,
        norm_rows,
    )
    if links.pairwise:
        cross_sides = exchange(cross_sides, [0, 0], flips)
    else:
        cross_part = links.scatter_whole(*[jnp.concatenate(side, axis=1) for side in (cross_send, cross_keep)])
    grad_k_cross, grad_v_cross = grad_k, grad_v

    grad_self_mixed, self_out = order.run(
        lambda branch, weights, mixed: (
            times_transposed(branch, weights).astype(low),
            weight_gradient(crossed, mixed, ([branch], False)),
        ),
        self_branch,
        self_output_low,
        self_mixed,
    )
    grad_q, grad_k, grad_v = order.run(
        lambda query_key, self_values, self_mixed, grad_self_mixed, self_totals: attention_backward(
            unit_lengths,
            query_key,
            0,
            query_key,
            width // LANES,
            self_values,
            0,
            self_mixed,
            grad_self_mixed,
            self_totals,
            True,
        ),
        query_key,
        self_values,
        self_mixed,
        grad_self_mixed,
        self_totals,
    )
    if links.pairwise:
        cross_sides = exchange(cross_sides, [1, 1], flips)
        feed_part = lax.psum_scatter(order.after(feed_chips), "fsdp", scatter_dimension=0, tiled=True)
    first_send, first_keep, second_send, second_keep = order.run(
        lambda normed, grad_q, grad_k, grad_v: weight_gradient(
            straight, normed, ([grad_q, grad_k], False), ([grad_v], links.pairwise)
        ),
        normed_self,
        grad_q,
        grad_k,
        grad_v,
    )
    second_send, second_keep = [
        jnp.concatenate(pair, axis=1) for pair in zip((second_send, second_keep), self_out)
    ]
    if links.pairwise:
        self_sides = [(first_keep, links.swap_core(first_send)), (second_keep, links.swap_core(second_send))]
        self_sides = exchange(self_sides, [0, 0], flips)
        cross_parts = finish(cross_sides)

    grad_states, sums_0 = order.run(
        lambda grad_q, grad_k, grad_v, first, value, *arrays: input_gradient(
            0, [grad_q, grad_k, grad_v], [(first, 0), (first, width), (value, 0)], *arrays, False
        ),
        grad_q,
        grad_k,
        grad_v,
        self_first,
        self_second,
        unit_states[0],
        grad_after_self,
        norm_rows,
    )
    sums = [sums_0, sums_1, sums_2, sums_3]
    grad_tables = jnp.stack([part[0] for part in sums] + [part[1] for part in sums])
    grad_tables = jnp.pad(grad_tables.T, ((0, 0), (0, LANES - 8))).astype(low)
    table_send, table_keep = links.halves(grad_tables, False)
    grad_encoded = times_transposed(jnp.concatenate([grad_k_cross, grad_v_cross], axis=1), cross_first)
    if links.pairwise:
        self_sides = exchange(self_sides, [1, 1], flips)
        table_other = links.swap_core(table_send)
        cross_part = order.run(links.sum_fsdp, cross_parts)
        table_goes, table_stays = order.run(links.first_pair, table_keep, table_other)
        table_side = (table_stays, links.swap(table_goes, links.bit(0, False)))
        feed_part = order.run(lambda part: part.astype(jnp.float32), feed_part)
        self_parts = finish(self_sides)
        table_goes, table_stays = order.run(links.first_pair, *table_side)
        table_side = (table_stays, links.swap(table_goes, links.bit(1, False)))
        table_part = links.sum_all_fsdp(links.sum_cores(*table_side))
        self_part = links.sum_fsdp(self_parts)
        feed_in_part, feed_out_part = feed_part[:, : 4 * width], feed_part[:, 4 * width :]
        feed_out_part = jnp.concatenate(
            [feed_out_part[:, at * width : (at + 1) * width] for at in range(4)], axis=0
        )
    else:
        self_part = jnp.concatenate(
            [links.scatter_whole(first_send, first_keep), links.scatter_whole(second_send, second_keep)], axis=1
        )
        table_part = links.scatter_whole(table_send, table_keep)
    self_in_part, self_out_part = self_part[:, : 3 * width], self_part[:, 3 * width :]
    cross_in_part = jnp.concatenate([cross_part[:, split : 3 * width], cross_part[:, :split]], axis=1)
    cross_out_part = cross_part[:, 3 * width :]

    return (
        block_output[None],
        grad_states[None],
        grad_encoded[None],
        self_in_part,
        self_out_part,
        cross_in_part,
        cross_out_part,
        feed_in_part,
        feed_out_part,
        table_part[:, :4].T,
        table_part[:, 4:8].T,
    )


def solution(mesh):
    dp_count, fsdp_count = mesh.shape["dp"], mesh.shape["fsdp"]
    split = Mesh(mesh.devices.reshape(dp_count // 2, 2, fsdp_count), BOTH)
    return jax.shard_map(
        body,
        mesh=split,
        in_specs=(
            P(BOTH, None, None),
            P(BOTH, None, None),
            P(BOTH, None, None),
            P(BOTH),
            P(BOTH),
            P(BOTH, None),
            P(BOTH, None),
            P(BOTH, None),
            P(BOTH, None),
            P(BOTH, None),
            P(BOTH, None),
            P(None, BOTH),
            P(None, BOTH),
        ),
        out_specs=(
            P(BOTH, None, None),
            P(BOTH, None, None),
            P(BOTH, None, None),
            P(BOTH, None),
            P(BOTH, None),
            P(BOTH, None),
            P(BOTH, None),
            P(BOTH, None),
            P(BOTH, None),
            P(None, BOTH),
            P(None, BOTH),
        ),
        check_vma=False,
    )
```

```python
import functools

import jax
import jax.numpy as jnp
from jax import lax
from jax.experimental import pallas as pl
from jax.experimental.pallas import tpu as pltpu
from jax.sharding import Mesh
from jax.sharding import PartitionSpec as P

HEAD = 64
LANES = 128
AHEAD = 1
BOTH = ("h", "c", "fsdp")
VMEM_BYTES = 60 * 1024 * 1024
SHORT = pl.CostEstimate(flops=1024, transcendentals=0, bytes_accessed=1024)


def product(left, right):
    return jnp.dot(left, right, preferred_element_type=jnp.float32)


def contract_rows(left, right):
    return lax.dot_general(
        left, right, (((0,), (0,)), ((), ())), preferred_element_type=jnp.float32
    )


def times_transposed(left, right):
    return lax.dot_general(
        left, right, (((1,), (1,)), ((), ())), preferred_element_type=jnp.float32
    )


def layer_norm(values, gain_row, bias_row):
    centre = values - jnp.mean(values, axis=-1, keepdims=True)
    spread = jnp.mean(centre * centre, axis=-1, keepdims=True)
    return centre * lax.rsqrt(spread + 1e-05) * gain_row + bias_row


def row_blocks(row_count, step):
    step = step if row_count % step == 0 else row_count
    return [slice(start, start + step) for start in range(0, row_count, step)]


def norm_backward_rows(norm, values_ref, grad_of, base_ref, rows_ref, grad_ref, low_ref, sums_ref, normed_ref=None):
    gain, bias = rows_ref[norm : norm + 1, :], rows_ref[4 + norm : 5 + norm, :]
    gain_sum, bias_sum = jnp.zeros_like(gain), jnp.zeros_like(gain)
    for rows in row_blocks(values_ref.shape[0], LANES):
        values = values_ref[rows, :].astype(jnp.float32)
        grad = grad_of(rows)
        centre = values - jnp.mean(values, axis=-1, keepdims=True)
        rate = lax.rsqrt(jnp.mean(centre * centre, axis=-1, keepdims=True) + 1e-05)
        normed = centre * rate
        if normed_ref is not None:
            normed_ref[rows, :] = (normed * gain + bias).astype(normed_ref.dtype)
        scaled = grad * gain
        total = rate * (
            scaled
            - jnp.mean(scaled, axis=-1, keepdims=True)
            - normed * jnp.mean(scaled * normed, axis=-1, keepdims=True)
        )
        if base_ref is not None:
            total = base_ref[rows, :] + total
        grad_ref[rows, :] = total
        if low_ref is not None:
            low_ref[rows, :] = total.astype(jnp.bfloat16)
        gain_sum += jnp.sum(grad * normed, axis=0, keepdims=True)
        bias_sum += jnp.sum(grad, axis=0, keepdims=True)
    sums_ref[0:1, :] = gain_sum
    sums_ref[1:2, :] = bias_sum


def with_bias_lane(matrix, head, bias):
    lane = lax.broadcasted_iota(jnp.int32, matrix.shape, 1)
    own = (lane >= head * HEAD) & (lane < (head + 1) * HEAD)
    rest = jnp.where(lane == (1 - head) * HEAD, bias, 0.0).astype(matrix.dtype)
    return jnp.where(own, matrix, rest)


def key_bias(key_count, key_limit):
    row = lax.broadcasted_iota(jnp.int32, (key_count, LANES), 0)
    return jnp.where(row < key_limit, 0.0, -1e30)


def masked_scores(keys, queries, diagonal_ref):
    scores = times_transposed(keys, queries)
    if diagonal_ref is None:
        return scores
    below = scores.shape[0] - scores.shape[1]
    diagonal = scores[below:, :] + diagonal_ref[...]
    return jnp.concatenate([scores[:below, :], diagonal], axis=0) if below else diagonal


def set_diagonal(diagonal_ref):
    @pl.when(pl.program_id(0) == 0)
    def _():
        row = lax.broadcasted_iota(jnp.int32, diagonal_ref.shape, 0)
        column = lax.broadcasted_iota(jnp.int32, diagonal_ref.shape, 1)
        diagonal_ref[...] = jnp.where(row <= column, 0.0, -1e30)


def query_width(row_count, causal):
    return 256 if causal and row_count % 256 == 0 else row_count


def query_blocks(row_count, key_count, causal):
    width = query_width(row_count, causal)
    return [
        (start, width, start + width if causal else key_count)
        for start in range(0, row_count, width)
    ]


def head_lanes(head, shape):
    lane = lax.broadcasted_iota(jnp.int32, shape, 1)
    return (lane >= head * HEAD) & (lane < (head + 1) * HEAD)


def staggered(items, first, middle, last, ahead):
    begun = [first(item) for item in items[:ahead]]
    waiting = None
    for at, item in enumerate(items):
        if at + ahead < len(items):
            begun.append(first(items[at + ahead]))
        done = middle(item, begun[at])
        begun[at] = None
        if waiting is not None:
            last(*waiting)
        waiting = (item, done)
    last(*waiting)


def attention_forward_kernel(
    causal, limit_ref, q_ref, k_ref, v_ref, mixed_ref, total_ref, mixed_turned, diagonal_ref
):
    row_count, key_count = q_ref.shape[0], k_ref.shape[0]
    bias = key_bias(key_count, limit_ref[0])
    if causal:
        set_diagonal(diagonal_ref)
    else:
        diagonal_ref = None
    values_turned = v_ref[...].T
    ones = jnp.ones((16, key_count), jnp.bfloat16)
    scaled = q_ref[...] * jnp.bfloat16(HEAD**-0.5)
    queries = [with_bias_lane(scaled, head, 1.0) for head in range(2)]
    keys = [with_bias_lane(k_ref[...], head, bias) for head in range(2)]
    lanes = [slice(head * HEAD, (head + 1) * HEAD) for head in range(2)]
    values = [jnp.concatenate([values_turned[at, :], ones], axis=0) for at in lanes]

    def scores_of(item):
        head, (start, width, stop) = item
        return masked_scores(keys[head][:stop, :], queries[head][start : start + width, :], diagonal_ref)

    def expand(item, scores):
        highest = jnp.max(scores, axis=0, keepdims=True)
        return highest, jnp.exp(scores - highest).astype(jnp.bfloat16)

    def mix(item, done):
        head, (start, width, stop) = item
        highest, expanded = done
        mixed = product(values[head][:, :stop], expanded)
        total = mixed[HEAD : HEAD + 1, :]
        mixed_turned[lanes[head], start : start + width] = mixed[:HEAD, :] / total
        total_ref[0, head : head + 1, start : start + width] = highest + jnp.log(total)

    items = [(head, block) for block in query_blocks(row_count, key_count, causal) for head in range(2)]
    staggered(items, scores_of, expand, mix, 2)
    mixed_ref[...] = mixed_turned[...].T.astype(jnp.bfloat16)


def attention_forward(limit, queries, q_at, keys, k_at, values, v_at, causal):
    row_count, key_count = queries.shape[0], keys.shape[0]
    width = 1024
    pairs = width // LANES
    return pl.pallas_call(
        functools.partial(attention_forward_kernel, causal),
        grid_spec=pltpu.PrefetchScalarGridSpec(
            num_scalar_prefetch=1,
            grid=(pairs,),
            in_specs=[
                pl.BlockSpec((row_count, LANES), lambda p, s: (0, q_at + p)),
                pl.BlockSpec((key_count, LANES), lambda p, s: (0, k_at + p)),
                pl.BlockSpec((key_count, LANES), lambda p, s: (0, v_at + p)),
            ],
            out_specs=[
                pl.BlockSpec((row_count, LANES), lambda p, s: (0, p)),
                pl.BlockSpec((1, 2, row_count), lambda p, s: (p, 0, 0)),
            ],
            scratch_shapes=[
                pltpu.VMEM((LANES, row_count), jnp.float32),
                pltpu.VMEM((query_width(row_count, causal),) * 2, jnp.float32),
            ],
        ),
        out_shape=[
            jax.ShapeDtypeStruct((row_count, width), jnp.bfloat16),
            jax.ShapeDtypeStruct((pairs, 2, row_count), jnp.float32),
        ],
        compiler_params=pltpu.CompilerParams(vmem_limit_bytes=VMEM_BYTES),
        cost_estimate=SHORT,
        name="attention_forward",
    )(limit, queries, keys, values)


def attention_backward_kernel(
    causal,
    limit_ref,
    q_ref,
    k_ref,
    v_ref,
    mixed_ref,
    grad_ref,
    total_ref,
    grad_q_ref,
    grad_k_ref,
    grad_v_ref,
    grad_q_turned,
    grad_k_sum,
    grad_v_sum,
    diagonal_ref,
):
    row_count, key_count = q_ref.shape[0], k_ref.shape[0]
    bias = key_bias(key_count, limit_ref[0])
    if causal:
        set_diagonal(diagonal_ref)
    else:
        diagonal_ref = None
    keys_turned = k_ref[...].T
    scaled = q_ref[...] * jnp.bfloat16(HEAD**-0.5)
    grad = grad_ref[...]
    inner_turned = (grad.astype(jnp.float32) * mixed_ref[...].astype(jnp.float32)).T
    grad_k_sum[...] = jnp.zeros_like(grad_k_sum)
    grad_v_sum[...] = jnp.zeros_like(grad_v_sum)
    masks = [head_lanes(head, scaled.shape) for head in range(2)]
    queries = [jnp.where(mask, scaled, jnp.zeros_like(scaled)) for mask in masks]
    grads = [jnp.where(mask, grad, jnp.zeros_like(grad)) for mask in masks]
    biased = [with_bias_lane(scaled, head, 1.0) for head in range(2)]
    keys = [with_bias_lane(k_ref[...], head, bias) for head in range(2)]
    lanes = [slice(head * HEAD, (head + 1) * HEAD) for head in range(2)]
    inner = [jnp.sum(inner_turned[at, :], axis=0, keepdims=True) for at in lanes]

    def scores_of(item):
        head, (start, width, stop) = item
        columns = slice(start, start + width)
        scores = masked_scores(keys[head][:stop, :], biased[head][columns, :], diagonal_ref)
        return scores, times_transposed(v_ref[:stop, :], grads[head][columns, :])

    def differentiate(item, begun):
        head, (start, width, stop) = item
        columns = slice(start, start + width)
        scores, grad_probs = begun
        probs = jnp.exp(scores - total_ref[0, head : head + 1, columns])
        grad_scores = probs * (grad_probs - inner[head][:, columns])
        return probs.astype(jnp.bfloat16), grad_scores.astype(jnp.bfloat16)

    def add(item, done):
        head, (start, width, stop) = item
        columns = slice(start, start + width)
        probs, grad_scores = done
        grad_v_sum[:stop, :] += product(probs, grads[head][columns, :])
        grad_k_sum[:stop, :] += product(grad_scores, queries[head][columns, :])
        grad_q_turned[lanes[head], columns] = product(keys_turned[lanes[head], :stop], grad_scores)

    items = [(head, block) for block in query_blocks(row_count, key_count, causal) for head in range(2)]
    staggered(items, scores_of, differentiate, add, AHEAD)
    grad_q_ref[...] = (grad_q_turned[...].T * HEAD**-0.5).astype(jnp.bfloat16)
    grad_k_ref[...] = grad_k_sum[...].astype(jnp.bfloat16)
    grad_v_ref[...] = grad_v_sum[...].astype(jnp.bfloat16)


def attention_backward(limit, queries, q_at, keys, k_at, values, v_at, mixed, grad_mixed, totals, causal):
    row_count, key_count = queries.shape[0], keys.shape[0]
    width = 1024
    pairs = width // LANES
    row_block = pl.BlockSpec((row_count, LANES), lambda p, s: (0, p))
    key_block = pl.BlockSpec((key_count, LANES), lambda p, s: (0, p))
    return pl.pallas_call(
        functools.partial(attention_backward_kernel, causal),
        grid_spec=pltpu.PrefetchScalarGridSpec(
            num_scalar_prefetch=1,
            grid=(pairs,),
            in_specs=[
                pl.BlockSpec((row_count, LANES), lambda p, s: (0, q_at + p)),
                pl.BlockSpec((key_count, LANES), lambda p, s: (0, k_at + p)),
                pl.BlockSpec((key_count, LANES), lambda p, s: (0, v_at + p)),
                row_block,
                row_block,
                pl.BlockSpec((1, 2, row_count), lambda p, s: (p, 0, 0)),
            ],
            out_specs=[row_block, key_block, key_block],
            scratch_shapes=[
                pltpu.VMEM((LANES, row_count), jnp.float32),
                pltpu.VMEM((key_count, LANES), jnp.float32),
                pltpu.VMEM((key_count, LANES), jnp.float32),
                pltpu.VMEM((query_width(row_count, causal),) * 2, jnp.float32),
            ],
        ),
        out_shape=[
            jax.ShapeDtypeStruct((row_count, width), jnp.bfloat16),
            jax.ShapeDtypeStruct((key_count, width), jnp.bfloat16),
            jax.ShapeDtypeStruct((key_count, width), jnp.bfloat16),
        ],
        compiler_params=pltpu.CompilerParams(vmem_limit_bytes=VMEM_BYTES),
        cost_estimate=SHORT,
        name="attention_backward",
    )(limit, queries, keys, values, mixed, grad_mixed, totals)


def gelu_and_slope(values):
    normal_cdf = 0.5 + 0.5 * lax.erf(values * 2.0 ** (-0.5))
    bell = jnp.exp(-0.5 * values * values) * (2.0 * jnp.pi) ** (-0.5)
    return values * normal_cdf, normal_cdf + values * bell


def unfold_rows(folded_ref, unfolded, rows):
    width = unfolded.shape[1]
    folds = folded_ref.shape[1] // width
    for shard in range(folded_ref.shape[0] // rows):
        for fold in range(folds):
            start = (shard * folds + fold) * rows
            unfolded[start : start + rows, :] = folded_ref[
                shard * rows : (shard + 1) * rows, fold * width : (fold + 1) * width
            ]


def fold_rows(unfolded, folded_ref, rows):
    width = unfolded.shape[1]
    folds = folded_ref.shape[1] // width
    for shard in range(folded_ref.shape[0] // rows):
        for fold in range(folds):
            start = (shard * folds + fold) * rows
            folded_ref[shard * rows : (shard + 1) * rows, fold * width : (fold + 1) * width] = unfolded[
                start : start + rows, :
            ]


def feed_forward_kernel(
    rows,
    limit_ref,
    normed_ref,
    input_ref,
    output_ref,
    base_ref,
    cotangent_ref,
    rows_ref,
    hidden_ref,
    slope_ref,
    block_ref,
    grad_ref,
    low_ref,
    sums_ref,
    after_ref,
    unfolded,
):
    if rows:
        unfold_rows(output_ref, unfolded, rows)
        output_ref = unfolded

    @pl.when(pl.program_id(0) == 0)
    def _():
        after_ref[...] = base_ref[...]

    row_count = normed_ref.shape[0]
    step = 256 if row_count % 256 == 0 else row_count
    blocks = [slice(start, start + step) for start in range(0, row_count, step)]
    hidden_pre = product(normed_ref[blocks[0], :], input_ref[...])
    ready = None
    for at, rows_at in enumerate(blocks):
        following = product(normed_ref[blocks[at + 1], :], input_ref[...]) if at + 1 < len(blocks) else None
        hidden, slope = gelu_and_slope(hidden_pre)
        hidden = hidden.astype(jnp.bfloat16)
        hidden_ref[rows_at, :] = hidden
        slope_ref[rows_at, :] = slope.astype(jnp.bfloat16)
        if ready is not None:
            after_ref[blocks[at - 1], :] += product(ready, output_ref[...])
        hidden_pre, ready = following, hidden
    after_ref[blocks[-1], :] += product(ready, output_ref[...])

    @pl.when(pl.program_id(0) == pl.num_programs(0) - 1)
    def _():
        def live_grad(rows_at):
            shape = (rows_at.stop - rows_at.start, after_ref.shape[1])
            row = rows_at.start + lax.broadcasted_iota(jnp.int32, shape, 0)
            return jnp.where(row < limit_ref[0], cotangent_ref[rows_at, :], 0.0)

        norm_backward_rows(3, after_ref, live_grad, None, rows_ref, grad_ref, low_ref, sums_ref, block_ref)


FEED_TILE = 512


def feed_weight_specs(folds, width, tile, index):
    first = pl.BlockSpec((width, tile), lambda *at: (0, index(*at)))
    if folds:
        return first, pl.BlockSpec((tile // folds, folds * width), lambda *at: (index(*at), 1))
    return first, pl.BlockSpec((tile, width), lambda *at: (index(*at), 0))


def feed_forward(rows, limit, normed, input_low, output_low, after_cross, cotangent, norm_rows):
    row_count, width = normed.shape
    hidden_width = 4 * width
    tile = FEED_TILE
    whole = pl.BlockSpec((row_count, width), lambda j, s: (0, 0))
    tall = pl.BlockSpec((row_count, tile), lambda j, s: (0, j))
    weight_specs = feed_weight_specs(hidden_width // width if rows else 0, width, tile, lambda j, s: j)
    return pl.pallas_call(
        functools.partial(feed_forward_kernel, rows),
        grid_spec=pltpu.PrefetchScalarGridSpec(
            num_scalar_prefetch=1,
            grid=(hidden_width // tile,),
            in_specs=[whole, *weight_specs, whole, whole, pl.BlockSpec((8, width), lambda j, s: (0, 0))],
            out_specs=[tall, tall, whole, whole, whole, pl.BlockSpec((2, width), lambda j, s: (0, 0))],
            scratch_shapes=[pltpu.VMEM((row_count, width), jnp.float32), pltpu.VMEM((tile, width), jnp.bfloat16)],
        ),
        out_shape=[
            jax.ShapeDtypeStruct((row_count, hidden_width), jnp.bfloat16),
            jax.ShapeDtypeStruct((row_count, hidden_width), jnp.bfloat16),
            jax.ShapeDtypeStruct((row_count, width), jnp.bfloat16),
            jax.ShapeDtypeStruct((row_count, width), jnp.float32),
            jax.ShapeDtypeStruct((row_count, width), jnp.bfloat16),
            jax.ShapeDtypeStruct((2, width), jnp.float32),
        ],
        compiler_params=pltpu.CompilerParams(vmem_limit_bytes=VMEM_BYTES),
        cost_estimate=SHORT,
        name="feed_forward",
    )(limit, normed, input_low, output_low, after_cross, cotangent, norm_rows)


def turn_rows(x_ref, turned, positions_ref):
    for j in range(turned.shape[0] // LANES):
        start = pl.multiple_of(positions_ref[j] * LANES, LANES)
        block = slice(j * LANES, (j + 1) * LANES)
        turned[pl.ds(start, LANES), :] = x_ref[block, :] if x_ref.shape == turned.shape else x_ref[:, block].T


def feed_backward_kernel(
    rows,
    tiles_ref,
    positions_ref,
    grad_ref,
    normed_ref,
    hidden_ref,
    slope_ref,
    input_ref,
    output_ref,
    values_ref,
    base_ref,
    rows_ref,
    in_send_ref,
    in_keep_ref,
    out_send_ref,
    out_keep_ref,
    total_ref,
    low_ref,
    sums_ref,
    grad_normed_ref,
    turned,
    unfolded,
):
    step = pl.program_id(0)
    if rows:
        unfold_rows(output_ref, unfolded, rows)
        output_ref = unfolded

    @pl.when(step == 0)
    def _():
        grad_normed_ref[...] = jnp.zeros_like(grad_normed_ref)
        turn_rows(normed_ref, turned, positions_ref)

    grad_hidden = times_transposed(grad_ref[...], output_ref[...])
    grad_pre = (grad_hidden * slope_ref[...].astype(jnp.float32)).astype(jnp.bfloat16)
    grad_out = contract_rows(hidden_ref[...], grad_ref[...]).astype(jnp.bfloat16)
    for out_ref, first in ((out_send_ref, True), (out_keep_ref, False)):

        @pl.when((step < pl.num_programs(0) // 2) == first)
        def _(out_ref=out_ref):
            if rows:
                fold_rows(grad_out, out_ref, rows)
            else:
                out_ref[...] = grad_out

    half = turned.shape[0] // 2
    in_send_ref[...] = product(turned[:half, :], grad_pre).astype(jnp.bfloat16)
    in_keep_ref[...] = product(turned[half:, :], grad_pre).astype(jnp.bfloat16)
    grad_normed_ref[...] += times_transposed(grad_pre, input_ref[...])

    @pl.when(step == pl.num_programs(0) - 1)
    def _():
        norm_backward_rows(
            2,
            values_ref,
            lambda rows_at: grad_normed_ref[rows_at, :],
            base_ref,
            rows_ref,
            total_ref,
            low_ref,
            sums_ref,
        )


def feed_backward(
    rows, tiles, positions, grad_branch, normed, hidden, slope, input_low, output_low, after_cross, grad_after, norm_rows
):
    row_count, width = grad_branch.shape
    hidden_width = hidden.shape[1]
    count = tiles.shape[0]
    half = count // 2
    tile = hidden_width // count
    whole = pl.BlockSpec((row_count, width), lambda j, t, p: (0, 0))
    tall = pl.BlockSpec((row_count, tile), lambda j, t, p: (0, t[j]))
    in_half = pl.BlockSpec((width // 2, tile), lambda j, t, p: (0, t[j]))
    folds = hidden_width // width if rows else 1
    weight_specs = feed_weight_specs(folds if rows else 0, width, tile, lambda j, t, p: t[j])
    return pl.pallas_call(
        functools.partial(feed_backward_kernel, rows),
        grid_spec=pltpu.PrefetchScalarGridSpec(
            num_scalar_prefetch=2,
            grid=(count,),
            in_specs=[
                whole,
                whole,
                tall,
                tall,
                *weight_specs,
                whole,
                whole,
                pl.BlockSpec((8, width), lambda j, t, p: (0, 0)),
            ],
            out_specs=[
                in_half,
                in_half,
                pl.BlockSpec((tile // folds, folds * width), lambda j, t, p: (jnp.minimum(j, half - 1), 0)),
                pl.BlockSpec((tile // folds, folds * width), lambda j, t, p: (jnp.maximum(j - half, 0), 0)),
                whole,
                whole,
                pl.BlockSpec((2, width), lambda j, t, p: (0, 0)),
            ],
            scratch_shapes=[
                pltpu.VMEM((row_count, width), jnp.float32),
                pltpu.VMEM((width, row_count), jnp.bfloat16),
                pltpu.VMEM((tile, width), jnp.bfloat16),
            ],
        ),
        out_shape=[
            jax.ShapeDtypeStruct((width // 2, hidden_width), jnp.bfloat16),
            jax.ShapeDtypeStruct((width // 2, hidden_width), jnp.bfloat16),
            jax.ShapeDtypeStruct((hidden_width // folds // 2, folds * width), jnp.bfloat16),
            jax.ShapeDtypeStruct((hidden_width // folds // 2, folds * width), jnp.bfloat16),
            jax.ShapeDtypeStruct((row_count, width), jnp.float32),
            jax.ShapeDtypeStruct((row_count, width), jnp.bfloat16),
            jax.ShapeDtypeStruct((2, width), jnp.float32),
        ],
        compiler_params=pltpu.CompilerParams(vmem_limit_bytes=VMEM_BYTES),
        cost_estimate=SHORT,
        name="feed_backward",
    )(
        tiles, positions, grad_branch, normed, hidden, slope, input_low, output_low, after_cross, grad_after, norm_rows
    )


WEIGHT_TILE = 512


def tile_starts(arrays):
    starts = [0]
    for array in arrays:
        starts.append(starts[-1] + array.shape[1] // WEIGHT_TILE)
    return starts


def tile_spec(rows, first, last, offset=0):
    return pl.BlockSpec(
        (rows, WEIGHT_TILE), lambda j, *_: (0, offset + jnp.clip(j - first, 0, last - first - 1))
    )


def weight_gradient_kernel(starts, groups, crossed, positions_ref, x_ref, *refs):
    grads, outs, turned = refs[: len(starts) - 1], refs[len(starts) - 1 : -1], refs[-1]
    step = pl.program_id(0)

    @pl.when(step == 0)
    def _():
        turn_rows(x_ref, turned, positions_ref)

    half = turned.shape[0] // 2
    for index, grad_ref in enumerate(grads):
        group = groups[index]

        @pl.when((step >= starts[index]) & (step < starts[index + 1]))
        def _(grad_ref=grad_ref, group=group):
            for out_ref, rows in ((outs[2 * group], slice(0, half)), (outs[2 * group + 1], slice(half, 2 * half))):
                result = product(turned[rows, :], grad_ref[...]).astype(jnp.bfloat16)
                if crossed[group]:
                    for block, place in enumerate((0, 2, 1, 3)):
                        out_ref[place * LANES : (place + 1) * LANES, :] = result[
                            block * LANES : (block + 1) * LANES, :
                        ]
                else:
                    out_ref[...] = result


def weight_gradient(positions, x, *groups):
    grads = [grad for group, _ in groups for grad in group]
    row_count = grads[0].shape[0]
    width = x.size // row_count
    group_of = [index for index, (group, _) in enumerate(groups) for _ in group]
    starts = tile_starts(grads)
    half = width // 2
    out_specs, out_shape = [], []
    for index in range(len(groups)):
        own = [at for at, group in enumerate(group_of) if group == index]
        first, last = starts[own[0]], starts[own[-1] + 1]
        out_specs += [tile_spec(half, first, last)] * 2
        out_shape += [jax.ShapeDtypeStruct((half, (last - first) * WEIGHT_TILE), jnp.bfloat16)] * 2
    return pl.pallas_call(
        functools.partial(weight_gradient_kernel, starts, group_of, [crossed for _, crossed in groups]),
        grid_spec=pltpu.PrefetchScalarGridSpec(
            num_scalar_prefetch=1,
            grid=(starts[-1],),
            in_specs=[pl.BlockSpec(x.shape, lambda j, p: (0, 0))]
            + [tile_spec(row_count, starts[i], starts[i + 1]) for i in range(len(grads))],
            out_specs=out_specs,
            scratch_shapes=[pltpu.VMEM((width, row_count), jnp.bfloat16)],
        ),
        out_shape=out_shape,
        compiler_params=pltpu.CompilerParams(vmem_limit_bytes=VMEM_BYTES),
        cost_estimate=SHORT,
        name="weight_gradient",
    )(positions, x, *grads)


def output_backward_kernel(positions_ref, x_ref, grad_ref, weight_ref, send_ref, keep_ref, mixed_ref, turned, summed):
    step = pl.program_id(0)

    @pl.when(step == 0)
    def _():
        turn_rows(x_ref, turned, positions_ref)
        summed[...] = jnp.zeros_like(summed)

    half = turned.shape[0] // 2
    summed[...] += times_transposed(grad_ref[...], weight_ref[...])
    send_ref[...] = product(turned[:half, :], grad_ref[...]).astype(jnp.bfloat16)
    keep_ref[...] = product(turned[half:, :], grad_ref[...]).astype(jnp.bfloat16)

    @pl.when(step == pl.num_programs(0) - 1)
    def _():
        mixed_ref[...] = summed[...].astype(jnp.bfloat16)


def output_backward(positions, x, grad, weights, column):
    row_count, width = grad.shape
    half = width // 2
    last = width // WEIGHT_TILE
    return pl.pallas_call(
        output_backward_kernel,
        grid_spec=pltpu.PrefetchScalarGridSpec(
            num_scalar_prefetch=1,
            grid=(last,),
            in_specs=[
                pl.BlockSpec(x.shape, lambda j, p: (0, 0)),
                tile_spec(row_count, 0, last),
                tile_spec(width, 0, last, offset=column // WEIGHT_TILE),
            ],
            out_specs=[
                tile_spec(half, 0, last),
                tile_spec(half, 0, last),
                pl.BlockSpec((row_count, width), lambda j, p: (0, 0)),
            ],
            scratch_shapes=[
                pltpu.VMEM((width, row_count), jnp.bfloat16),
                pltpu.VMEM((row_count, width), jnp.float32),
            ],
        ),
        out_shape=[jax.ShapeDtypeStruct((half, width), jnp.bfloat16)] * 2
        + [jax.ShapeDtypeStruct((row_count, width), jnp.bfloat16)],
        compiler_params=pltpu.CompilerParams(vmem_limit_bytes=VMEM_BYTES),
        cost_estimate=SHORT,
        name="output_backward",
    )(positions, x, grad, weights)


def weights_back_kernel(starts, *refs):
    count = len(starts) - 1
    grads, weights_ref, total_ref = refs[:count], refs[count], refs[-1]
    step = pl.program_id(0)

    @pl.when(step == 0)
    def _():
        total_ref[...] = jnp.zeros_like(total_ref)

    for index in range(count):

        @pl.when((step >= starts[index]) & (step < starts[index + 1]))
        def _(index=index):
            total_ref[...] += times_transposed(grads[index][...], weights_ref[...])


def weights_back(grads, weights, column):
    row_count, width = grads[0].shape[0], weights.shape[0]
    starts = tile_starts(grads)
    return pl.pallas_call(
        functools.partial(weights_back_kernel, starts),
        grid=(starts[-1],),
        in_specs=[tile_spec(row_count, starts[i], starts[i + 1]) for i in range(len(grads))]
        + [tile_spec(width, 0, starts[-1], offset=column // WEIGHT_TILE)],
        out_specs=pl.BlockSpec((row_count, width), lambda j: (0, 0)),
        out_shape=jax.ShapeDtypeStruct((row_count, width), jnp.float32),
        compiler_params=pltpu.CompilerParams(vmem_limit_bytes=VMEM_BYTES),
        cost_estimate=SHORT,
        name="weights_back",
    )(*grads, weights)


def input_gradient_kernel(norm, starts, has_low, *refs):
    count = len(starts) - 1
    grads, weights = refs[:count], refs[count : 2 * count]
    values_ref, base_ref, rows_ref, total_ref = refs[2 * count : 2 * count + 4]
    low_ref = refs[2 * count + 4] if has_low else None
    sums_ref, summed = refs[-2:]
    step = pl.program_id(0)

    @pl.when(step == 0)
    def _():
        summed[...] = jnp.zeros_like(summed)

    for index in range(count):

        @pl.when((step >= starts[index]) & (step < starts[index + 1]))
        def _(index=index):
            summed[...] += times_transposed(grads[index][...], weights[index][...])

    @pl.when(step == starts[-1] - 1)
    def _():
        norm_backward_rows(
            norm, values_ref, lambda rows: summed[rows, :], base_ref, rows_ref, total_ref, low_ref, sums_ref
        )


def input_gradient(norm, grads, weights, values, base, norm_rows, has_low):
    row_count, width = values.shape
    starts = tile_starts(grads)
    whole = pl.BlockSpec((row_count, width), lambda j: (0, 0))
    spans = [(starts[i], starts[i + 1]) for i in range(len(grads))]
    lows = [jax.ShapeDtypeStruct((row_count, width), jnp.bfloat16)] if has_low else []
    return pl.pallas_call(
        functools.partial(input_gradient_kernel, norm, starts, has_low),
        grid=(starts[-1],),
        in_specs=[tile_spec(row_count, *span) for span in spans]
        + [
            tile_spec(width, *span, offset=column // WEIGHT_TILE) for span, (_, column) in zip(spans, weights)
        ]
        + [whole, whole, pl.BlockSpec((8, width), lambda j: (0, 0))],
        out_specs=[whole] * (1 + len(lows)) + [pl.BlockSpec((2, width), lambda j: (0, 0))],
        out_shape=[jax.ShapeDtypeStruct((row_count, width), jnp.float32)]
        + lows
        + [jax.ShapeDtypeStruct((2, width), jnp.float32)],
        scratch_shapes=[pltpu.VMEM((row_count, width), jnp.float32)],
        compiler_params=pltpu.CompilerParams(vmem_limit_bytes=VMEM_BYTES),
        cost_estimate=SHORT,
        name="input_gradient",
    )(*grads, *[array for array, _ in weights], values, base, norm_rows)


class Order:
    def __init__(self):
        self.last = ()

    def after(self, *values):
        values, _ = lax.optimization_barrier((values, self.last))
        return values if len(values) > 1 else values[0]

    def run(self, work, *values):
        values, _ = lax.optimization_barrier((values, self.last))
        result = work(*values)
        self.last = result
        return result


def place_rows_kernel(counts, rows, table_ref, *refs):
    pieces, out_ref, held, sems_in, sems_out = refs[:-4], *refs[-4:]
    loads, stores = [], []
    for piece, count in zip(pieces, counts):
        for block in range(count):
            at = len(loads)
            start = pl.multiple_of(table_ref[at] * rows, rows)
            loads.append(
                pltpu.make_async_copy(piece.at[pl.ds(block * rows, rows), :], held.at[at], sems_in.at[at])
            )
            stores.append(
                pltpu.make_async_copy(held.at[at], out_ref.at[pl.ds(start, rows), :], sems_out.at[at])
            )
    for load in loads:
        load.start()
    for load, store in zip(loads, stores):
        load.wait()
        store.start()
    for store in stores:
        store.wait()


def place_rows(table, pieces, rows):
    counts = [piece.shape[0] // rows for piece in pieces]
    total, columns = sum(counts), pieces[0].shape[1]
    anywhere = pl.BlockSpec(memory_space=pl.ANY)
    return pl.pallas_call(
        functools.partial(place_rows_kernel, counts, rows),
        grid_spec=pltpu.PrefetchScalarGridSpec(
            num_scalar_prefetch=1,
            grid=(1,),
            in_specs=[anywhere] * len(pieces),
            out_specs=anywhere,
            scratch_shapes=[
                pltpu.VMEM((total, rows, columns), pieces[0].dtype),
                pltpu.SemaphoreType.DMA((total,)),
                pltpu.SemaphoreType.DMA((total,)),
            ],
        ),
        out_shape=jax.ShapeDtypeStruct((total * rows, columns), pieces[0].dtype),
        compiler_params=pltpu.CompilerParams(vmem_limit_bytes=VMEM_BYTES),
        cost_estimate=SHORT,
        name="place_rows",
    )(table, *pieces)


class Links:
    def __init__(self, width):
        self.h_count, self.fsdp_count = lax.axis_size("h"), lax.axis_size("fsdp")
        self.core, self.h, self.fsdp = lax.axis_index("c"), lax.axis_index("h"), lax.axis_index("fsdp")
        dp_count = 2 * self.h_count
        self.pairwise = (
            (self.h_count & (self.h_count - 1)) == 0
            and (self.fsdp_count & (self.fsdp_count - 1)) == 0
            and width == dp_count * LANES
        )
        self.blocks = width // LANES
        self.bits = [1 << b for b in range(self.h_count.bit_length() - 1)]
        self.fsdp_table = (self.fsdp ^ jnp.arange(self.fsdp_count, dtype=jnp.int32)).astype(jnp.int32)

    def order(self, flip):
        return self.bits[::-1] if flip else self.bits

    def swap(self, array, bit):
        return lax.ppermute(array, "h", [(i, i ^ bit) for i in range(self.h_count)])

    def swap_core(self, array):
        return lax.ppermute(array, "c", [(0, 1), (1, 0)])

    def swap_fsdp(self, array, bit):
        return lax.ppermute(array, "fsdp", [(i, i ^ bit) for i in range(self.fsdp_count)])

    def gather(self, shard):
        return lax.all_gather(shard, BOTH, axis=0, tiled=True)

    def spread_fsdp(self, shard):
        return [shard] + [self.swap_fsdp(shard, k) for k in range(1, self.fsdp_count)]

    def place_fsdp(self, parts):
        return place_rows(self.fsdp_table, parts, parts[0].shape[0])

    def spread(self, block, at, flip):
        return jnp.concatenate([block, self.swap(block, self.order(flip)[at])], axis=0)

    def place(self, block, other, flip):
        masks = [0]
        for bit in self.order(flip):
            masks = masks + [mask ^ bit for mask in masks]
        h = self.h ^ jnp.asarray(masks, dtype=jnp.int32)
        table = jnp.concatenate([2 * h + self.core, 2 * h + 1 - self.core]).astype(jnp.int32)
        return place_rows(table, [block, other], block.shape[0] // self.h_count)

    def tiles(self):
        if not self.pairwise:
            return jnp.arange(self.blocks, dtype=jnp.int32)
        h = 2 * jnp.arange(self.h_count, dtype=jnp.int32)
        return jnp.concatenate([h + 1 - self.core, h + self.core]).astype(jnp.int32)

    def positions(self, flip=None):
        block = jnp.arange(self.blocks, dtype=jnp.int32)
        if not self.pairwise:
            return block
        place, own = block >> 1, (block & 1) == self.core
        if flip is not None:
            mask, place = place ^ self.h, jnp.zeros_like(place)
            for at, bit in enumerate(self.order(flip)):
                place = place + jnp.where((mask & bit) == 0, 1 << at, 0)
        return (place + jnp.where(own, self.h_count, 0)).astype(jnp.int32)

    def halves(self, rows, flip):
        ordered = place_rows(self.positions(flip), [rows], rows.shape[0] // self.blocks)
        half = rows.shape[0] // 2
        return ordered[:half], ordered[half:]

    def sum_cores(self, keep, other):
        return (keep.astype(jnp.float32) + other.astype(jnp.float32)).astype(jnp.bfloat16)

    def send_fsdp(self, grad):
        return lax.all_to_all(grad, "fsdp", 0, 0, tiled=True)

    def sum_fsdp(self, parts):
        rows = parts.shape[0] // self.fsdp_count
        parts = parts.astype(jnp.float32)
        return sum(parts[k * rows : (k + 1) * rows] for k in range(self.fsdp_count))

    def scatter_whole(self, send, keep):
        grad = jnp.concatenate([send, keep], axis=0).astype(jnp.float32)
        part = lax.psum_scatter(grad, ("h", "c"), scatter_dimension=0, tiled=True)
        return lax.psum_scatter(part, "fsdp", scatter_dimension=0, tiled=True)

    def sum_chips(self, grad):
        return lax.psum_scatter(grad, "h", scatter_dimension=0, tiled=True)

    def first_pair(self, keep, other):
        half = keep.shape[0] // 2
        return self.sum_cores(keep[:half], other[:half]), self.sum_cores(keep[half:], other[half:])

    def bit(self, at, flip):
        return self.order(flip)[::-1][at]


def body(
    unit_states,
    encoder_states,
    cotangent,
    unit_lengths,
    text_lengths,
    self_project,
    self_output,
    cross_project,
    cross_output,
    feed_input,
    feed_output,
    norm_gains,
    norm_biases,
):
    low = jnp.bfloat16
    layer_input = unit_states[0].astype(jnp.float32)
    encoded = encoder_states[0]
    row_count, width = layer_input.shape
    links = Links(width)

    tables = jnp.concatenate([norm_gains, norm_biases], axis=0).T
    tables = jnp.pad(tables, ((0, 0), (0, LANES - tables.shape[1])))
    self_shard = jnp.concatenate([self_project.astype(low), self_output.astype(low), tables], axis=1)
    cross_shard = jnp.concatenate(
        [cross_project[:, width:].astype(low), cross_project[:, :width].astype(low), cross_output.astype(low)],
        axis=1,
    )
    feed_shard = feed_input.astype(low)
    order = Order()
    flips = [False, True]
    split = 2 * width
    if links.pairwise:
        fold_count = feed_input.shape[0]
        folded = [
            feed_output[at : at + fold_count].astype(low) for at in range(0, feed_output.shape[0], fold_count)
        ]
        feed_shard = jnp.concatenate([feed_shard] + folded, axis=1)
        bits = [links.order(flip) for flip in flips]

        def send(sides, at):
            return [links.swap(side, bit[at]) for side, bit in zip(sides, bits)]

        def join(*arrays):
            half = len(arrays) // 2
            return [jnp.concatenate(pair, axis=0) for pair in zip(arrays[:half], arrays[half:])]

        def lay(*arrays):
            half = len(arrays) // 2
            return [links.place(*pair, flip) for pair, flip in zip(zip(arrays[:half], arrays[half:]), flips)]

        def lay_fsdp(*parts):
            return links.place_fsdp(parts)

        gathered = links.gather(jnp.concatenate([feed_shard, cross_shard], axis=1))
        feed_input_low, feed_output_low, cross_whole = gathered, gathered, gathered[:, 8 * width :]
        cross_held, cross_at = gathered, 8 * width
        self_part = order.run(lay_fsdp, *links.spread_fsdp(self_shard))
        self_sides = [self_part[:, :split], self_part[:, split:]]
        self_swaps = send(self_sides, 0)
        self_sides = order.run(join, *self_sides, *self_swaps)
        self_swaps = send(self_sides, 1)
        self_sides = order.run(join, *self_sides, *self_swaps)
        self_others = [links.swap_core(side) for side in self_sides]
        self_first, self_second = order.run(lay, *self_sides, *self_others)
    else:
        fold_count = 0
        self_whole, cross_whole = links.gather(self_shard), links.gather(cross_shard)
        self_first, self_second = self_whole[:, :split], self_whole[:, split:]
        cross_held, cross_at = cross_whole, 0
        feed_input_low = links.gather(feed_shard)
        feed_output_low = links.gather(feed_output.astype(low))

    self_value, self_output_low = self_second[:, :width], self_second[:, width : 2 * width]
    norm_rows = self_second[:, 2 * width : 2 * width + 8].astype(jnp.float32).T
    gain_table, bias_table = norm_rows[:4], norm_rows[4:]

    def self_projections(layer_input, self_first, self_value, gain_row, bias_row):
        normed_self = layer_norm(layer_input, gain_row, bias_row).astype(low)
        return (
            normed_self,
            product(normed_self, self_first).astype(low),
            product(normed_self, self_value).astype(low),
        )

    normed_self, query_key, self_values = order.run(
        self_projections, layer_input, self_first, self_value, gain_table[0], bias_table[0]
    )
    self_mixed, self_totals = order.run(
        lambda query_key, self_values: attention_forward(
            unit_lengths, query_key, 0, query_key, width // LANES, self_values, 0, True
        ),
        query_key,
        self_values,
    )
    after_self, normed_cross = order.run(
        lambda self_mixed, self_output_low, gain_row, bias_row: (
            lambda after_self: (after_self, layer_norm(after_self, gain_row, bias_row).astype(low))
        )(layer_input + product(self_mixed, self_output_low)),
        self_mixed,
        self_output_low,
        gain_table[1],
        bias_table[1],
    )
    cross_first, cross_second = cross_whole[:, :split], cross_whole[:, split:]
    normed_self_turned, self_mixed_turned, encoded_turned = order.run(
        lambda *arrays: [array.T for array in arrays], normed_self, self_mixed, encoded
    )
    cross_query, cross_output_low = cross_second[:, :width], cross_second[:, width:]
    cross_queries = product(normed_cross, cross_query).astype(low)
    cross_kv = product(encoded, cross_first).astype(low)
    cross_mixed, cross_totals = attention_forward(
        text_lengths, cross_queries, 0, cross_kv, 0, cross_kv, width // LANES, False
    )
    after_cross = after_self + product(cross_mixed, cross_output_low)
    normed_feed = layer_norm(after_cross, gain_table[2], bias_table[2]).astype(low)
    hidden, slope, block_output, grad_after_feed, feed_branch, sums_3 = feed_forward(
        fold_count,
        unit_lengths,
        normed_feed,
        feed_input_low,
        feed_output_low,
        after_cross,
        cotangent[0],
        norm_rows,
    )

    positions = links.positions()
    in_send, in_keep, down_send, down_keep, grad_after_cross, cross_branch, sums_2 = order.run(
        lambda *arrays: feed_backward(fold_count, links.tiles(), positions, *arrays),
        feed_branch,
        normed_feed,
        hidden,
        slope,
        feed_input_low,
        feed_output_low,
        after_cross,
        grad_after_feed,
        norm_rows,
    )
    if links.pairwise:
        in_other, down_other = links.swap_core(in_send), links.swap_core(down_send)

    crossed, straight = links.positions(True), links.positions(False)
    *cross_out, grad_cross_mixed = order.run(
        lambda *arrays: output_backward(crossed, *arrays, cross_at + 3 * width), cross_mixed, cross_branch, cross_held
    )
    if links.pairwise:
        feed_sum = order.run(
            lambda *arrays: links.sum_cores(
                jnp.concatenate(arrays[:2], axis=1), jnp.concatenate(arrays[2:], axis=1)
            ),
            in_keep,
            down_keep,
            in_other,
            down_other,
        )
        feed_chips = links.sum_chips(feed_sum)
    else:
        feed_in_part = links.scatter_whole(in_send, in_keep)
        feed_out_part = links.scatter_whole(down_send, down_keep)

    def cross_middle(cross_queries, cross_kv, cross_mixed, grad_cross_mixed, cross_totals):
        grad_q, grad_k, grad_v = attention_backward(
            text_lengths,
            cross_queries,
            0,
            cross_kv,
            0,
            cross_kv,
            width // LANES,
            cross_mixed,
            grad_cross_mixed,
            cross_totals,
            False,
        )
        return (
            grad_q,
            grad_k,
            grad_v,
            weight_gradient(crossed, normed_cross, ([grad_q], False)),
            weight_gradient(straight, encoded_turned, ([grad_k, grad_v], False)),
        )

    grad_q, grad_k, grad_v, cross_query_grad, cross_kv_grad = order.run(
        cross_middle, cross_queries, cross_kv, cross_mixed, grad_cross_mixed, cross_totals
    )
    cross_send, cross_keep = [
        [kv, jnp.concatenate([query, out], axis=1)]
        for kv, query, out in zip(cross_kv_grad, cross_query_grad, cross_out)
    ]
    if links.pairwise:
        cross_sides = list(zip(cross_keep, [links.swap_core(side) for side in cross_send]))

        def exchange(sides, ats, flips):
            halves = order.run(
                lambda *arrays: [links.first_pair(*arrays[i : i + 2]) for i in range(0, len(arrays), 2)],
                *[array for side in sides for array in side],
            )
            return [
                (stays, links.swap(goes, links.bit(at, flip)))
                for (goes, stays), at, flip in zip(halves, ats, flips)
            ]

        def finish(sides):
            arrays = [array for side in sides for array in side]
            return links.send_fsdp(
                order.run(
                    lambda *arrays: jnp.concatenate(
                        [links.sum_cores(*arrays[i : i + 2]) for i in range(0, len(arrays), 2)], axis=1
                    ),
                    *arrays,
                )
            )

    grad_after_self, self_branch, sums_1 = order.run(
        lambda grad_q, held, *arrays: input_gradient(1, [grad_q], [(held, cross_at + split)], *arrays, True),
        grad_q,
        cross_held,
        after_self,
        grad_after_cross,
        norm_rows,
    )
    if links.pairwise:
        cross_sides = exchange(cross_sides, [0, 0], flips)
    else:
        cross_part = links.scatter_whole(*[jnp.concatenate(side, axis=1) for side in (cross_send, cross_keep)])
    grad_k_cross, grad_v_cross = grad_k, grad_v

    *self_out, grad_self_mixed = order.run(
        lambda *arrays: output_backward(crossed, *arrays, width), self_mixed_turned, self_branch, self_second
    )
    grad_q, grad_k, grad_v = order.run(
        lambda query_key, self_values, self_mixed, grad_self_mixed, self_totals: attention_backward(
            unit_lengths,
            query_key,
            0,
            query_key,
            width // LANES,
            self_values,
            0,
            self_mixed,
            grad_self_mixed,
            self_totals,
            True,
        ),
        query_key,
        self_values,
        self_mixed,
        grad_self_mixed,
        self_totals,
    )
    if links.pairwise:
        cross_sides = exchange(cross_sides, [1, 1], flips)
    first_send, first_keep, second_send, second_keep = order.run(
        lambda normed, grad_q, grad_k, grad_v: weight_gradient(
            straight, normed, ([grad_q, grad_k], False), ([grad_v], links.pairwise)
        ),
        normed_self_turned,
        grad_q,
        grad_k,
        grad_v,
    )
    if links.pairwise:
        feed_part = lax.psum_scatter(order.after(feed_chips), "fsdp", scatter_dimension=0, tiled=True)
    second_send, second_keep = [
        jnp.concatenate(pair, axis=1) for pair in zip((second_send, second_keep), self_out)
    ]
    if links.pairwise:
        self_sides = [(first_keep, links.swap_core(first_send)), (second_keep, links.swap_core(second_send))]
        self_sides = exchange(self_sides, [0, 0], flips)

    grad_states, sums_0 = order.run(
        lambda grad_q, grad_k, grad_v, first, value, *arrays: input_gradient(
            0, [grad_q, grad_k, grad_v], [(first, 0), (first, width), (value, 0)], *arrays, False
        ),
        grad_q,
        grad_k,
        grad_v,
        self_first,
        self_second,
        unit_states[0],
        grad_after_self,
        norm_rows,
    )
    if links.pairwise:
        cross_parts = finish(cross_sides)
        self_sides = exchange(self_sides, [1, 1], flips)
        feed_part = order.run(lambda part: part.astype(jnp.float32), feed_part)

    def table_halves(*sums):
        tables = jnp.stack([part[0] for part in sums] + [part[1] for part in sums])
        return links.halves(jnp.pad(tables.T, ((0, 0), (0, LANES - 8))).astype(low), False)

    table_send, table_keep = order.run(table_halves, sums_0, sums_1, sums_2, sums_3)
    if links.pairwise:
        table_other = links.swap_core(table_send)
    if links.pairwise:
        table_goes, table_stays = order.run(links.first_pair, table_keep, table_other)
        table_side = (table_stays, links.swap(table_goes, links.bit(0, False)))
        table_goes, table_stays = order.run(links.first_pair, *table_side)
        table_side = (table_stays, links.swap(table_goes, links.bit(1, False)))
        cross_part = order.run(links.sum_fsdp, cross_parts)
        self_parts = finish([*self_sides, table_side])
        feed_in_part, feed_out_part = feed_part[:, : 4 * width], feed_part[:, 4 * width :]
        feed_out_part = jnp.concatenate(
            [feed_out_part[:, at * width : (at + 1) * width] for at in range(4)], axis=0
        )
    else:
        self_part = jnp.concatenate(
            [links.scatter_whole(first_send, first_keep), links.scatter_whole(second_send, second_keep)], axis=1
        )
        table_part = links.scatter_whole(table_send, table_keep)
    grad_encoded = order.run(
        lambda grad_k, grad_v, weights: weights_back([grad_k, grad_v], weights, cross_at),
        grad_k_cross,
        grad_v_cross,
        cross_held,
    )
    if links.pairwise:
        self_part = order.run(links.sum_fsdp, self_parts)
        self_part, table_part = self_part[:, : 4 * width], self_part[:, 4 * width :]
    self_in_part, self_out_part = self_part[:, : 3 * width], self_part[:, 3 * width :]
    cross_in_part = jnp.concatenate([cross_part[:, split : 3 * width], cross_part[:, :split]], axis=1)
    cross_out_part = cross_part[:, 3 * width :]

    return (
        block_output[None],
        grad_states[None],
        grad_encoded[None],
        self_in_part,
        self_out_part,
        cross_in_part,
        cross_out_part,
        feed_in_part,
        feed_out_part,
        table_part[:, :4].T,
        table_part[:, 4:8].T,
    )


def solution(mesh):
    dp_count, fsdp_count = mesh.shape["dp"], mesh.shape["fsdp"]
    split = Mesh(mesh.devices.reshape(dp_count // 2, 2, fsdp_count), BOTH)
    return jax.shard_map(
        body,
        mesh=split,
        in_specs=(
            P(BOTH, None, None),
            P(BOTH, None, None),
            P(BOTH, None, None),
            P(BOTH),
            P(BOTH),
            P(BOTH, None),
            P(BOTH, None),
            P(BOTH, None),
            P(BOTH, None),
            P(BOTH, None),
            P(BOTH, None),
            P(None, BOTH),
            P(None, BOTH),
        ),
        out_specs=(
            P(BOTH, None, None),
            P(BOTH, None, None),
            P(BOTH, None, None),
            P(BOTH, None),
            P(BOTH, None),
            P(BOTH, None),
            P(BOTH, None),
            P(BOTH, None),
            P(BOTH, None),
            P(None, BOTH),
            P(None, BOTH),
        ),
        check_vma=False,
    )
```

```python
import functools

import jax
import jax.numpy as jnp
from jax import lax
from jax.experimental import pallas as pl
from jax.experimental.pallas import tpu as pltpu
from jax.sharding import Mesh
from jax.sharding import PartitionSpec as P

HEAD = 64
LANES = 128
AHEAD = 1
BOTH = ("h", "c", "fsdp")
VMEM_BYTES = 60 * 1024 * 1024
SHORT = pl.CostEstimate(flops=1024, transcendentals=0, bytes_accessed=1024)


def product(left, right):
    return jnp.dot(left, right, preferred_element_type=jnp.float32)


def contract_rows(left, right):
    return lax.dot_general(
        left, right, (((0,), (0,)), ((), ())), preferred_element_type=jnp.float32
    )


def times_transposed(left, right):
    return lax.dot_general(
        left, right, (((1,), (1,)), ((), ())), preferred_element_type=jnp.float32
    )


def layer_norm(values, gain_row, bias_row):
    centre = values - jnp.mean(values, axis=-1, keepdims=True)
    spread = jnp.mean(centre * centre, axis=-1, keepdims=True)
    return centre * lax.rsqrt(spread + 1e-05) * gain_row + bias_row


def row_blocks(row_count, step):
    step = step if row_count % step == 0 else row_count
    return [slice(start, start + step) for start in range(0, row_count, step)]


def norm_backward_rows(norm, values_ref, grad_of, base_ref, rows_ref, grad_ref, low_ref, sums_ref, normed_ref=None):
    gain, bias = rows_ref[norm : norm + 1, :], rows_ref[4 + norm : 5 + norm, :]
    gain_sum, bias_sum = jnp.zeros_like(gain), jnp.zeros_like(gain)
    for rows in row_blocks(values_ref.shape[0], LANES):
        values = values_ref[rows, :].astype(jnp.float32)
        grad = grad_of(rows)
        centre = values - jnp.mean(values, axis=-1, keepdims=True)
        rate = lax.rsqrt(jnp.mean(centre * centre, axis=-1, keepdims=True) + 1e-05)
        normed = centre * rate
        if normed_ref is not None:
            normed_ref[rows, :] = (normed * gain + bias).astype(normed_ref.dtype)
        scaled = grad * gain
        total = rate * (
            scaled
            - jnp.mean(scaled, axis=-1, keepdims=True)
            - normed * jnp.mean(scaled * normed, axis=-1, keepdims=True)
        )
        if base_ref is not None:
            total = base_ref[rows, :] + total
        grad_ref[rows, :] = total
        if low_ref is not None:
            low_ref[rows, :] = total.astype(jnp.bfloat16)
        gain_sum += jnp.sum(grad * normed, axis=0, keepdims=True)
        bias_sum += jnp.sum(grad, axis=0, keepdims=True)
    sums_ref[0:1, :] = gain_sum
    sums_ref[1:2, :] = bias_sum


def with_bias_lane(matrix, head, bias):
    lane = lax.broadcasted_iota(jnp.int32, matrix.shape, 1)
    own = (lane >= head * HEAD) & (lane < (head + 1) * HEAD)
    rest = jnp.where(lane == (1 - head) * HEAD, bias, 0.0).astype(matrix.dtype)
    return jnp.where(own, matrix, rest)


def key_bias(key_count, key_limit):
    row = lax.broadcasted_iota(jnp.int32, (key_count, LANES), 0)
    return jnp.where(row < key_limit, 0.0, -1e30)


def masked_scores(keys, queries, diagonal_ref):
    scores = times_transposed(keys, queries)
    if diagonal_ref is None:
        return scores
    below = scores.shape[0] - scores.shape[1]
    diagonal = scores[below:, :] + diagonal_ref[...]
    return jnp.concatenate([scores[:below, :], diagonal], axis=0) if below else diagonal


def set_diagonal(diagonal_ref):
    @pl.when(pl.program_id(0) == 0)
    def _():
        row = lax.broadcasted_iota(jnp.int32, diagonal_ref.shape, 0)
        column = lax.broadcasted_iota(jnp.int32, diagonal_ref.shape, 1)
        diagonal_ref[...] = jnp.where(row <= column, 0.0, -1e30)


def query_width(row_count, causal):
    return 256 if causal and row_count % 256 == 0 else row_count


def query_blocks(row_count, key_count, causal):
    width = query_width(row_count, causal)
    return [
        (start, width, start + width if causal else key_count)
        for start in range(0, row_count, width)
    ]


def head_lanes(head, shape):
    lane = lax.broadcasted_iota(jnp.int32, shape, 1)
    return (lane >= head * HEAD) & (lane < (head + 1) * HEAD)


def staggered(items, first, middle, last, ahead):
    begun = [first(item) for item in items[:ahead]]
    waiting = None
    for at, item in enumerate(items):
        if at + ahead < len(items):
            begun.append(first(items[at + ahead]))
        done = middle(item, begun[at])
        begun[at] = None
        if waiting is not None:
            last(*waiting)
        waiting = (item, done)
    last(*waiting)


def attention_forward_kernel(
    causal, limit_ref, q_ref, k_ref, v_ref, mixed_ref, total_ref, mixed_turned, diagonal_ref
):
    row_count, key_count = q_ref.shape[0], k_ref.shape[0]
    bias = key_bias(key_count, limit_ref[0])
    if causal:
        set_diagonal(diagonal_ref)
    else:
        diagonal_ref = None
    values_turned = v_ref[...].T
    ones = jnp.ones((16, key_count), jnp.bfloat16)
    scaled = q_ref[...] * jnp.bfloat16(HEAD**-0.5)
    queries = [with_bias_lane(scaled, head, 1.0) for head in range(2)]
    keys = [with_bias_lane(k_ref[...], head, bias) for head in range(2)]
    lanes = [slice(head * HEAD, (head + 1) * HEAD) for head in range(2)]
    values = [jnp.concatenate([values_turned[at, :], ones], axis=0) for at in lanes]

    def scores_of(item):
        head, (start, width, stop) = item
        return masked_scores(keys[head][:stop, :], queries[head][start : start + width, :], diagonal_ref)

    def expand(item, scores):
        highest = jnp.max(scores, axis=0, keepdims=True)
        return highest, jnp.exp(scores - highest).astype(jnp.bfloat16)

    def mix(item, done):
        head, (start, width, stop) = item
        highest, expanded = done
        mixed = product(values[head][:, :stop], expanded)
        total = mixed[HEAD : HEAD + 1, :]
        mixed_turned[lanes[head], start : start + width] = mixed[:HEAD, :] / total
        total_ref[0, head : head + 1, start : start + width] = highest + jnp.log(total)

    items = [(head, block) for block in query_blocks(row_count, key_count, causal) for head in range(2)]
    staggered(items, scores_of, expand, mix, 2)
    mixed_ref[...] = mixed_turned[...].T.astype(jnp.bfloat16)


def attention_forward(limit, queries, q_at, keys, k_at, values, v_at, causal):
    row_count, key_count = queries.shape[0], keys.shape[0]
    width = 1024
    pairs = width // LANES
    return pl.pallas_call(
        functools.partial(attention_forward_kernel, causal),
        grid_spec=pltpu.PrefetchScalarGridSpec(
            num_scalar_prefetch=1,
            grid=(pairs,),
            in_specs=[
                pl.BlockSpec((row_count, LANES), lambda p, s: (0, q_at + p)),
                pl.BlockSpec((key_count, LANES), lambda p, s: (0, k_at + p)),
                pl.BlockSpec((key_count, LANES), lambda p, s: (0, v_at + p)),
            ],
            out_specs=[
                pl.BlockSpec((row_count, LANES), lambda p, s: (0, p)),
                pl.BlockSpec((1, 2, row_count), lambda p, s: (p, 0, 0)),
            ],
            scratch_shapes=[
                pltpu.VMEM((LANES, row_count), jnp.float32),
                pltpu.VMEM((query_width(row_count, causal),) * 2, jnp.float32),
            ],
        ),
        out_shape=[
            jax.ShapeDtypeStruct((row_count, width), jnp.bfloat16),
            jax.ShapeDtypeStruct((pairs, 2, row_count), jnp.float32),
        ],
        compiler_params=pltpu.CompilerParams(vmem_limit_bytes=VMEM_BYTES),
        cost_estimate=SHORT,
        name="attention_forward",
    )(limit, queries, keys, values)


def attention_backward_kernel(
    causal,
    limit_ref,
    q_ref,
    k_ref,
    v_ref,
    mixed_ref,
    grad_ref,
    total_ref,
    grad_q_ref,
    grad_k_ref,
    grad_v_ref,
    grad_q_turned,
    grad_k_sum,
    grad_v_sum,
    diagonal_ref,
):
    row_count, key_count = q_ref.shape[0], k_ref.shape[0]
    bias = key_bias(key_count, limit_ref[0])
    if causal:
        set_diagonal(diagonal_ref)
    else:
        diagonal_ref = None
    keys_turned = k_ref[...].T
    scaled = q_ref[...] * jnp.bfloat16(HEAD**-0.5)
    grad = grad_ref[...]
    inner_turned = (grad.astype(jnp.float32) * mixed_ref[...].astype(jnp.float32)).T
    grad_k_sum[...] = jnp.zeros_like(grad_k_sum)
    grad_v_sum[...] = jnp.zeros_like(grad_v_sum)
    masks = [head_lanes(head, scaled.shape) for head in range(2)]
    queries = [jnp.where(mask, scaled, jnp.zeros_like(scaled)) for mask in masks]
    grads = [jnp.where(mask, grad, jnp.zeros_like(grad)) for mask in masks]
    biased = [with_bias_lane(scaled, head, 1.0) for head in range(2)]
    keys = [with_bias_lane(k_ref[...], head, bias) for head in range(2)]
    lanes = [slice(head * HEAD, (head + 1) * HEAD) for head in range(2)]
    inner = [jnp.sum(inner_turned[at, :], axis=0, keepdims=True) for at in lanes]

    def scores_of(item):
        head, (start, width, stop) = item
        columns = slice(start, start + width)
        scores = masked_scores(keys[head][:stop, :], biased[head][columns, :], diagonal_ref)
        return scores, times_transposed(v_ref[:stop, :], grads[head][columns, :])

    def differentiate(item, begun):
        head, (start, width, stop) = item
        columns = slice(start, start + width)
        scores, grad_probs = begun
        probs = jnp.exp(scores - total_ref[0, head : head + 1, columns])
        grad_scores = probs * (grad_probs - inner[head][:, columns])
        return probs.astype(jnp.bfloat16), grad_scores.astype(jnp.bfloat16)

    def add(item, done):
        head, (start, width, stop) = item
        columns = slice(start, start + width)
        probs, grad_scores = done
        grad_v_sum[:stop, :] += product(probs, grads[head][columns, :])
        grad_k_sum[:stop, :] += product(grad_scores, queries[head][columns, :])
        grad_q_turned[lanes[head], columns] = product(keys_turned[lanes[head], :stop], grad_scores)

    items = [(head, block) for block in query_blocks(row_count, key_count, causal) for head in range(2)]
    staggered(items, scores_of, differentiate, add, AHEAD)
    grad_q_ref[...] = (grad_q_turned[...].T * HEAD**-0.5).astype(jnp.bfloat16)
    grad_k_ref[...] = grad_k_sum[...].astype(jnp.bfloat16)
    grad_v_ref[...] = grad_v_sum[...].astype(jnp.bfloat16)


def attention_backward(limit, queries, q_at, keys, k_at, values, v_at, mixed, grad_mixed, totals, causal):
    row_count, key_count = queries.shape[0], keys.shape[0]
    width = 1024
    pairs = width // LANES
    row_block = pl.BlockSpec((row_count, LANES), lambda p, s: (0, p))
    key_block = pl.BlockSpec((key_count, LANES), lambda p, s: (0, p))
    return pl.pallas_call(
        functools.partial(attention_backward_kernel, causal),
        grid_spec=pltpu.PrefetchScalarGridSpec(
            num_scalar_prefetch=1,
            grid=(pairs,),
            in_specs=[
                pl.BlockSpec((row_count, LANES), lambda p, s: (0, q_at + p)),
                pl.BlockSpec((key_count, LANES), lambda p, s: (0, k_at + p)),
                pl.BlockSpec((key_count, LANES), lambda p, s: (0, v_at + p)),
                row_block,
                row_block,
                pl.BlockSpec((1, 2, row_count), lambda p, s: (p, 0, 0)),
            ],
            out_specs=[row_block, key_block, key_block],
            scratch_shapes=[
                pltpu.VMEM((LANES, row_count), jnp.float32),
                pltpu.VMEM((key_count, LANES), jnp.float32),
                pltpu.VMEM((key_count, LANES), jnp.float32),
                pltpu.VMEM((query_width(row_count, causal),) * 2, jnp.float32),
            ],
        ),
        out_shape=[
            jax.ShapeDtypeStruct((row_count, width), jnp.bfloat16),
            jax.ShapeDtypeStruct((key_count, width), jnp.bfloat16),
            jax.ShapeDtypeStruct((key_count, width), jnp.bfloat16),
        ],
        compiler_params=pltpu.CompilerParams(vmem_limit_bytes=VMEM_BYTES),
        cost_estimate=SHORT,
        name="attention_backward",
    )(limit, queries, keys, values, mixed, grad_mixed, totals)


def gelu_and_slope(values):
    normal_cdf = 0.5 + 0.5 * lax.erf(values * 2.0 ** (-0.5))
    bell = jnp.exp(-0.5 * values * values) * (2.0 * jnp.pi) ** (-0.5)
    return values * normal_cdf, normal_cdf + values * bell


def unfold_rows(folded_ref, unfolded, rows):
    width = unfolded.shape[1]
    folds = folded_ref.shape[1] // width
    for shard in range(folded_ref.shape[0] // rows):
        for fold in range(folds):
            start = (shard * folds + fold) * rows
            unfolded[start : start + rows, :] = folded_ref[
                shard * rows : (shard + 1) * rows, fold * width : (fold + 1) * width
            ]


def fold_rows(unfolded, folded_ref, rows):
    width = unfolded.shape[1]
    folds = folded_ref.shape[1] // width
    for shard in range(folded_ref.shape[0] // rows):
        for fold in range(folds):
            start = (shard * folds + fold) * rows
            folded_ref[shard * rows : (shard + 1) * rows, fold * width : (fold + 1) * width] = unfolded[
                start : start + rows, :
            ]


def feed_forward_kernel(
    rows,
    limit_ref,
    normed_ref,
    input_ref,
    output_ref,
    base_ref,
    cotangent_ref,
    rows_ref,
    hidden_ref,
    slope_ref,
    block_ref,
    grad_ref,
    low_ref,
    sums_ref,
    after_ref,
    unfolded,
):
    if rows:
        unfold_rows(output_ref, unfolded, rows)
        output_ref = unfolded

    @pl.when(pl.program_id(0) == 0)
    def _():
        after_ref[...] = base_ref[...]

    row_count = normed_ref.shape[0]
    step = 256 if row_count % 256 == 0 else row_count
    blocks = [slice(start, start + step) for start in range(0, row_count, step)]
    hidden_pre = product(normed_ref[blocks[0], :], input_ref[...])
    ready = None
    for at, rows_at in enumerate(blocks):
        following = product(normed_ref[blocks[at + 1], :], input_ref[...]) if at + 1 < len(blocks) else None
        hidden, slope = gelu_and_slope(hidden_pre)
        hidden = hidden.astype(jnp.bfloat16)
        hidden_ref[rows_at, :] = hidden
        slope_ref[rows_at, :] = slope.astype(jnp.bfloat16)
        if ready is not None:
            after_ref[blocks[at - 1], :] += product(ready, output_ref[...])
        hidden_pre, ready = following, hidden
    after_ref[blocks[-1], :] += product(ready, output_ref[...])

    @pl.when(pl.program_id(0) == pl.num_programs(0) - 1)
    def _():
        def live_grad(rows_at):
            shape = (rows_at.stop - rows_at.start, after_ref.shape[1])
            row = rows_at.start + lax.broadcasted_iota(jnp.int32, shape, 0)
            return jnp.where(row < limit_ref[0], cotangent_ref[rows_at, :], 0.0)

        norm_backward_rows(3, after_ref, live_grad, None, rows_ref, grad_ref, low_ref, sums_ref, block_ref)


FEED_TILE = 512


def feed_weight_specs(folds, width, tile, index):
    first = pl.BlockSpec((width, tile), lambda *at: (0, index(*at)))
    if folds:
        return first, pl.BlockSpec((tile // folds, folds * width), lambda *at: (index(*at), 1))
    return first, pl.BlockSpec((tile, width), lambda *at: (index(*at), 0))


def feed_forward(rows, limit, normed, input_low, output_low, after_cross, cotangent, norm_rows):
    row_count, width = normed.shape
    hidden_width = 4 * width
    tile = FEED_TILE
    whole = pl.BlockSpec((row_count, width), lambda j, s: (0, 0))
    tall = pl.BlockSpec((row_count, tile), lambda j, s: (0, j))
    weight_specs = feed_weight_specs(hidden_width // width if rows else 0, width, tile, lambda j, s: j)
    return pl.pallas_call(
        functools.partial(feed_forward_kernel, rows),
        grid_spec=pltpu.PrefetchScalarGridSpec(
            num_scalar_prefetch=1,
            grid=(hidden_width // tile,),
            in_specs=[whole, *weight_specs, whole, whole, pl.BlockSpec((8, width), lambda j, s: (0, 0))],
            out_specs=[tall, tall, whole, whole, whole, pl.BlockSpec((2, width), lambda j, s: (0, 0))],
            scratch_shapes=[pltpu.VMEM((row_count, width), jnp.float32), pltpu.VMEM((tile, width), jnp.bfloat16)],
        ),
        out_shape=[
            jax.ShapeDtypeStruct((row_count, hidden_width), jnp.bfloat16),
            jax.ShapeDtypeStruct((row_count, hidden_width), jnp.bfloat16),
            jax.ShapeDtypeStruct((row_count, width), jnp.bfloat16),
            jax.ShapeDtypeStruct((row_count, width), jnp.float32),
            jax.ShapeDtypeStruct((row_count, width), jnp.bfloat16),
            jax.ShapeDtypeStruct((2, width), jnp.float32),
        ],
        compiler_params=pltpu.CompilerParams(vmem_limit_bytes=VMEM_BYTES),
        cost_estimate=SHORT,
        name="feed_forward",
    )(limit, normed, input_low, output_low, after_cross, cotangent, norm_rows)


def turn_rows(x_ref, turned, positions_ref):
    for j in range(turned.shape[0] // LANES):
        start = pl.multiple_of(positions_ref[j] * LANES, LANES)
        block = slice(j * LANES, (j + 1) * LANES)
        turned[pl.ds(start, LANES), :] = x_ref[block, :] if x_ref.shape == turned.shape else x_ref[:, block].T


def feed_backward_kernel(
    rows,
    tiles_ref,
    positions_ref,
    grad_ref,
    normed_ref,
    hidden_ref,
    slope_ref,
    input_ref,
    output_ref,
    values_ref,
    base_ref,
    rows_ref,
    in_send_ref,
    in_keep_ref,
    out_send_ref,
    out_keep_ref,
    total_ref,
    low_ref,
    sums_ref,
    grad_normed_ref,
    turned,
    unfolded,
):
    step = pl.program_id(0)
    if rows:
        unfold_rows(output_ref, unfolded, rows)
        output_ref = unfolded

    @pl.when(step == 0)
    def _():
        grad_normed_ref[...] = jnp.zeros_like(grad_normed_ref)
        turn_rows(normed_ref, turned, positions_ref)

    grad_hidden = times_transposed(grad_ref[...], output_ref[...])
    grad_pre = (grad_hidden * slope_ref[...].astype(jnp.float32)).astype(jnp.bfloat16)
    grad_out = contract_rows(hidden_ref[...], grad_ref[...]).astype(jnp.bfloat16)
    for out_ref, first in ((out_send_ref, True), (out_keep_ref, False)):

        @pl.when((step < pl.num_programs(0) // 2) == first)
        def _(out_ref=out_ref):
            if rows:
                fold_rows(grad_out, out_ref, rows)
            else:
                out_ref[...] = grad_out

    half = turned.shape[0] // 2
    in_send_ref[...] = product(turned[:half, :], grad_pre).astype(jnp.bfloat16)
    in_keep_ref[...] = product(turned[half:, :], grad_pre).astype(jnp.bfloat16)
    grad_normed_ref[...] += times_transposed(grad_pre, input_ref[...])

    @pl.when(step == pl.num_programs(0) - 1)
    def _():
        norm_backward_rows(
            2,
            values_ref,
            lambda rows_at: grad_normed_ref[rows_at, :],
            base_ref,
            rows_ref,
            total_ref,
            low_ref,
            sums_ref,
        )


def feed_backward(
    rows, tiles, positions, grad_branch, normed, hidden, slope, input_low, output_low, after_cross, grad_after, norm_rows
):
    row_count, width = grad_branch.shape
    hidden_width = hidden.shape[1]
    count = tiles.shape[0]
    half = count // 2
    tile = hidden_width // count
    whole = pl.BlockSpec((row_count, width), lambda j, t, p: (0, 0))
    tall = pl.BlockSpec((row_count, tile), lambda j, t, p: (0, t[j]))
    in_half = pl.BlockSpec((width // 2, tile), lambda j, t, p: (0, t[j]))
    folds = hidden_width // width if rows else 1
    weight_specs = feed_weight_specs(folds if rows else 0, width, tile, lambda j, t, p: t[j])
    return pl.pallas_call(
        functools.partial(feed_backward_kernel, rows),
        grid_spec=pltpu.PrefetchScalarGridSpec(
            num_scalar_prefetch=2,
            grid=(count,),
            in_specs=[
                whole,
                whole,
                tall,
                tall,
                *weight_specs,
                whole,
                whole,
                pl.BlockSpec((8, width), lambda j, t, p: (0, 0)),
            ],
            out_specs=[
                in_half,
                in_half,
                pl.BlockSpec((tile // folds, folds * width), lambda j, t, p: (jnp.minimum(j, half - 1), 0)),
                pl.BlockSpec((tile // folds, folds * width), lambda j, t, p: (jnp.maximum(j - half, 0), 0)),
                whole,
                whole,
                pl.BlockSpec((2, width), lambda j, t, p: (0, 0)),
            ],
            scratch_shapes=[
                pltpu.VMEM((row_count, width), jnp.float32),
                pltpu.VMEM((width, row_count), jnp.bfloat16),
                pltpu.VMEM((tile, width), jnp.bfloat16),
            ],
        ),
        out_shape=[
            jax.ShapeDtypeStruct((width // 2, hidden_width), jnp.bfloat16),
            jax.ShapeDtypeStruct((width // 2, hidden_width), jnp.bfloat16),
            jax.ShapeDtypeStruct((hidden_width // folds // 2, folds * width), jnp.bfloat16),
            jax.ShapeDtypeStruct((hidden_width // folds // 2, folds * width), jnp.bfloat16),
            jax.ShapeDtypeStruct((row_count, width), jnp.float32),
            jax.ShapeDtypeStruct((row_count, width), jnp.bfloat16),
            jax.ShapeDtypeStruct((2, width), jnp.float32),
        ],
        compiler_params=pltpu.CompilerParams(vmem_limit_bytes=VMEM_BYTES),
        cost_estimate=SHORT,
        name="feed_backward",
    )(
        tiles, positions, grad_branch, normed, hidden, slope, input_low, output_low, after_cross, grad_after, norm_rows
    )


WEIGHT_TILE = 512


def tile_starts(arrays):
    starts = [0]
    for array in arrays:
        starts.append(starts[-1] + array.shape[1] // WEIGHT_TILE)
    return starts


def tile_spec(rows, first, last, offset=0):
    return pl.BlockSpec(
        (rows, WEIGHT_TILE), lambda j, *_: (0, offset + jnp.clip(j - first, 0, last - first - 1))
    )


def turn_kernel(count, *refs):
    for x_ref, turned_ref in zip(refs[:count], refs[count:]):
        for block in row_blocks(x_ref.shape[1], LANES):
            turned_ref[block, :] = x_ref[:, block].T


def turn(*arrays):
    return pl.pallas_call(
        functools.partial(turn_kernel, len(arrays)),
        grid=(1,),
        in_specs=[pl.BlockSpec(array.shape, lambda j: (0, 0)) for array in arrays],
        out_specs=[pl.BlockSpec(array.shape[::-1], lambda j: (0, 0)) for array in arrays],
        out_shape=[jax.ShapeDtypeStruct(array.shape[::-1], array.dtype) for array in arrays],
        compiler_params=pltpu.CompilerParams(vmem_limit_bytes=VMEM_BYTES),
        cost_estimate=SHORT,
        name="turn",
    )(*arrays)


def weight_gradient_kernel(starts, groups, crossed, positions_ref, x_ref, *refs):
    grads, outs, turned = refs[: len(starts) - 1], refs[len(starts) - 1 : -1], refs[-1]
    step = pl.program_id(0)

    @pl.when(step == 0)
    def _():
        turn_rows(x_ref, turned, positions_ref)

    half = turned.shape[0] // 2
    for index, grad_ref in enumerate(grads):
        group = groups[index]

        @pl.when((step >= starts[index]) & (step < starts[index + 1]))
        def _(grad_ref=grad_ref, group=group):
            for out_ref, rows in ((outs[2 * group], slice(0, half)), (outs[2 * group + 1], slice(half, 2 * half))):
                result = product(turned[rows, :], grad_ref[...]).astype(jnp.bfloat16)
                if crossed[group]:
                    for block, place in enumerate((0, 2, 1, 3)):
                        out_ref[place * LANES : (place + 1) * LANES, :] = result[
                            block * LANES : (block + 1) * LANES, :
                        ]
                else:
                    out_ref[...] = result


def weight_gradient(positions, x, *groups):
    grads = [grad for group, _ in groups for grad in group]
    row_count = grads[0].shape[0]
    width = x.size // row_count
    group_of = [index for index, (group, _) in enumerate(groups) for _ in group]
    starts = tile_starts(grads)
    half = width // 2
    out_specs, out_shape = [], []
    for index in range(len(groups)):
        own = [at for at, group in enumerate(group_of) if group == index]
        first, last = starts[own[0]], starts[own[-1] + 1]
        out_specs += [tile_spec(half, first, last)] * 2
        out_shape += [jax.ShapeDtypeStruct((half, (last - first) * WEIGHT_TILE), jnp.bfloat16)] * 2
    return pl.pallas_call(
        functools.partial(weight_gradient_kernel, starts, group_of, [crossed for _, crossed in groups]),
        grid_spec=pltpu.PrefetchScalarGridSpec(
            num_scalar_prefetch=1,
            grid=(starts[-1],),
            in_specs=[pl.BlockSpec(x.shape, lambda j, p: (0, 0))]
            + [tile_spec(row_count, starts[i], starts[i + 1]) for i in range(len(grads))],
            out_specs=out_specs,
            scratch_shapes=[pltpu.VMEM((width, row_count), jnp.bfloat16)],
        ),
        out_shape=out_shape,
        compiler_params=pltpu.CompilerParams(vmem_limit_bytes=VMEM_BYTES),
        cost_estimate=SHORT,
        name="weight_gradient",
    )(positions, x, *grads)


def output_backward_kernel(positions_ref, x_ref, grad_ref, weight_ref, send_ref, keep_ref, mixed_ref, turned, summed):
    step = pl.program_id(0)

    @pl.when(step == 0)
    def _():
        turn_rows(x_ref, turned, positions_ref)
        summed[...] = jnp.zeros_like(summed)

    half = turned.shape[0] // 2
    summed[...] += times_transposed(grad_ref[...], weight_ref[...])
    send_ref[...] = product(turned[:half, :], grad_ref[...]).astype(jnp.bfloat16)
    keep_ref[...] = product(turned[half:, :], grad_ref[...]).astype(jnp.bfloat16)

    @pl.when(step == pl.num_programs(0) - 1)
    def _():
        mixed_ref[...] = summed[...].astype(jnp.bfloat16)


def output_backward(positions, x, grad, weights, column):
    row_count, width = grad.shape
    half = width // 2
    last = width // WEIGHT_TILE
    return pl.pallas_call(
        output_backward_kernel,
        grid_spec=pltpu.PrefetchScalarGridSpec(
            num_scalar_prefetch=1,
            grid=(last,),
            in_specs=[
                pl.BlockSpec(x.shape, lambda j, p: (0, 0)),
                tile_spec(row_count, 0, last),
                tile_spec(width, 0, last, offset=column // WEIGHT_TILE),
            ],
            out_specs=[
                tile_spec(half, 0, last),
                tile_spec(half, 0, last),
                pl.BlockSpec((row_count, width), lambda j, p: (0, 0)),
            ],
            scratch_shapes=[
                pltpu.VMEM((width, row_count), jnp.bfloat16),
                pltpu.VMEM((row_count, width), jnp.float32),
            ],
        ),
        out_shape=[jax.ShapeDtypeStruct((half, width), jnp.bfloat16)] * 2
        + [jax.ShapeDtypeStruct((row_count, width), jnp.bfloat16)],
        compiler_params=pltpu.CompilerParams(vmem_limit_bytes=VMEM_BYTES),
        cost_estimate=SHORT,
        name="output_backward",
    )(positions, x, grad, weights)


def weights_back_kernel(starts, *refs):
    count = len(starts) - 1
    grads, weights_ref, total_ref = refs[:count], refs[count], refs[-1]
    step = pl.program_id(0)

    @pl.when(step == 0)
    def _():
        total_ref[...] = jnp.zeros_like(total_ref)

    for index in range(count):

        @pl.when((step >= starts[index]) & (step < starts[index + 1]))
        def _(index=index):
            total_ref[...] += times_transposed(grads[index][...], weights_ref[...])


def weights_back(grads, weights, column):
    row_count, width = grads[0].shape[0], weights.shape[0]
    starts = tile_starts(grads)
    return pl.pallas_call(
        functools.partial(weights_back_kernel, starts),
        grid=(starts[-1],),
        in_specs=[tile_spec(row_count, starts[i], starts[i + 1]) for i in range(len(grads))]
        + [tile_spec(width, 0, starts[-1], offset=column // WEIGHT_TILE)],
        out_specs=pl.BlockSpec((row_count, width), lambda j: (0, 0)),
        out_shape=jax.ShapeDtypeStruct((row_count, width), jnp.float32),
        compiler_params=pltpu.CompilerParams(vmem_limit_bytes=VMEM_BYTES),
        cost_estimate=SHORT,
        name="weights_back",
    )(*grads, weights)


def input_gradient_kernel(norm, starts, has_low, *refs):
    count = len(starts) - 1
    grads, weights = refs[:count], refs[count : 2 * count]
    values_ref, base_ref, rows_ref, total_ref = refs[2 * count : 2 * count + 4]
    low_ref = refs[2 * count + 4] if has_low else None
    sums_ref, summed = refs[-2:]
    step = pl.program_id(0)

    @pl.when(step == 0)
    def _():
        summed[...] = jnp.zeros_like(summed)

    for index in range(count):

        @pl.when((step >= starts[index]) & (step < starts[index + 1]))
        def _(index=index):
            summed[...] += times_transposed(grads[index][...], weights[index][...])

    @pl.when(step == starts[-1] - 1)
    def _():
        norm_backward_rows(
            norm, values_ref, lambda rows: summed[rows, :], base_ref, rows_ref, total_ref, low_ref, sums_ref
        )


def input_gradient(norm, grads, weights, values, base, norm_rows, has_low):
    row_count, width = values.shape
    starts = tile_starts(grads)
    whole = pl.BlockSpec((row_count, width), lambda j: (0, 0))
    spans = [(starts[i], starts[i + 1]) for i in range(len(grads))]
    lows = [jax.ShapeDtypeStruct((row_count, width), jnp.bfloat16)] if has_low else []
    return pl.pallas_call(
        functools.partial(input_gradient_kernel, norm, starts, has_low),
        grid=(starts[-1],),
        in_specs=[tile_spec(row_count, *span) for span in spans]
        + [
            tile_spec(width, *span, offset=column // WEIGHT_TILE) for span, (_, column) in zip(spans, weights)
        ]
        + [whole, whole, pl.BlockSpec((8, width), lambda j: (0, 0))],
        out_specs=[whole] * (1 + len(lows)) + [pl.BlockSpec((2, width), lambda j: (0, 0))],
        out_shape=[jax.ShapeDtypeStruct((row_count, width), jnp.float32)]
        + lows
        + [jax.ShapeDtypeStruct((2, width), jnp.float32)],
        scratch_shapes=[pltpu.VMEM((row_count, width), jnp.float32)],
        compiler_params=pltpu.CompilerParams(vmem_limit_bytes=VMEM_BYTES),
        cost_estimate=SHORT,
        name="input_gradient",
    )(*grads, *[array for array, _ in weights], values, base, norm_rows)


class Order:
    def __init__(self):
        self.last = ()

    def after(self, *values):
        values, _ = lax.optimization_barrier((values, self.last))
        return values if len(values) > 1 else values[0]

    def run(self, work, *values):
        values, _ = lax.optimization_barrier((values, self.last))
        result = work(*values)
        self.last = result
        return result


def place_rows_kernel(counts, rows, table_ref, *refs):
    pieces, out_ref, held, sems_in, sems_out = refs[:-4], *refs[-4:]
    loads, stores = [], []
    for piece, count in zip(pieces, counts):
        for block in range(count):
            at = len(loads)
            start = pl.multiple_of(table_ref[at] * rows, rows)
            loads.append(
                pltpu.make_async_copy(piece.at[pl.ds(block * rows, rows), :], held.at[at], sems_in.at[at])
            )
            stores.append(
                pltpu.make_async_copy(held.at[at], out_ref.at[pl.ds(start, rows), :], sems_out.at[at])
            )
    for load in loads:
        load.start()
    for load, store in zip(loads, stores):
        load.wait()
        store.start()
    for store in stores:
        store.wait()


def place_rows(table, pieces, rows):
    counts = [piece.shape[0] // rows for piece in pieces]
    total, columns = sum(counts), pieces[0].shape[1]
    anywhere = pl.BlockSpec(memory_space=pl.ANY)
    return pl.pallas_call(
        functools.partial(place_rows_kernel, counts, rows),
        grid_spec=pltpu.PrefetchScalarGridSpec(
            num_scalar_prefetch=1,
            grid=(1,),
            in_specs=[anywhere] * len(pieces),
            out_specs=anywhere,
            scratch_shapes=[
                pltpu.VMEM((total, rows, columns), pieces[0].dtype),
                pltpu.SemaphoreType.DMA((total,)),
                pltpu.SemaphoreType.DMA((total,)),
            ],
        ),
        out_shape=jax.ShapeDtypeStruct((total * rows, columns), pieces[0].dtype),
        compiler_params=pltpu.CompilerParams(vmem_limit_bytes=VMEM_BYTES),
        cost_estimate=SHORT,
        name="place_rows",
    )(table, *pieces)


class Links:
    def __init__(self, width):
        self.h_count, self.fsdp_count = lax.axis_size("h"), lax.axis_size("fsdp")
        self.core, self.h, self.fsdp = lax.axis_index("c"), lax.axis_index("h"), lax.axis_index("fsdp")
        dp_count = 2 * self.h_count
        self.pairwise = (
            (self.h_count & (self.h_count - 1)) == 0
            and (self.fsdp_count & (self.fsdp_count - 1)) == 0
            and width == dp_count * LANES
        )
        self.blocks = width // LANES
        self.bits = [1 << b for b in range(self.h_count.bit_length() - 1)]
        self.fsdp_table = (self.fsdp ^ jnp.arange(self.fsdp_count, dtype=jnp.int32)).astype(jnp.int32)

    def order(self, flip):
        return self.bits[::-1] if flip else self.bits

    def swap(self, array, bit):
        return lax.ppermute(array, "h", [(i, i ^ bit) for i in range(self.h_count)])

    def swap_core(self, array):
        return lax.ppermute(array, "c", [(0, 1), (1, 0)])

    def swap_fsdp(self, array, bit):
        return lax.ppermute(array, "fsdp", [(i, i ^ bit) for i in range(self.fsdp_count)])

    def gather(self, shard):
        return lax.all_gather(shard, BOTH, axis=0, tiled=True)

    def spread_fsdp(self, shard):
        return [shard] + [self.swap_fsdp(shard, k) for k in range(1, self.fsdp_count)]

    def place_fsdp(self, parts):
        return place_rows(self.fsdp_table, parts, parts[0].shape[0])

    def spread(self, block, at, flip):
        return jnp.concatenate([block, self.swap(block, self.order(flip)[at])], axis=0)

    def place(self, block, other, flip):
        masks = [0]
        for bit in self.order(flip):
            masks = masks + [mask ^ bit for mask in masks]
        h = self.h ^ jnp.asarray(masks, dtype=jnp.int32)
        table = jnp.concatenate([2 * h + self.core, 2 * h + 1 - self.core]).astype(jnp.int32)
        return place_rows(table, [block, other], block.shape[0] // self.h_count)

    def tiles(self):
        if not self.pairwise:
            return jnp.arange(self.blocks, dtype=jnp.int32)
        h = 2 * jnp.arange(self.h_count, dtype=jnp.int32)
        return jnp.concatenate([h + 1 - self.core, h + self.core]).astype(jnp.int32)

    def positions(self, flip=None):
        block = jnp.arange(self.blocks, dtype=jnp.int32)
        if not self.pairwise:
            return block
        place, own = block >> 1, (block & 1) == self.core
        if flip is not None:
            mask, place = place ^ self.h, jnp.zeros_like(place)
            for at, bit in enumerate(self.order(flip)):
                place = place + jnp.where((mask & bit) == 0, 1 << at, 0)
        return (place + jnp.where(own, self.h_count, 0)).astype(jnp.int32)

    def halves(self, rows, flip):
        ordered = place_rows(self.positions(flip), [rows], rows.shape[0] // self.blocks)
        half = rows.shape[0] // 2
        return ordered[:half], ordered[half:]

    def sum_cores(self, keep, other):
        return (keep.astype(jnp.float32) + other.astype(jnp.float32)).astype(jnp.bfloat16)

    def send_fsdp(self, grad):
        return lax.all_to_all(grad, "fsdp", 0, 0, tiled=True)

    def sum_fsdp(self, parts):
        rows = parts.shape[0] // self.fsdp_count
        parts = parts.astype(jnp.float32)
        return sum(parts[k * rows : (k + 1) * rows] for k in range(self.fsdp_count))

    def scatter_whole(self, send, keep):
        grad = jnp.concatenate([send, keep], axis=0).astype(jnp.float32)
        part = lax.psum_scatter(grad, ("h", "c"), scatter_dimension=0, tiled=True)
        return lax.psum_scatter(part, "fsdp", scatter_dimension=0, tiled=True)

    def sum_chips(self, grad):
        return lax.psum_scatter(grad, "h", scatter_dimension=0, tiled=True)

    def first_pair(self, keep, other):
        half = keep.shape[0] // 2
        return self.sum_cores(keep[:half], other[:half]), self.sum_cores(keep[half:], other[half:])

    def bit(self, at, flip):
        return self.order(flip)[::-1][at]


def body(
    unit_states,
    encoder_states,
    cotangent,
    unit_lengths,
    text_lengths,
    self_project,
    self_output,
    cross_project,
    cross_output,
    feed_input,
    feed_output,
    norm_gains,
    norm_biases,
):
    low = jnp.bfloat16
    layer_input = unit_states[0].astype(jnp.float32)
    encoded = encoder_states[0]
    row_count, width = layer_input.shape
    links = Links(width)

    tables = jnp.concatenate([norm_gains, norm_biases], axis=0).T
    tables = jnp.pad(tables, ((0, 0), (0, LANES - tables.shape[1])))
    self_shard = jnp.concatenate([self_project.astype(low), self_output.astype(low), tables], axis=1)
    cross_shard = jnp.concatenate(
        [cross_project[:, width:].astype(low), cross_project[:, :width].astype(low), cross_output.astype(low)],
        axis=1,
    )
    feed_shard = feed_input.astype(low)
    order = Order()
    flips = [False, True]
    split = 2 * width
    if links.pairwise:
        fold_count = feed_input.shape[0]
        folded = [
            feed_output[at : at + fold_count].astype(low) for at in range(0, feed_output.shape[0], fold_count)
        ]
        feed_shard = jnp.concatenate([feed_shard] + folded, axis=1)
        bits = [links.order(flip) for flip in flips]

        def send(sides, at):
            return [links.swap(side, bit[at]) for side, bit in zip(sides, bits)]

        def join(*arrays):
            half = len(arrays) // 2
            return [jnp.concatenate(pair, axis=0) for pair in zip(arrays[:half], arrays[half:])]

        def lay(*arrays):
            half = len(arrays) // 2
            return [links.place(*pair, flip) for pair, flip in zip(zip(arrays[:half], arrays[half:]), flips)]

        def lay_fsdp(*parts):
            return links.place_fsdp(parts)

        gathered = links.gather(jnp.concatenate([feed_shard, cross_shard], axis=1))
        feed_input_low, feed_output_low, cross_whole = gathered, gathered, gathered[:, 8 * width :]
        cross_held, cross_at = gathered, 8 * width
        self_part = order.run(lay_fsdp, *links.spread_fsdp(self_shard))
        self_sides = [self_part[:, :split], self_part[:, split:]]
        self_swaps = send(self_sides, 0)
        self_sides = order.run(join, *self_sides, *self_swaps)
        self_swaps = send(self_sides, 1)
        self_sides = order.run(join, *self_sides, *self_swaps)
        self_others = [links.swap_core(side) for side in self_sides]
        self_first, self_second = order.run(lay, *self_sides, *self_others)
    else:
        fold_count = 0
        self_whole, cross_whole = links.gather(self_shard), links.gather(cross_shard)
        self_first, self_second = self_whole[:, :split], self_whole[:, split:]
        cross_held, cross_at = cross_whole, 0
        feed_input_low = links.gather(feed_shard)
        feed_output_low = links.gather(feed_output.astype(low))

    self_value, self_output_low = self_second[:, :width], self_second[:, width : 2 * width]
    norm_rows = self_second[:, 2 * width : 2 * width + 8].astype(jnp.float32).T
    gain_table, bias_table = norm_rows[:4], norm_rows[4:]

    def self_projections(layer_input, self_first, self_value, gain_row, bias_row):
        normed_self = layer_norm(layer_input, gain_row, bias_row).astype(low)
        return (
            normed_self,
            product(normed_self, self_first).astype(low),
            product(normed_self, self_value).astype(low),
        )

    normed_self, query_key, self_values = order.run(
        self_projections, layer_input, self_first, self_value, gain_table[0], bias_table[0]
    )
    self_mixed, self_totals = order.run(
        lambda query_key, self_values: attention_forward(
            unit_lengths, query_key, 0, query_key, width // LANES, self_values, 0, True
        ),
        query_key,
        self_values,
    )
    after_self, normed_cross = order.run(
        lambda self_mixed, self_output_low, gain_row, bias_row: (
            lambda after_self: (after_self, layer_norm(after_self, gain_row, bias_row).astype(low))
        )(layer_input + product(self_mixed, self_output_low)),
        self_mixed,
        self_output_low,
        gain_table[1],
        bias_table[1],
    )
    normed_self_turned, self_mixed_turned, encoded_turned = order.run(
        turn, normed_self, self_mixed, encoded
    )
    if links.pairwise:
        gathered = order.after(gathered)
        feed_input_low, feed_output_low, cross_held = gathered, gathered, gathered
        cross_whole = gathered[:, 8 * width :]
    cross_first, cross_second = cross_whole[:, :split], cross_whole[:, split:]
    cross_query, cross_output_low = cross_second[:, :width], cross_second[:, width:]
    cross_queries = product(normed_cross, cross_query).astype(low)
    cross_kv = product(encoded, cross_first).astype(low)
    cross_mixed, cross_totals = attention_forward(
        text_lengths, cross_queries, 0, cross_kv, 0, cross_kv, width // LANES, False
    )
    after_cross = after_self + product(cross_mixed, cross_output_low)
    normed_feed = layer_norm(after_cross, gain_table[2], bias_table[2]).astype(low)
    hidden, slope, block_output, grad_after_feed, feed_branch, sums_3 = feed_forward(
        fold_count,
        unit_lengths,
        normed_feed,
        feed_input_low,
        feed_output_low,
        after_cross,
        cotangent[0],
        norm_rows,
    )

    positions = links.positions()
    in_send, in_keep, down_send, down_keep, grad_after_cross, cross_branch, sums_2 = order.run(
        lambda *arrays: feed_backward(fold_count, links.tiles(), positions, *arrays),
        feed_branch,
        normed_feed,
        hidden,
        slope,
        feed_input_low,
        feed_output_low,
        after_cross,
        grad_after_feed,
        norm_rows,
    )
    if links.pairwise:
        in_other, down_other = links.swap_core(in_send), links.swap_core(down_send)

    crossed, straight = links.positions(True), links.positions(False)
    *cross_out, grad_cross_mixed = order.run(
        lambda *arrays: output_backward(crossed, *arrays, cross_at + 3 * width), cross_mixed, cross_branch, cross_held
    )
    if links.pairwise:
        feed_sum = order.run(
            lambda *arrays: links.sum_cores(
                jnp.concatenate(arrays[:2], axis=1), jnp.concatenate(arrays[2:], axis=1)
            ),
            in_keep,
            down_keep,
            in_other,
            down_other,
        )
        feed_chips = links.sum_chips(feed_sum)
    else:
        feed_in_part = links.scatter_whole(in_send, in_keep)
        feed_out_part = links.scatter_whole(down_send, down_keep)

    def cross_middle(cross_queries, cross_kv, cross_mixed, grad_cross_mixed, cross_totals):
        grad_q, grad_k, grad_v = attention_backward(
            text_lengths,
            cross_queries,
            0,
            cross_kv,
            0,
            cross_kv,
            width // LANES,
            cross_mixed,
            grad_cross_mixed,
            cross_totals,
            False,
        )
        return (
            grad_q,
            grad_k,
            grad_v,
            weight_gradient(crossed, normed_cross, ([grad_q], False)),
            weight_gradient(straight, encoded_turned, ([grad_k, grad_v], False)),
        )

    grad_q, grad_k, grad_v, cross_query_grad, cross_kv_grad = order.run(
        cross_middle, cross_queries, cross_kv, cross_mixed, grad_cross_mixed, cross_totals
    )
    cross_send, cross_keep = [
        [kv, jnp.concatenate([query, out], axis=1)]
        for kv, query, out in zip(cross_kv_grad, cross_query_grad, cross_out)
    ]
    if links.pairwise:
        cross_sides = list(zip(cross_keep, [links.swap_core(side) for side in cross_send]))

        def exchange(sides, ats, flips):
            halves = order.run(
                lambda *arrays: [links.first_pair(*arrays[i : i + 2]) for i in range(0, len(arrays), 2)],
                *[array for side in sides for array in side],
            )
            return [
                (stays, links.swap(goes, links.bit(at, flip)))
                for (goes, stays), at, flip in zip(halves, ats, flips)
            ]

        def finish(sides):
            arrays = [array for side in sides for array in side]
            return links.send_fsdp(
                order.run(
                    lambda *arrays: jnp.concatenate(
                        [links.sum_cores(*arrays[i : i + 2]) for i in range(0, len(arrays), 2)], axis=1
                    ),
                    *arrays,
                )
            )

    grad_after_self, self_branch, sums_1 = order.run(
        lambda grad_q, held, *arrays: input_gradient(1, [grad_q], [(held, cross_at + split)], *arrays, True),
        grad_q,
        cross_held,
        after_self,
        grad_after_cross,
        norm_rows,
    )
    if links.pairwise:
        cross_sides = exchange(cross_sides, [0, 0], flips)
    else:
        cross_part = links.scatter_whole(*[jnp.concatenate(side, axis=1) for side in (cross_send, cross_keep)])
    grad_k_cross, grad_v_cross = grad_k, grad_v

    *self_out, grad_self_mixed = order.run(
        lambda *arrays: output_backward(crossed, *arrays, width), self_mixed_turned, self_branch, self_second
    )
    grad_q, grad_k, grad_v = order.run(
        lambda query_key, self_values, self_mixed, grad_self_mixed, self_totals: attention_backward(
            unit_lengths,
            query_key,
            0,
            query_key,
            width // LANES,
            self_values,
            0,
            self_mixed,
            grad_self_mixed,
            self_totals,
            True,
        ),
        query_key,
        self_values,
        self_mixed,
        grad_self_mixed,
        self_totals,
    )
    if links.pairwise:
        cross_sides = exchange(cross_sides, [1, 1], flips)
    first_send, first_keep, second_send, second_keep = order.run(
        lambda normed, grad_q, grad_k, grad_v: weight_gradient(
            straight, normed, ([grad_q, grad_k], False), ([grad_v], links.pairwise)
        ),
        normed_self_turned,
        grad_q,
        grad_k,
        grad_v,
    )
    if links.pairwise:
        feed_part = lax.psum_scatter(order.after(feed_chips), "fsdp", scatter_dimension=0, tiled=True)
    second_send, second_keep = [
        jnp.concatenate(pair, axis=1) for pair in zip((second_send, second_keep), self_out)
    ]
    if links.pairwise:
        self_sides = [(first_keep, links.swap_core(first_send)), (second_keep, links.swap_core(second_send))]
        self_sides = exchange(self_sides, [0, 0], flips)

    grad_states, sums_0 = order.run(
        lambda grad_q, grad_k, grad_v, first, value, *arrays: input_gradient(
            0, [grad_q, grad_k, grad_v], [(first, 0), (first, width), (value, 0)], *arrays, False
        ),
        grad_q,
        grad_k,
        grad_v,
        self_first,
        self_second,
        unit_states[0],
        grad_after_self,
        norm_rows,
    )
    if links.pairwise:
        cross_parts = finish(cross_sides)
        self_sides = exchange(self_sides, [1, 1], flips)
        feed_part = order.run(lambda part: part.astype(jnp.float32), feed_part)

    def table_halves(*sums):
        tables = jnp.stack([part[0] for part in sums] + [part[1] for part in sums])
        return links.halves(jnp.pad(tables.T, ((0, 0), (0, LANES - 8))).astype(low), False)

    table_send, table_keep = order.run(table_halves, sums_0, sums_1, sums_2, sums_3)
    if links.pairwise:
        table_other = links.swap_core(table_send)
    if links.pairwise:
        table_goes, table_stays = order.run(links.first_pair, table_keep, table_other)
        table_side = (table_stays, links.swap(table_goes, links.bit(0, False)))
        table_goes, table_stays = order.run(links.first_pair, *table_side)
        table_side = (table_stays, links.swap(table_goes, links.bit(1, False)))
        cross_part = order.run(links.sum_fsdp, cross_parts)
        self_parts = finish([*self_sides, table_side])
        feed_in_part, feed_out_part = feed_part[:, : 4 * width], feed_part[:, 4 * width :]
        feed_out_part = jnp.concatenate(
            [feed_out_part[:, at * width : (at + 1) * width] for at in range(4)], axis=0
        )
    else:
        self_part = jnp.concatenate(
            [links.scatter_whole(first_send, first_keep), links.scatter_whole(second_send, second_keep)], axis=1
        )
        table_part = links.scatter_whole(table_send, table_keep)
    grad_encoded = order.run(
        lambda grad_k, grad_v, weights: weights_back([grad_k, grad_v], weights, cross_at),
        grad_k_cross,
        grad_v_cross,
        cross_held,
    )
    if links.pairwise:
        self_part = order.run(links.sum_fsdp, self_parts)
        self_part, table_part = self_part[:, : 4 * width], self_part[:, 4 * width :]
    self_in_part, self_out_part = self_part[:, : 3 * width], self_part[:, 3 * width :]
    cross_in_part = jnp.concatenate([cross_part[:, split : 3 * width], cross_part[:, :split]], axis=1)
    cross_out_part = cross_part[:, 3 * width :]

    return (
        block_output[None],
        grad_states[None],
        grad_encoded[None],
        self_in_part,
        self_out_part,
        cross_in_part,
        cross_out_part,
        feed_in_part,
        feed_out_part,
        table_part[:, :4].T,
        table_part[:, 4:8].T,
    )


def solution(mesh):
    dp_count, fsdp_count = mesh.shape["dp"], mesh.shape["fsdp"]
    split = Mesh(mesh.devices.reshape(dp_count // 2, 2, fsdp_count), BOTH)
    return jax.shard_map(
        body,
        mesh=split,
        in_specs=(
            P(BOTH, None, None),
            P(BOTH, None, None),
            P(BOTH, None, None),
            P(BOTH),
            P(BOTH),
            P(BOTH, None),
            P(BOTH, None),
            P(BOTH, None),
            P(BOTH, None),
            P(BOTH, None),
            P(BOTH, None),
            P(None, BOTH),
            P(None, BOTH),
        ),
        out_specs=(
            P(BOTH, None, None),
            P(BOTH, None, None),
            P(BOTH, None, None),
            P(BOTH, None),
            P(BOTH, None),
            P(BOTH, None),
            P(BOTH, None),
            P(BOTH, None),
            P(BOTH, None),
            P(None, BOTH),
            P(None, BOTH),
        ),
        check_vma=False,
    )
```
